32 devices in a mesh: dp: 16 (over z, x, core), tensor: 2 (over y).
Axes of the slice: x: 2, y: 2, z: 4, core: 2. Of those that a mesh axis runs over, the one named last changes fastest.
Arguments:
- inputs: bfloat16 [3152, 768], P('dp'), may hold values from -6 to 6
- norm1_gain: float32 [768], replicated, may hold values from 0.5 to 1.5
- norm1_bias: float32 [768], replicated, may hold values from -4 to 4
- qkv_weight: bfloat16 [3, 768, 768], P(None, None, 'tensor'), may hold values from -0.21875 to 0.21875
- qv_bias: float32 [2, 768], P(None, 'tensor'), may hold values from -4 to 4
- proj_weight: bfloat16 [768, 768], P('tensor'), may hold values from -2 to 2
- proj_bias: float32 [768], replicated, may hold values from -4 to 4
- norm2_gain: float32 [768], replicated, may hold values from 0.5 to 1.5
- norm2_bias: float32 [768], replicated, may hold values from -4 to 4
- router: bfloat16 [768, 16], replicated, may hold values from -0.21582031 to 0.21582031
- expert_in: bfloat16 [16, 768, 3072], P('dp', None, 'tensor'), may hold values from -0.21875 to 0.21875
- expert_in_bias: float32 [16, 3072], P('dp', 'tensor'), may hold values from -4 to 4
- expert_out: bfloat16 [16, 3072, 768], P('dp', 'tensor'), may hold values from -0.109375 to 0.109375
- expert_out_bias: float32 [16, 768], replicated, may hold values from -4 to 4
- routes: int32 [3152, 2], P('dp'), may hold values from 0 to 15, all different within a row; in each aligned block of 197 rows (0 to 196, 197 to 393, ...) at most 42 rows name the same one
- cotangent: bfloat16 [3152, 768], P('dp'), may hold values from -6 to 6
Outputs:
- output: bfloat16 [3152, 768], P('dp')
- input_grad: float32 [3152, 768], P('dp')
- norm1_gain_grad: float32 [768], replicated
- norm1_bias_grad: float32 [768], replicated
- qkv_grad: float32 [3, 768, 768], P(None, None, 'tensor')
- qv_bias_grad: float32 [2, 768], P(None, 'tensor')
- proj_grad: float32 [768, 768], P('tensor')
- proj_bias_grad: float32 [768], replicated
- norm2_gain_grad: float32 [768], replicated
- norm2_bias_grad: float32 [768], replicated
- router_grad: float32 [768, 16], replicated
- expert_in_grad: float32 [16, 768, 3072], P('dp', None, 'tensor')
- expert_in_bias_grad: float32 [16, 3072], P('dp', 'tensor')
- expert_out_grad: float32 [16, 3072, 768], P('dp', 'tensor')
- expert_out_bias_grad: float32 [16, 768], replicated
The draws below stay inside these ranges and needn't reach their ends.
Inputs may be any that keep to these rules, and one draw needn't show every extreme that they name: `routes`: each token names two different experts; among the tokens of one aligned block of 197 no expert is named more than 42 times, and in some block one expert is named exactly 42 times.
All inputs are finite; a program needn't handle non-finite values.
Results may differ from the reference program's by a relative error of at most 0.011.
Values may be sent and summed in bfloat16 or wider, within the bound.
No kernel may reach another device: no remote copies, remote signals or barrier semaphores. Data moves between devices by JAX's collectives and lax.ppermute only.
A program may use at most 192 MiB of HBM per device.

```python
import math
import jax
import jax.numpy as jnp
import numpy as np
from jax import lax

D = 768
HEADS = 12
HEAD = 64
FF = 3072
SEQ = 197
EXPERTS = 16
GROUP = 1
TOK_DEV = 197
IMAGES = 16
TOKENS = 3152
CAP = 42
N_DP = 16


def block_scale(own_key, shape, cuts, least, largest):
    def one(axis_at, parts):
        draws = jax.random.uniform(jax.random.fold_in(jax.random.fold_in(own_key, 6), axis_at), (parts,), jnp.float32, least / len(cuts), largest / len(cuts))
        return jnp.repeat(jnp.exp(draws), shape[axis_at] // parts).reshape((-1,) + (1,) * (len(shape) - axis_at - 1))

    loudness = one(*cuts[0])
    for cut in cuts[1:]:
        loudness = loudness * one(*cut)
    return loudness


def routed_block(rng, own, number, rows, count, top, reach, lean):
    sequence = jax.random.permutation(rng, count)
    packed, ordinary = load_shares(count, rows * top, reach, lean, True), load_shares(count, rows * top, reach, lean, False)
    places = jnp.arange(count)

    def named(tallies, offset_by):
        used = int((tallies > 0).sum())
        fixed = max(1, used // 4)
        moved = fixed + (places - fixed + offset_by * (used - fixed)) % max(1, count - fixed)
        return jnp.zeros((count,), jnp.int32).at[sequence[jnp.where(places < fixed, places, moved)]].set(jnp.asarray(tallies, jnp.int32))

    tallies = jnp.where(number % 4 == 0, named(packed, number // 4), named(ordinary, number - number // 4 - 1))
    mixed = jax.random.permutation(jax.random.fold_in(own, 3), count)
    giver, receiver = mixed[0:count // 2 * 2:2], mixed[1:count // 2 * 2:2]
    slack = jnp.minimum(tallies[giver] - 1, reach - tallies[receiver]) // 2
    slack = jnp.where((giver == sequence[0]) | (receiver == sequence[0]) | (tallies[receiver] == 0), 0, jnp.maximum(slack, 0))
    moved = jax.random.randint(jax.random.fold_in(own, 4), (count // 2,), 0, 1 << 20) % (slack + 1)
    tallies = tallies.at[giver].add(-moved).at[receiver].add(moved)
    members = jnp.searchsorted(jnp.cumsum(tallies), jnp.arange(rows * top), side="right").astype(jnp.int32)
    listing = members.reshape(top, rows).T
    listing = listing[jax.random.permutation(jax.random.fold_in(own, 1), rows)]
    offset_by = jax.random.randint(jax.random.fold_in(own, 2), (rows, 1), 0, top)
    return jnp.take_along_axis(listing, (jnp.arange(top)[None, :] + offset_by) % top, axis=1)


def load_shares(count, total, reach, lean, full):
    weights = [(1 << 20) // math.isqrt(rank ** lean) + 1 for rank in range(1, count + 1)]
    largest = reach if full else min(reach, max(-(-total // count), total * weights[0] // sum(weights)))
    least = 1 if total - largest >= count - 1 else 0
    given, spare = [largest] + [least] * (count - 1), total - largest - least * (count - 1)
    while spare > 0:
        free = [i for i in range(1, count) if given[i] < largest] or [i for i in range(1, count) if given[i] < reach]
        pool, budget = sum([weights[i] for i in free]), spare
        for i in free:
            extra = min(reach - given[i], max(1, budget * weights[i] // pool), spare)
            given[i] = given[i] + extra
            spare = spare - extra
    return np.array(given)


def bell_draw(own_key, shape, scale, bound, cuts=(), kind=jnp.bfloat16):
    entries = jax.random.normal(own_key, shape, jnp.float32) * scale
    if len(cuts) > 0:
        entries = block_scale(own_key, shape, cuts, -0.22, 0.18) * entries
    return jnp.clip(entries, min=-bound, max=bound).astype(kind)


def setup_inputs(seed: int = 0) -> dict:
    arg_keys = jax.random.split(jax.random.key(seed), 17)
    inputs = bell_draw(arg_keys[0], (TOKENS, D), 1.0, 6.0, ((0, 16),))
    norm1_gain = jnp.clip(1.0 + 0.1 * jax.random.normal(arg_keys[1], (D,), jnp.float32), 0.5, 1.5)
    norm1_bias = bell_draw(arg_keys[2], (D,), 0.3, 4.0, (), jnp.float32)
    qkv_weight = bell_draw(arg_keys[3], (3, D, HEADS * HEAD), D ** -0.5, 0.21875, ((2, 2),))
    qv_bias = bell_draw(arg_keys[4], (2, HEADS * HEAD), 0.5, 4.0, ((1, 2),), jnp.float32)
    proj_weight = bell_draw(arg_keys[5], (HEADS * HEAD, D), 8 ** -0.5, 2.0, ((0, 2),))
    proj_bias = bell_draw(arg_keys[6], (D,), 0.3, 4.0, (), jnp.float32)
    norm2_gain = jnp.clip(1.0 + 0.1 * jax.random.normal(arg_keys[7], (D,), jnp.float32), 0.5, 1.5)
    norm2_bias = bell_draw(arg_keys[8], (D,), 0.3, 4.0, (), jnp.float32)
    router = bell_draw(arg_keys[9], (D, EXPERTS), (0.75 * D ** -0.5), 0.21582031)
    expert_in = bell_draw(arg_keys[10], (N_DP, D, FF // GROUP), D ** -0.5, 0.21875, ((0, 16), (2, 2)))
    expert_in_bias = bell_draw(arg_keys[11], (N_DP, FF // GROUP), 0.5, 4.0, ((0, 16), (1, 2)), jnp.float32)
    expert_out = bell_draw(arg_keys[12], (N_DP, FF // GROUP, D), FF ** -0.5, 0.109375, ((0, 16), (1, 2)))
    expert_out_bias = bell_draw(arg_keys[13], (EXPERTS, D), 0.3, 4.0, (), jnp.float32)
    routes_keys = jax.random.split(jax.random.fold_in(arg_keys[14], 1), TOKENS // TOK_DEV)
    routes_turns = jax.random.permutation(jax.random.fold_in(arg_keys[14], 3), TOKENS // TOK_DEV)
    routes = jax.vmap(lambda own, number: routed_block(jax.random.fold_in(arg_keys[14], 2), own, number, TOK_DEV, EXPERTS, 2, CAP, 2))(routes_keys, routes_turns).reshape((TOKENS, 2))
    cotangent = bell_draw(arg_keys[15], (TOKENS, D), 1.0, 6.0, ((0, 16),))
    return {"inputs": inputs, "norm1_gain": norm1_gain, "norm1_bias": norm1_bias, "qkv_weight": qkv_weight, "qv_bias": qv_bias, "proj_weight": proj_weight, "proj_bias": proj_bias, "norm2_gain": norm2_gain, "norm2_bias": norm2_bias, "router": router, "expert_in": expert_in, "expert_in_bias": expert_in_bias, "expert_out": expert_out, "expert_out_bias": expert_out_bias, "routes": routes, "cotangent": cotangent}


@jax.custom_vjp
def low(v):
    return lax.optimization_barrier(v.astype(jnp.bfloat16)).astype(jnp.float32)

@jax.custom_vjp
def low_back(v):
    return v

def low_keep(v):
    return (low(v), None)

def low_pass(kept, grad):
    return (grad,)

def back_keep(v):
    return (v, None)

def back_low(kept, grad):
    return (low(grad),)
low.defvjp(low_keep, low_pass)
low_back.defvjp(back_keep, back_low)
epsilon = 1e-06
highest = lax.Precision.HIGHEST

def layer_norm(values, gain, shift):
    average = lax.optimization_barrier(jnp.mean(values, axis=-1, keepdims=True))
    centred = values - average
    spread = lax.optimization_barrier(jnp.mean(centred * centred, axis=-1, keepdims=True))
    return centred * lax.rsqrt(spread + epsilon) * gain + shift

def softmax_rows(values, axis):
    row_max = lax.optimization_barrier(jnp.max(values, axis=axis, keepdims=True))
    exp_vals = jnp.exp(values - row_max)
    return exp_vals / lax.optimization_barrier(jnp.sum(exp_vals, axis=axis, keepdims=True))

def slot_positions(routes):
    per_block = routes.reshape(N_DP, 2 * TOK_DEV)
    expert_ids = jnp.arange(EXPERTS, dtype=jnp.int32)
    onehot = (per_block[:, :, None] == expert_ids[None, None, :]).astype(jnp.int32)
    rank_vals = lax.optimization_barrier(jnp.sum(onehot * (jnp.cumsum(onehot, axis=1) - 1), axis=2))
    source = jnp.arange(N_DP, dtype=jnp.int32)[:, None]
    return ((per_block * N_DP + source) * CAP + rank_vals).reshape(-1).astype(jnp.int32)

def reference(inputs, norm1_gain, norm1_bias, qkv_weight, qv_bias, proj_weight, proj_bias, norm2_gain, norm2_bias, router, expert_in, expert_in_bias, expert_out, expert_out_bias, routes, cotangent):
    slot_index = slot_positions(routes)
    block_ff = FF // GROUP

    def forward(x_in, gain_one, bias_one, qkv_w, qv_b, proj_w, proj_b, gain_two, bias_two, router_w, in_w, in_b, out_w, out_b):
        in_full = in_w.reshape(EXPERTS, GROUP, D, block_ff).transpose(0, 2, 1, 3).reshape(EXPERTS, D, FF)
        in_bias_full = in_b.reshape(EXPERTS, FF)
        out_full = out_w.reshape(EXPERTS, FF, D)
        hidden1 = low(layer_norm(x_in, gain_one, bias_one))
        projected = jnp.einsum('td,jde->jte', hidden1, qkv_w, precision=highest)
        bias_rows = jnp.stack([qv_b[0], jnp.zeros_like(qv_b[0]), qv_b[1]])
        projected = low_back(low(projected + bias_rows[:, None, :]))
        split_heads = projected.reshape(3, IMAGES, SEQ, HEADS, HEAD)
        scores = jnp.einsum('bqhd,bkhd->bhqk', split_heads[0], split_heads[1], precision=highest) * HEAD ** (-0.5)
        scores = low_back(scores)
        prob_low = low(softmax_rows(scores, -1))
        attended = jnp.einsum('bhqk,bkhd->bqhd', prob_low, split_heads[2], precision=highest)
        attended = low_back(low(attended.reshape(TOKENS, HEADS * HEAD)))
        middle = x_in + low_back(jnp.dot(attended, proj_w, precision=highest)) + proj_b
        hidden2 = low(layer_norm(middle, gain_two, bias_two))
        logits = low_back(jnp.dot(hidden2, router_w, precision=highest))
        gate_vals = softmax_rows(jnp.take_along_axis(logits, routes, axis=1), 1)
        dispatched = jnp.zeros((EXPERTS * N_DP * CAP, D), hidden2.dtype)
        dispatched = dispatched.at[slot_index].set(jnp.repeat(hidden2, 2, axis=0))
        dispatched = low_back(dispatched).reshape(EXPERTS, N_DP * CAP, D)
        pre_act = low_back(jnp.einsum('erd,edf->erf', dispatched, in_full, precision=highest)) + in_bias_full[:, None, :]
        activated = low(jax.nn.gelu(pre_act, approximate=False))
        results = jnp.einsum('erf,efd->erd', activated, out_full, precision=highest) + out_b[:, None, :]
        results = low_back(low(results)).reshape(EXPERTS * N_DP * CAP, D)
        picked = results[slot_index].reshape(TOKENS, 2, D)
        return middle + lax.optimization_barrier(jnp.sum(gate_vals[:, :, None] * picked, axis=1))
    params = (inputs.astype(jnp.float32), norm1_gain, norm1_bias, qkv_weight.astype(jnp.float32), qv_bias, proj_weight.astype(jnp.float32), proj_bias, norm2_gain, norm2_bias, router.astype(jnp.float32), expert_in.astype(jnp.float32), expert_in_bias, expert_out.astype(jnp.float32), expert_out_bias)
    result, pullback = jax.vjp(forward, *params)
    grads = pullback(cotangent.astype(jnp.float32))
    return (result.astype(jnp.bfloat16), grads[0], grads[1], grads[2], grads[3], grads[4], grads[5], grads[6], grads[7], grads[8], grads[9], grads[10], grads[11], grads[12], grads[13])
```

```python
import jax
import jax.numpy as jnp
from jax import lax
from jax.sharding import PartitionSpec as P

HEAD = 64
SEQ = 197
F32 = jnp.float32
BF16 = jnp.bfloat16

epsilon = 1e-06


def norm_parts(values):
    average = jnp.mean(values, axis=-1, keepdims=True)
    centred = values - average
    inverse = lax.rsqrt(jnp.mean(centred * centred, axis=-1, keepdims=True) + epsilon)
    return (centred * inverse, inverse)


def norm_back(inner_grad, normed, inverse):
    first_mean = jnp.mean(inner_grad, axis=-1, keepdims=True)
    second_mean = jnp.mean(inner_grad * normed, axis=-1, keepdims=True)
    return inverse * (inner_grad - first_mean - normed * second_mean)


def gelu_parts(pre_act):
    normal_cdf = 0.5 * (1.0 + lax.erf(pre_act * 0.7071067811865476))
    density = jnp.exp(-0.5 * pre_act * pre_act) * 0.3989422804014327
    return (pre_act * normal_cdf, normal_cdf + pre_act * density)


def dot(a, b, dims, out=F32):
    return lax.dot_general(a, b, (dims, ((), ())), preferred_element_type=out)


def nn(a, b):
    return dot(a, b, ((1,), (0,)))


def nt(a, b):
    return dot(a, b, ((1,), (1,)))


def tn(a, b):
    return dot(a, b, ((0,), (0,)))


def exact(a, b):
    return lax.dot_general(
        a,
        b,
        (((1,), (0,)), ((), ())),
        precision=lax.Precision.HIGHEST,
        preferred_element_type=F32,
    )


def swap(x):
    return lax.ppermute(x, "tensor", [(0, 1), (1, 0)])


def across(x, bit, count):
    return lax.ppermute(x, "dp", [(i, i ^ bit) for i in range(count)])


def in_order(plane, mine, other, axis):
    first = jnp.where(plane == 0, mine, other)
    second = jnp.where(plane == 0, other, mine)
    return jnp.concatenate([first, second], axis=axis)


def half_of(plane, x, which):
    width = x.shape[-1] // 2
    low, high = x[..., :width], x[..., width:]
    return jnp.where((plane == which), low, high)


def reduce_pieces(total, order, count):
    size = total.shape[0] // count
    live = {r: total[r * size : (r + 1) * size] for r in range(count)}
    for bit in order:
        outgoing = [r for r in sorted(live) if r & bit]
        keep = [r for r in sorted(live) if not r & bit]
        sent = jnp.concatenate([live[r] for r in outgoing], axis=0).astype(BF16)
        got = across(sent, bit, count).astype(F32)
        live = {r: live[r] + got[i * size : (i + 1) * size] for i, r in enumerate(keep)}
    return live[0].astype(BF16)


def spread_pieces(piece, order, count):
    names, held = [0], piece
    for bit in order:
        got = across(held, bit, count)
        held = jnp.concatenate([held, got], axis=0)
        names = names + [r | bit for r in names]
    return held, names


def local(
    inputs,
    norm1_gain,
    norm1_bias,
    qkv_weight,
    qv_bias,
    proj_weight,
    proj_bias,
    norm2_gain,
    norm2_bias,
    router,
    expert_in,
    expert_in_bias,
    expert_out,
    expert_out_bias,
    routes,
    cotangent,
):
    tok_count = inputs.shape[0]
    feat_dim = inputs.shape[1]
    half_dim = feat_dim // 2
    head_cols = qkv_weight.shape[2]
    heads_here = head_cols // HEAD
    images = tok_count // SEQ
    experts = router.shape[1]
    sources = lax.axis_size("dp")
    group_size = sources // experts
    capacity = max(2, (10 * tok_count + 3 * experts - 1) // (3 * experts))
    slots = (capacity + 3 + 15) // 16 * 16
    score_scale = HEAD ** (-0.5)
    plane = lax.axis_index("tensor")
    me = lax.axis_index("dp")
    own_expert = me // group_size
    in_weight, out_weight = expert_in[0], expert_out[0]

    expert_ids = jnp.arange(experts, dtype=jnp.int32)
    slot_ids = jnp.arange(slots, dtype=jnp.int32)
    all_ids = jnp.arange(experts * slots, dtype=jnp.int32)
    pick = [(routes[:, k : k + 1] == expert_ids[None, :]) for k in range(2)]
    named = (pick[0] | pick[1]).astype(BF16)
    before = (
        jnp.arange(tok_count)[:, None] > jnp.arange(tok_count)[None, :]
    ).astype(BF16)
    earlier = nn(before, named)
    rank = [
        jnp.sum(jnp.where(pick[k], earlier, 0.0), axis=1, keepdims=True).astype(jnp.int32)
        for k in range(2)
    ]
    place = [routes[:, k : k + 1] * slots + rank[k] for k in range(2)]
    onehot = ((place[0] == all_ids[None, :]) | (place[1] == all_ids[None, :])).astype(BF16)
    rank_hot = [(rank[k] == slot_ids[None, :]) for k in range(2)]
    pick_low = [pick[k].astype(BF16) for k in range(2)]
    partner = [
        jnp.where(rank_hot[k], routes[:, 1 - k : 2 - k].astype(F32), 0.0).astype(BF16)
        for k in range(2)
    ]
    partner_map = tn(pick_low[0], partner[0]) + tn(pick_low[1], partner[1])

    cot_half = half_of(plane, cotangent, 0)
    cot_send = tn(onehot, cot_half).astype(BF16).reshape(experts, slots, half_dim)
    note = jnp.pad(partner_map.astype(BF16), ((0, 0), (0, half_dim - slots)))[:, None, :]
    cot_send = jnp.where(slot_ids[None, :, None] == slots - 1, note, cot_send)
    cot_send = jnp.repeat(cot_send, group_size, axis=0)
    cot_mine = lax.all_to_all(cot_send, "dp", split_axis=0, concat_axis=0, tiled=True)
    cot_mine = cot_mine.reshape(-1, half_dim)
    cot_other = swap(cot_mine)
    proj_other = swap(proj_weight)
    proj_full = in_order(plane, proj_weight, proj_other, 0)

    x_in = inputs.astype(F32)
    normed1, inverse1 = norm_parts(x_in)
    hidden1 = (normed1 * norm1_gain + norm1_bias).astype(BF16)
    projected = jnp.einsum("td,jde->jte", hidden1, qkv_weight, preferred_element_type=F32)
    bias_rows = jnp.stack([qv_bias[0], jnp.zeros_like(qv_bias[0]), qv_bias[1]])
    projected = (projected + bias_rows[:, None, :]).astype(BF16)
    heads_view = projected.reshape(3, images, SEQ, heads_here, HEAD)
    queries, key_vals, values_in = (heads_view[0], heads_view[1], heads_view[2])
    scores = (
        jnp.einsum("bqhd,bkhd->bhqk", queries, key_vals, preferred_element_type=F32)
        * score_scale
    )
    row_max = jnp.max(scores, axis=-1, keepdims=True)
    exp_scores = jnp.exp(scores - row_max)
    row_total = jnp.sum(exp_scores, axis=-1, keepdims=True)
    prob_vals = exp_scores / row_total
    prob_low = prob_vals.astype(BF16)
    attended = jnp.einsum("bhqk,bkhd->bqhd", prob_low, values_in, preferred_element_type=F32)
    attended = attended.reshape(tok_count, head_cols).astype(BF16)
    attended_all = in_order(plane, attended, swap(attended), 1)
    middle = x_in + nn(attended_all, proj_full) + proj_bias
    normed2, inverse2 = norm_parts(middle)
    hidden2 = (normed2 * norm2_gain + norm2_bias).astype(BF16)

    send = tn(onehot, hidden2).astype(BF16).reshape(experts, slots, feat_dim)
    send = jnp.repeat(send, group_size, axis=0)
    arrived = lax.all_to_all(send, "dp", split_axis=0, concat_axis=0, tiled=True)
    arrived = arrived.reshape(-1, feat_dim)

    logits = nn(hidden2, router)
    chosen = [jnp.sum(jnp.where(pick[k], logits, 0.0), axis=1, keepdims=True) for k in range(2)]
    chosen_max = jnp.maximum(chosen[0], chosen[1])
    chosen_exp = [jnp.exp(chosen[k] - chosen_max) for k in range(2)]
    chosen_sum = chosen_exp[0] + chosen_exp[1]
    gate_vals = [chosen_exp[k] / chosen_sum for k in range(2)]
    gate_map = jnp.where(pick[0], gate_vals[0], 0.0) + jnp.where(pick[1], gate_vals[1], 0.0)
    grad_out = cotangent.astype(F32)
    row_grad = [(gate_vals[k] * grad_out).astype(BF16) for k in range(2)]
    out_bias_grad = tn(pick_low[0], row_grad[0]) + tn(pick_low[1], row_grad[1])

    note_rows = jnp.where(plane == 0, cot_mine, cot_other).reshape(sources, slots, half_dim)
    other_expert = note_rows[:, slots - 1, :slots].reshape(-1, 1).astype(jnp.int32)
    real_slot = (jnp.arange(sources * slots, dtype=jnp.int32)[:, None] % slots) < capacity
    row_logits = nn(arrived, router)
    own_logit = jnp.sum(
        jnp.where(expert_ids[None, :] == own_expert, row_logits, 0.0), axis=1, keepdims=True
    )
    other_logit = jnp.sum(
        jnp.where(expert_ids[None, :] == other_expert, row_logits, 0.0), axis=1, keepdims=True
    )
    top_logit = jnp.maximum(own_logit, other_logit)
    own_exp = jnp.exp(own_logit - top_logit)
    row_gate = own_exp / (own_exp + jnp.exp(other_logit - top_logit))
    row_gate = jnp.where(real_slot, row_gate, 0.0)
    cot_rows = in_order(plane, cot_mine, cot_other, 1)
    grad_rows = (row_gate * cot_rows.astype(F32)).astype(BF16)

    pre_act = nn(arrived, in_weight) + expert_in_bias[0]
    activ_vals, gelu_slope = gelu_parts(pre_act)
    activ_low = activ_vals.astype(BF16)
    act_grad = nt(grad_rows, out_weight) * gelu_slope
    in_bias_grad = jnp.sum(act_grad, axis=0)
    act_low = act_grad.astype(BF16)
    row_part = nt(act_low, in_weight)
    part_out = nn(activ_low, out_weight)

    inner_part = jnp.sum(cot_rows.astype(F32) * part_out, axis=1).reshape(sources, slots)
    inner_all = inner_part + swap(inner_part)
    row_half = half_of(plane, row_part, 0) + swap(half_of(plane, row_part, 1).astype(BF16)).astype(F32)
    gated_out = row_gate * part_out
    out_half = half_of(plane, gated_out, 0) + swap(half_of(plane, gated_out, 1).astype(BF16)).astype(F32)
    inner_high = inner_all.astype(BF16)
    inner_low = (inner_all - inner_high.astype(F32)).astype(BF16)

    def widen(x):
        return jnp.pad(x, ((0, 0), (0, half_dim - slots)))[:, None, :]

    row_send = row_half.astype(BF16).reshape(sources, slots, half_dim)
    row_send = jnp.where(slot_ids[None, :, None] == slots - 1, widen(inner_high), row_send)
    row_send = jnp.where(slot_ids[None, :, None] == slots - 2, widen(inner_low), row_send)
    row_back = lax.all_to_all(row_send, "dp", split_axis=0, concat_axis=0, tiled=True)
    out_send = out_half.astype(BF16).reshape(sources, slots, half_dim)
    out_back = lax.all_to_all(out_send, "dp", split_axis=0, concat_axis=0, tiled=True)
    out_weight_grad = tn(activ_low, grad_rows)
    in_weight_grad = tn(arrived, act_low)

    def over_group(x):
        if group_size == 1:
            return x
        shape = (experts, group_size) + x.shape[1:]
        return jnp.sum(x.reshape(shape).astype(F32), axis=1).astype(BF16)

    inner_high = row_back[:, slots - 1, :slots].reshape(experts, group_size, slots)
    inner_low = row_back[:, slots - 2, :slots].reshape(experts, group_size, slots)
    gate_grad = []
    for k in range(2):
        found = 0.0
        for g in range(group_size):
            found = found + nn(pick_low[k], inner_high[:, g]) + nn(pick_low[k], inner_low[:, g])
        found = jnp.sum(jnp.where(rank_hot[k], found, 0.0), axis=1, keepdims=True)
        bias_row = exact(pick[k].astype(F32), expert_out_bias)
        gate_grad.append(found + jnp.sum(bias_row * grad_out, axis=1, keepdims=True))
    gate_mean = gate_vals[0] * gate_grad[0] + gate_vals[1] * gate_grad[1]
    chosen_grad = [gate_vals[k] * (gate_grad[k] - gate_mean) for k in range(2)]
    logit_grad = (
        jnp.where(pick[0], chosen_grad[0], 0.0) + jnp.where(pick[1], chosen_grad[1], 0.0)
    ).astype(BF16)
    row_home = nn(onehot, over_group(row_back).reshape(-1, half_dim)).astype(BF16)
    row_home = in_order(plane, row_home, swap(row_home), 1).astype(F32)
    hidden2_grad = row_home + nt(logit_grad, router)
    router_grad = tn(logit_grad, hidden2)
    norm2_gain_grad = jnp.sum(hidden2_grad * normed2, axis=0)
    norm2_bias_grad = jnp.sum(hidden2_grad, axis=0)
    middle_grad = grad_out + norm_back(hidden2_grad * norm2_gain, normed2, inverse2)
    proj_bias_grad = jnp.sum(middle_grad, axis=0)
    middle_low = middle_grad.astype(BF16)

    out_home = nn(onehot, over_group(out_back).reshape(-1, half_dim))
    bias_home = exact(gate_map, half_of(plane, expert_out_bias, 0))
    out_own = (half_of(plane, middle, 0) + out_home + bias_home).astype(BF16)
    output = in_order(plane, out_own, swap(out_own), 1)

    def shuffle(width):
        chunk = width // sources
        rows = jnp.arange(width, dtype=jnp.int32)[:, None]
        cols = jnp.arange(width, dtype=jnp.int32)[None, :]
        return (
            ((rows // chunk) == jnp.bitwise_xor(cols // chunk, me)) & (rows % chunk == cols % chunk)
        ).astype(BF16)

    bits = [1 << i for i in range(sources.bit_length() - 1)]
    first_order = bits
    second_order = bits[:1] + bits[2:] + bits[1:2]
    mix_in, mix_proj = shuffle(feat_dim), shuffle(head_cols)
    hidden1_mixed = nn(hidden1, mix_in).astype(BF16)
    attended_mixed = nn(attended, mix_proj).astype(BF16)
    proj_total = tn(attended_mixed, middle_low)
    attended_grad = nt(middle_low, proj_weight).astype(BF16)
    attended_grad = attended_grad.reshape(images, SEQ, heads_here, HEAD)
    value_grad = jnp.einsum("bhqk,bqhd->bkhd", prob_low, attended_grad, preferred_element_type=F32)
    prob_grad = jnp.einsum("bqhd,bkhd->bhqk", attended_grad, values_in, preferred_element_type=F32)
    score_grad = prob_vals * (prob_grad - jnp.sum(prob_vals * prob_grad, axis=-1, keepdims=True))
    score_low = score_grad.astype(BF16)
    query_grad = (
        jnp.einsum("bhqk,bkhd->bqhd", score_low, key_vals, preferred_element_type=F32)
        * score_scale
    )
    key_grad = (
        jnp.einsum("bhqk,bqhd->bkhd", score_low, queries, preferred_element_type=F32)
        * score_scale
    )
    proj_low = [
        g.reshape(tok_count, head_cols).astype(BF16) for g in (query_grad, key_grad, value_grad)
    ]
    proj_low = jnp.concatenate(proj_low, axis=1)
    qkv_total = tn(hidden1_mixed, proj_low)
    qv_sums = jnp.sum(proj_low.astype(F32), axis=0)
    hidden1_part = sum(
        nt(proj_low[:, j * head_cols : (j + 1) * head_cols], qkv_weight[j]) for j in range(3)
    ).astype(BF16)
    hidden1_grad = hidden1_part.astype(F32) + swap(hidden1_part).astype(F32)
    norm1_gain_grad = jnp.sum(hidden1_grad * normed1, axis=0)
    norm1_bias_grad = jnp.sum(hidden1_grad, axis=0)
    input_grad = middle_grad + norm_back(hidden1_grad * norm1_gain, normed1, inverse1)

    early = jnp.concatenate(
        [
            router_grad,
            out_bias_grad,
            norm2_gain_grad[None],
            norm2_bias_grad[None],
            proj_bias_grad[None],
        ],
        axis=0,
    )
    early = lax.psum(early, "dp")
    router_grad, out_bias_grad = early[:experts].T, early[experts : 2 * experts]
    norm2_gain_grad, norm2_bias_grad, proj_bias_grad = (early[2 * experts + i] for i in range(3))
    late = jnp.stack(
        [
            norm1_gain_grad,
            norm1_bias_grad,
            jnp.concatenate([qv_sums[:head_cols], qv_sums[2 * head_cols :]]),
        ]
    )
    for bit in bits:
        late = late + across(late, bit, sources)
    qv_bias_grad = late[2].reshape(2, head_cols)

    def all_sum(total, order, mix):
        held, names = spread_pieces(reduce_pieces(total, order, sources), order[::-1], sources)
        size = held.shape[0] // sources
        back = [names.index(r) for r in range(sources)]
        held = jnp.concatenate([held[i * size : (i + 1) * size] for i in back], axis=0)
        return nn(mix, held)

    proj_grad = all_sum(proj_total, second_order, mix_proj)
    split = (3 * head_cols // 2 + 127) // 128 * 128
    qkv_sum = jnp.concatenate(
        [
            all_sum(qkv_total[:, :split], first_order, mix_in),
            all_sum(qkv_total[:, split:], second_order, mix_in),
        ],
        axis=1,
    )
    qkv_grad = jnp.stack(
        [qkv_sum[:, j * head_cols : (j + 1) * head_cols] for j in range(3)]
    )
    return (
        output,
        input_grad,
        late[0],
        late[1],
        qkv_grad,
        qv_bias_grad,
        proj_grad,
        proj_bias_grad,
        norm2_gain_grad,
        norm2_bias_grad,
        router_grad,
        in_weight_grad[None],
        in_bias_grad[None],
        out_weight_grad[None],
        out_bias_grad,
    )


def solution(mesh):
    return jax.shard_map(
        local,
        mesh=mesh,
        in_specs=(
            P("dp", None),
            P(),
            P(),
            P(None, None, "tensor"),
            P(None, "tensor"),
            P("tensor", None),
            P(),
            P(),
            P(),
            P(),
            P("dp", None, "tensor"),
            P("dp", "tensor"),
            P("dp", "tensor", None),
            P(),
            P("dp", None),
            P("dp", None),
        ),
        out_specs=(
            P("dp", None),
            P("dp", None),
            P(),
            P(),
            P(None, None, "tensor"),
            P(None, "tensor"),
            P("tensor", None),
            P(),
            P(),
            P(),
            P(),
            P("dp", None, "tensor"),
            P("dp", "tensor"),
            P("dp", "tensor", None),
            P(),
        ),
        check_vma=False,
    )
```

```python
import jax
import jax.numpy as jnp
from jax import lax
from jax.experimental import pallas as pl
from jax.experimental.pallas import tpu as pltpu
from jax.sharding import PartitionSpec as P

HEAD = 64
SEQ = 197
F32 = jnp.float32
BF16 = jnp.bfloat16

epsilon = 1e-06


def norm_parts(values):
    average = jnp.mean(values, axis=-1, keepdims=True)
    centred = values - average
    inverse = lax.rsqrt(jnp.mean(centred * centred, axis=-1, keepdims=True) + epsilon)
    return (centred * inverse, inverse)


def norm_back(inner_grad, normed, inverse):
    first_mean = jnp.mean(inner_grad, axis=-1, keepdims=True)
    second_mean = jnp.mean(inner_grad * normed, axis=-1, keepdims=True)
    return inverse * (inner_grad - first_mean - normed * second_mean)


def gelu_parts(pre_act):
    normal_cdf = 0.5 * (1.0 + lax.erf(pre_act * 0.7071067811865476))
    density = jnp.exp(-0.5 * pre_act * pre_act) * 0.3989422804014327
    return (pre_act * normal_cdf, normal_cdf + pre_act * density)


def dot(a, b, dims, out=F32):
    return lax.dot_general(a, b, (dims, ((), ())), preferred_element_type=out)


def nn(a, b):
    return dot(a, b, ((1,), (0,)))


def nt(a, b):
    return dot(a, b, ((1,), (1,)))


def tn(a, b):
    return dot(a, b, ((0,), (0,)))


def exact(a, b):
    return lax.dot_general(
        a,
        b,
        (((1,), (0,)), ((), ())),
        precision=lax.Precision.HIGHEST,
        preferred_element_type=F32,
    )


def swap(x):
    return lax.ppermute(x, "tensor", [(0, 1), (1, 0)])


def across(x, bit, count):
    return lax.ppermute(x, "dp", [(i, i ^ bit) for i in range(count)])


def in_order(plane, mine, other, axis):
    first = jnp.where(plane == 0, mine, other)
    second = jnp.where(plane == 0, other, mine)
    return jnp.concatenate([first, second], axis=axis)


def half_of(plane, x, which):
    width = x.shape[-1] // 2
    low, high = x[..., :width], x[..., width:]
    return jnp.where((plane == which), low, high)


def reduce_rounds(parts, orders, count):
    def split(part):
        middle = part.shape[0] // 2
        return part[:middle], part[middle:]

    both = jnp.concatenate([split(part)[1].astype(BF16) for part in parts], axis=1)
    both = across(both, orders[0][0], count)
    place = 0
    held = []
    for part in parts:
        width = part.shape[1]
        held.append(split(part)[0] + both[:, place : place + width].astype(F32))
        place += width
    for turn in range(1, len(orders[0])):
        held = [
            split(part)[0] + across(split(part)[1].astype(BF16), order[turn], count).astype(F32)
            for part, order in zip(held, orders)
        ]
    return [part.astype(BF16) for part in held]


def spread_rounds(parts, orders, count):
    for turn in range(len(orders[0]) - 1, 0, -1):
        parts = [
            jnp.concatenate([part, across(part, order[turn], count)], axis=0)
            for part, order in zip(parts, orders)
        ]
    mine = jnp.concatenate(parts, axis=1)
    return mine, across(mine, orders[0][0], count)


def finish_kernel(head_cols, width, mix_a, mix_b, mine, got, qkv_ref, proj_ref, small_ref):
    rows = mine.shape[0]

    def ordered(mix, start, size):
        low = jnp.dot(mix[:, :rows], mine[:, start : start + size], preferred_element_type=F32)
        high = jnp.dot(mix[:, rows:], got[:, start : start + size], preferred_element_type=F32)
        return low + high

    qkv_ref[0] = ordered(mix_a, 0, head_cols)
    qkv_ref[1] = ordered(mix_a, head_cols, head_cols)
    small_ref[...] = ordered(mix_a, 2 * head_cols, width)
    start = 2 * head_cols + width
    qkv_ref[2] = ordered(mix_b, start, head_cols)
    proj_ref[...] = ordered(mix_b, start + head_cols, head_cols).T


def finish(mix_a, mix_b, mine, got, head_cols, width):
    feat_dim = mix_a.shape[0]
    return pl.pallas_call(
        lambda *refs: finish_kernel(head_cols, width, *refs),
        out_shape=(
            jax.ShapeDtypeStruct((3, feat_dim, head_cols), F32),
            jax.ShapeDtypeStruct((head_cols, feat_dim), F32),
            jax.ShapeDtypeStruct((feat_dim, width), F32),
        ),
        compiler_params=pltpu.CompilerParams(vmem_limit_bytes=48 << 20),
        name="finish",
    )(mix_a, mix_b, mine, got)


def local(
    inputs,
    norm1_gain,
    norm1_bias,
    qkv_weight,
    qv_bias,
    proj_weight,
    proj_bias,
    norm2_gain,
    norm2_bias,
    router,
    expert_in,
    expert_in_bias,
    expert_out,
    expert_out_bias,
    routes,
    cotangent,
):
    tok_count = inputs.shape[0]
    feat_dim = inputs.shape[1]
    half_dim = feat_dim // 2
    head_cols = qkv_weight.shape[2]
    heads_here = head_cols // HEAD
    images = tok_count // SEQ
    experts = router.shape[1]
    sources = lax.axis_size("dp")
    group_size = sources // experts
    capacity = max(2, (10 * tok_count + 3 * experts - 1) // (3 * experts))
    slots = (capacity + 3 + 15) // 16 * 16
    score_scale = HEAD ** (-0.5)
    plane = lax.axis_index("tensor")
    me = lax.axis_index("dp")
    own_expert = me // group_size
    in_weight, out_weight = expert_in[0], expert_out[0]

    expert_ids = jnp.arange(experts, dtype=jnp.int32)
    slot_ids = jnp.arange(slots, dtype=jnp.int32)
    all_ids = jnp.arange(experts * slots, dtype=jnp.int32)
    pick = [(routes[:, k : k + 1] == expert_ids[None, :]) for k in range(2)]
    named = (pick[0] | pick[1]).astype(BF16)
    before = (
        jnp.arange(tok_count)[:, None] > jnp.arange(tok_count)[None, :]
    ).astype(BF16)
    earlier = nn(before, named)
    rank = [
        jnp.sum(jnp.where(pick[k], earlier, 0.0), axis=1, keepdims=True).astype(jnp.int32)
        for k in range(2)
    ]
    place = [routes[:, k : k + 1] * slots + rank[k] for k in range(2)]
    onehot = ((place[0] == all_ids[None, :]) | (place[1] == all_ids[None, :])).astype(BF16)
    rank_hot = [(rank[k] == slot_ids[None, :]) for k in range(2)]
    pick_low = [pick[k].astype(BF16) for k in range(2)]
    partner = [
        jnp.where(rank_hot[k], routes[:, 1 - k : 2 - k].astype(F32), 0.0).astype(BF16)
        for k in range(2)
    ]
    partner_map = tn(pick_low[0], partner[0]) + tn(pick_low[1], partner[1])

    cot_half = half_of(plane, cotangent, 0)
    cot_send = tn(onehot, cot_half).astype(BF16).reshape(experts, slots, half_dim)
    note = jnp.pad(partner_map.astype(BF16), ((0, 0), (0, half_dim - slots)))[:, None, :]
    cot_send = jnp.where(slot_ids[None, :, None] == slots - 1, note, cot_send)
    cot_send = jnp.repeat(cot_send, group_size, axis=0)
    proj_other = swap(proj_weight)
    proj_full = in_order(plane, proj_weight, proj_other, 0)

    inputs, cot_send = lax.optimization_barrier((inputs, cot_send))
    cot_mine = lax.all_to_all(cot_send, "dp", split_axis=0, concat_axis=0, tiled=True)
    cot_mine = cot_mine.reshape(-1, half_dim)
    x_in = inputs.astype(F32)
    normed1, inverse1 = norm_parts(x_in)
    hidden1 = (normed1 * norm1_gain + norm1_bias).astype(BF16)
    projected = jnp.einsum("td,jde->jte", hidden1, qkv_weight, preferred_element_type=F32)
    bias_rows = jnp.stack([qv_bias[0], jnp.zeros_like(qv_bias[0]), qv_bias[1]])
    projected = (projected + bias_rows[:, None, :]).astype(BF16)
    heads_view = projected.reshape(3, images, SEQ, heads_here, HEAD)
    queries, key_vals, values_in = (heads_view[0], heads_view[1], heads_view[2])
    scores = (
        jnp.einsum("bqhd,bkhd->bhqk", queries, key_vals, preferred_element_type=F32)
        * score_scale
    )
    row_max = jnp.max(scores, axis=-1, keepdims=True)
    exp_scores = jnp.exp(scores - row_max)
    row_total = jnp.sum(exp_scores, axis=-1, keepdims=True)
    prob_vals = exp_scores / row_total
    prob_low = prob_vals.astype(BF16)
    attended = jnp.einsum("bhqk,bkhd->bqhd", prob_low, values_in, preferred_element_type=F32)
    attended = attended.reshape(tok_count, head_cols).astype(BF16)
    attended_other, cot_mine = lax.optimization_barrier((swap(attended), cot_mine))
    attended_all = in_order(plane, attended, attended_other, 1)
    middle = x_in + nn(attended_all, proj_full) + proj_bias
    normed2, inverse2 = norm_parts(middle)
    hidden2 = (normed2 * norm2_gain + norm2_bias).astype(BF16)

    send = tn(onehot, hidden2).astype(BF16).reshape(experts, slots, feat_dim)
    send = jnp.repeat(send, group_size, axis=0)
    cot_other = swap(cot_mine)
    arrived = lax.all_to_all(send, "dp", split_axis=0, concat_axis=0, tiled=True)
    arrived = arrived.reshape(-1, feat_dim)

    logits = nn(hidden2, router)
    chosen = [jnp.sum(jnp.where(pick[k], logits, 0.0), axis=1, keepdims=True) for k in range(2)]
    chosen_max = jnp.maximum(chosen[0], chosen[1])
    chosen_exp = [jnp.exp(chosen[k] - chosen_max) for k in range(2)]
    chosen_sum = chosen_exp[0] + chosen_exp[1]
    gate_vals = [chosen_exp[k] / chosen_sum for k in range(2)]
    gate_map = jnp.where(pick[0], gate_vals[0], 0.0) + jnp.where(pick[1], gate_vals[1], 0.0)
    grad_out = cotangent.astype(F32)
    row_grad = [(gate_vals[k] * grad_out).astype(BF16) for k in range(2)]
    out_bias_grad = tn(row_grad[0], pick_low[0]) + tn(row_grad[1], pick_low[1])

    note_rows = jnp.where(plane == 0, cot_mine, cot_other).reshape(sources, slots, half_dim)
    other_expert = note_rows[:, slots - 1, :slots].reshape(-1, 1).astype(jnp.int32)
    real_slot = (jnp.arange(sources * slots, dtype=jnp.int32)[:, None] % slots) < capacity
    row_logits = nn(arrived, router)
    own_logit = jnp.sum(
        jnp.where(expert_ids[None, :] == own_expert, row_logits, 0.0), axis=1, keepdims=True
    )
    other_logit = jnp.sum(
        jnp.where(expert_ids[None, :] == other_expert, row_logits, 0.0), axis=1, keepdims=True
    )
    top_logit = jnp.maximum(own_logit, other_logit)
    own_exp = jnp.exp(own_logit - top_logit)
    row_gate = own_exp / (own_exp + jnp.exp(other_logit - top_logit))
    row_gate = jnp.where(real_slot, row_gate, 0.0)
    cot_rows = in_order(plane, cot_mine, cot_other, 1)
    grad_rows = (row_gate * cot_rows.astype(F32)).astype(BF16)

    pre_act = nn(arrived, in_weight) + expert_in_bias[0]
    activ_vals, gelu_slope = gelu_parts(pre_act)
    activ_low = activ_vals.astype(BF16)
    act_grad = nt(grad_rows, out_weight) * gelu_slope
    in_bias_grad = jnp.sum(act_grad, axis=0)
    act_low = act_grad.astype(BF16)
    row_part = nt(act_low, in_weight)
    part_out = nn(activ_low, out_weight)

    inner = jnp.sum(cot_rows.astype(F32) * part_out, axis=1).reshape(sources, slots)
    inner_high = inner.astype(BF16)
    inner_low = (inner - inner_high.astype(F32)).astype(BF16)

    def widen(x):
        return jnp.pad(x, ((0, 0), (0, feat_dim - slots)))[:, None, :]

    row_send = row_part.astype(BF16).reshape(sources, slots, feat_dim)
    row_send = jnp.where(slot_ids[None, :, None] == slots - 1, widen(inner_high), row_send)
    row_send = jnp.where(slot_ids[None, :, None] == slots - 2, widen(inner_low), row_send)
    row_back = lax.all_to_all(row_send, "dp", split_axis=0, concat_axis=0, tiled=True)
    out_send = (row_gate * part_out).astype(BF16).reshape(sources, slots, feat_dim)
    out_send, row_back = lax.optimization_barrier((out_send, row_back))
    out_back = lax.all_to_all(out_send, "dp", split_axis=0, concat_axis=0, tiled=True)
    out_weight_grad = tn(activ_low, grad_rows)
    in_weight_grad = tn(arrived, act_low)

    def over_group(x):
        if group_size == 1:
            return x
        shape = (experts, group_size) + x.shape[1:]
        return jnp.sum(x.reshape(shape).astype(F32), axis=1).astype(BF16)

    inner = row_back[:, slots - 2 :, :slots].astype(F32)
    inner = jnp.sum(inner.reshape(experts, 2 * group_size, slots), axis=1)
    inner = inner + swap(inner)
    gate_grad = []
    for k in range(2):
        found = exact(pick[k].astype(F32), inner)
        found = jnp.sum(jnp.where(rank_hot[k], found, 0.0), axis=1, keepdims=True)
        bias_row = exact(pick[k].astype(F32), expert_out_bias)
        gate_grad.append(found + jnp.sum(bias_row * grad_out, axis=1, keepdims=True))
    gate_mean = gate_vals[0] * gate_grad[0] + gate_vals[1] * gate_grad[1]
    chosen_grad = [gate_vals[k] * (gate_grad[k] - gate_mean) for k in range(2)]
    logit_grad = (
        jnp.where(pick[0], chosen_grad[0], 0.0) + jnp.where(pick[1], chosen_grad[1], 0.0)
    ).astype(BF16)
    row_home = nn(onehot, over_group(row_back).reshape(-1, feat_dim)).astype(BF16)
    row_home = row_home.astype(F32) + swap(row_home).astype(F32)
    hidden2_grad = row_home + nt(logit_grad, router)
    norm2_gain_grad = jnp.sum(hidden2_grad * normed2, axis=0)
    norm2_bias_grad = jnp.sum(hidden2_grad, axis=0)
    middle_grad = grad_out + norm_back(hidden2_grad * norm2_gain, normed2, inverse2)
    proj_bias_grad = jnp.sum(middle_grad, axis=0)
    middle_low = middle_grad.astype(BF16)

    bits = [1 << i for i in range(sources.bit_length() - 1)]
    orders = [bits, bits[:1] + bits[2:] + bits[1:2]]
    chunk = feat_dim // sources

    def mixer(order):
        rows = jnp.arange(feat_dim, dtype=jnp.int32)[:, None]
        cols = jnp.arange(feat_dim, dtype=jnp.int32)[None, :]
        spot = cols // chunk
        piece = jnp.zeros_like(spot)
        for i, bit in enumerate(order):
            piece = piece | jnp.where((spot >> (len(order) - 1 - i)) & 1, bit, 0)
        return ((rows // chunk == (piece ^ me)) & (rows % chunk == cols % chunk)).astype(BF16)

    mix_a, mix_b = mixer(orders[0]), mixer(orders[1])
    hidden1_a, hidden1_b = nn(hidden1, mix_a).astype(BF16), nn(hidden1, mix_b).astype(BF16)
    middle_b = nn(middle_low, mix_b).astype(BF16)
    proj_total = tn(middle_b, attended)
    attended_grad = nt(middle_low, proj_weight).astype(BF16)
    attended_grad = attended_grad.reshape(images, SEQ, heads_here, HEAD)
    value_grad = jnp.einsum("bhqk,bqhd->bkhd", prob_low, attended_grad, preferred_element_type=F32)
    prob_grad = jnp.einsum("bqhd,bkhd->bhqk", attended_grad, values_in, preferred_element_type=F32)
    score_grad = prob_vals * (prob_grad - jnp.sum(prob_vals * prob_grad, axis=-1, keepdims=True))
    score_low = score_grad.astype(BF16)
    query_grad = (
        jnp.einsum("bhqk,bkhd->bqhd", score_low, key_vals, preferred_element_type=F32)
        * score_scale
    )
    key_grad = (
        jnp.einsum("bhqk,bqhd->bkhd", score_low, queries, preferred_element_type=F32)
        * score_scale
    )
    proj_low = [
        g.reshape(tok_count, head_cols).astype(BF16) for g in (query_grad, key_grad, value_grad)
    ]
    proj_low = jnp.concatenate(proj_low, axis=1)
    qk_total = tn(hidden1_a, proj_low[:, : 2 * head_cols])
    v_total = tn(hidden1_b, proj_low[:, 2 * head_cols :])
    qv_sums = jnp.sum(proj_low.astype(F32), axis=0)
    hidden1_part = sum(
        nt(proj_low[:, j * head_cols : (j + 1) * head_cols], qkv_weight[j]) for j in range(3)
    ).astype(BF16)
    hidden1_grad = hidden1_part.astype(F32) + swap(hidden1_part).astype(F32)
    norm1_gain_grad = jnp.sum(hidden1_grad * normed1, axis=0)
    norm1_bias_grad = jnp.sum(hidden1_grad, axis=0)
    input_grad = middle_grad + norm_back(hidden1_grad * norm1_gain, normed1, inverse1)

    small = jnp.concatenate(
        [
            tn(hidden2, logit_grad),
            out_bias_grad,
            norm2_gain_grad[:, None],
            norm2_bias_grad[:, None],
            proj_bias_grad[:, None],
        ],
        axis=1,
    )
    width = -(-small.shape[1] // 128) * 128
    small = jnp.pad(small, ((0, 0), (0, width - small.shape[1]))).astype(BF16)
    small = tn(mix_a, small)
    late = jnp.stack(
        [
            norm1_gain_grad,
            norm1_bias_grad,
            jnp.concatenate([qv_sums[:head_cols], qv_sums[2 * head_cols :]]),
        ]
    )
    for bit in bits:
        late = late + across(late, bit, sources)
    qv_bias_grad = late[2].reshape(2, head_cols)
    v_total, out_back = lax.optimization_barrier((v_total, out_back))
    out_home = nn(onehot, over_group(out_back).reshape(-1, feat_dim)).astype(BF16)
    out_home = out_home.astype(F32) + swap(out_home).astype(F32)
    output = (middle + (out_home + exact(gate_map, expert_out_bias))).astype(BF16)

    part_a = jnp.concatenate([qk_total, small], axis=1)
    part_b = jnp.concatenate([v_total, proj_total], axis=1)
    sums = reduce_rounds([part_a, part_b], orders, sources)
    mine, got = spread_rounds(sums, orders, sources)
    qkv_grad, proj_grad, small = finish(mix_a, mix_b, mine, got, head_cols, width)
    router_grad = small[:, :experts]
    out_bias_grad = small[:, experts : 2 * experts].T
    norm2_gain_grad, norm2_bias_grad, proj_bias_grad = (
        small[:, 2 * experts + i] for i in range(3)
    )
    return (
        output,
        input_grad,
        late[0],
        late[1],
        qkv_grad,
        qv_bias_grad,
        proj_grad,
        proj_bias_grad,
        norm2_gain_grad,
        norm2_bias_grad,
        router_grad,
        in_weight_grad[None],
        in_bias_grad[None],
        out_weight_grad[None],
        out_bias_grad,
    )


def solution(mesh):
    return jax.shard_map(
        local,
        mesh=mesh,
        in_specs=(
            P("dp", None),
            P(),
            P(),
            P(None, None, "tensor"),
            P(None, "tensor"),
            P("tensor", None),
            P(),
            P(),
            P(),
            P(),
            P("dp", None, "tensor"),
            P("dp", "tensor"),
            P("dp", "tensor", None),
            P(),
            P("dp", None),
            P("dp", None),
        ),
        out_specs=(
            P("dp", None),
            P("dp", None),
            P(),
            P(),
            P(None, None, "tensor"),
            P(None, "tensor"),
            P("tensor", None),
            P(),
            P(),
            P(),
            P(),
            P("dp", None, "tensor"),
            P("dp", "tensor"),
            P("dp", "tensor", None),
            P(),
        ),
        check_vma=False,
    )
```

```python
import jax
import jax.numpy as jnp
from jax import lax
from jax.experimental import pallas as pl
from jax.experimental.pallas import tpu as pltpu
from jax.sharding import PartitionSpec as P

HEAD = 64
SEQ = 197
F32 = jnp.float32
BF16 = jnp.bfloat16

epsilon = 1e-06


def norm_parts(values):
    average = jnp.mean(values, axis=-1, keepdims=True)
    centred = values - average
    inverse = lax.rsqrt(jnp.mean(centred * centred, axis=-1, keepdims=True) + epsilon)
    return (centred * inverse, inverse)


def norm_back(inner_grad, normed, inverse):
    first_mean = jnp.mean(inner_grad, axis=-1, keepdims=True)
    second_mean = jnp.mean(inner_grad * normed, axis=-1, keepdims=True)
    return inverse * (inner_grad - first_mean - normed * second_mean)


def gelu_parts(pre_act):
    normal_cdf = 0.5 * (1.0 + lax.erf(pre_act * 0.7071067811865476))
    density = jnp.exp(-0.5 * pre_act * pre_act) * 0.3989422804014327
    return (pre_act * normal_cdf, normal_cdf + pre_act * density)


def dot(a, b, dims, out=F32):
    return lax.dot_general(a, b, (dims, ((), ())), preferred_element_type=out)


def nn(a, b):
    return dot(a, b, ((1,), (0,)))


def nt(a, b):
    return dot(a, b, ((1,), (1,)))


def tn(a, b):
    return dot(a, b, ((0,), (0,)))


def exact(a, b):
    return lax.dot_general(
        a,
        b,
        (((1,), (0,)), ((), ())),
        precision=lax.Precision.HIGHEST,
        preferred_element_type=F32,
    )


def swap(x):
    return lax.ppermute(x, "tensor", [(0, 1), (1, 0)])


def across(x, bit, count):
    return lax.ppermute(x, "dp", [(i, i ^ bit) for i in range(count)])


def in_order(plane, mine, other, axis):
    first = jnp.where(plane == 0, mine, other)
    second = jnp.where(plane == 0, other, mine)
    return jnp.concatenate([first, second], axis=axis)


def half_of(plane, x, which):
    width = x.shape[-1] // 2
    low, high = x[..., :width], x[..., width:]
    return jnp.where((plane == which), low, high)


def along(x, orders, turn, count):
    return lax.ppermute(x, "dp", [(i, i ^ orders[i & 1][turn]) for i in range(count)])


def halve(total, orders, turn, count):
    middle = total.shape[0] // 2
    return total[:middle] + along(total[middle:].astype(BF16), orders, turn, count).astype(F32)


def finish_kernel(head_cols, experts, orders, me_ref, mine, got, qkv_ref, proj_ref, router_ref, bias_ref, norm_ref, held_proj, held_small):
    me = me_ref[0]
    count = 1 << len(orders[0])
    feat_dim = qkv_ref.shape[1]
    chunk = feat_dim // count
    half = count // 2
    odd = me % 2
    width = held_small.shape[1]
    for spot in range(count):
        names = []
        for order in orders:
            names.append(sum(bit for i, bit in enumerate(order) if (spot >> (len(order) - 1 - i)) & 1))
        if spot >= half:
            names = names[::-1]
        name = names[0] + odd * (names[1] - names[0])
        start = pl.multiple_of((name ^ me) * chunk, chunk)
        source = mine if spot < half else got
        first = (spot % half) * chunk
        piece = source[first : first + chunk, :].astype(F32)
        for j in range(3):
            qkv_ref[j, pl.ds(start, chunk), :] = piece[:, j * head_cols : (j + 1) * head_cols]
        held_proj[pl.ds(start, chunk), :] = piece[:, 3 * head_cols : 4 * head_cols]
        held_small[pl.ds(start, chunk), :] = piece[:, 4 * head_cols :]
    proj_ref[...] = held_proj[...].T
    small = held_small[...]
    router_ref[...] = small[:, :experts]
    flat = small.T
    bias_ref[...] = flat[experts : 2 * experts]
    norm_ref[...] = flat[2 * experts : 2 * experts + 8]


def finish(me, mine, got, head_cols, experts, feat_dim, orders):
    width = mine.shape[1] - 4 * head_cols
    vmem = pl.BlockSpec(memory_space=pltpu.VMEM)
    return pl.pallas_call(
        lambda *refs: finish_kernel(head_cols, experts, orders, *refs),
        in_specs=[pl.BlockSpec(memory_space=pltpu.SMEM), vmem, vmem],
        out_specs=[vmem] * 5,
        out_shape=(
            jax.ShapeDtypeStruct((3, feat_dim, head_cols), F32),
            jax.ShapeDtypeStruct((head_cols, feat_dim), F32),
            jax.ShapeDtypeStruct((feat_dim, experts), F32),
            jax.ShapeDtypeStruct((experts, feat_dim), F32),
            jax.ShapeDtypeStruct((8, feat_dim), F32),
        ),
        scratch_shapes=[
            pltpu.VMEM((feat_dim, head_cols), F32),
            pltpu.VMEM((feat_dim, width), F32),
        ],
        compiler_params=pltpu.CompilerParams(vmem_limit_bytes=40 << 20),
        name="finish",
    )(me[None], mine, got)


def local(
    inputs,
    norm1_gain,
    norm1_bias,
    qkv_weight,
    qv_bias,
    proj_weight,
    proj_bias,
    norm2_gain,
    norm2_bias,
    router,
    expert_in,
    expert_in_bias,
    expert_out,
    expert_out_bias,
    routes,
    cotangent,
):
    tok_count = inputs.shape[0]
    feat_dim = inputs.shape[1]
    half_dim = feat_dim // 2
    head_cols = qkv_weight.shape[2]
    heads_here = head_cols // HEAD
    images = tok_count // SEQ
    experts = router.shape[1]
    sources = lax.axis_size("dp")
    group_size = sources // experts
    capacity = max(2, (10 * tok_count + 3 * experts - 1) // (3 * experts))
    slots = (capacity + 3 + 15) // 16 * 16
    score_scale = HEAD ** (-0.5)
    plane = lax.axis_index("tensor")
    me = lax.axis_index("dp")
    own_expert = me // group_size
    in_weight, out_weight = expert_in[0], expert_out[0]

    expert_ids = jnp.arange(experts, dtype=jnp.int32)
    slot_ids = jnp.arange(slots, dtype=jnp.int32)
    all_ids = jnp.arange(experts * slots, dtype=jnp.int32)
    pick = [(routes[:, k : k + 1] == expert_ids[None, :]) for k in range(2)]
    named = (pick[0] | pick[1]).astype(BF16)
    before = (
        jnp.arange(tok_count)[:, None] > jnp.arange(tok_count)[None, :]
    ).astype(BF16)
    earlier = nn(before, named)
    rank = [
        jnp.sum(jnp.where(pick[k], earlier, 0.0), axis=1, keepdims=True).astype(jnp.int32)
        for k in range(2)
    ]
    place = [routes[:, k : k + 1] * slots + rank[k] for k in range(2)]
    onehot = ((place[0] == all_ids[None, :]) | (place[1] == all_ids[None, :])).astype(BF16)
    rank_hot = [(rank[k] == slot_ids[None, :]) for k in range(2)]
    pick_low = [pick[k].astype(BF16) for k in range(2)]
    partner = [
        jnp.where(rank_hot[k], routes[:, 1 - k : 2 - k].astype(F32), 0.0).astype(BF16)
        for k in range(2)
    ]
    partner_map = tn(pick_low[0], partner[0]) + tn(pick_low[1], partner[1])

    cot_half = half_of(plane, cotangent, 0)
    cot_send = tn(onehot, cot_half).astype(BF16).reshape(experts, slots, half_dim)
    note = jnp.pad(partner_map.astype(BF16), ((0, 0), (0, half_dim - slots)))[:, None, :]
    cot_send = jnp.where(slot_ids[None, :, None] == slots - 1, note, cot_send)
    cot_send = jnp.repeat(cot_send, group_size, axis=0)
    proj_other = swap(proj_weight)
    proj_full = in_order(plane, proj_weight, proj_other, 0)

    inputs, cot_send = lax.optimization_barrier((inputs, cot_send))
    cot_mine = lax.all_to_all(cot_send, "dp", split_axis=0, concat_axis=0, tiled=True)
    cot_mine = cot_mine.reshape(-1, half_dim)
    x_in = inputs.astype(F32)
    normed1, inverse1 = norm_parts(x_in)
    hidden1 = (normed1 * norm1_gain + norm1_bias).astype(BF16)
    projected = jnp.einsum("td,jde->jte", hidden1, qkv_weight, preferred_element_type=F32)
    bias_rows = jnp.stack([qv_bias[0], jnp.zeros_like(qv_bias[0]), qv_bias[1]])
    projected = (projected + bias_rows[:, None, :]).astype(BF16)
    heads_view = projected.reshape(3, images, SEQ, heads_here, HEAD)
    queries, key_vals, values_in = (heads_view[0], heads_view[1], heads_view[2])
    scores = (
        jnp.einsum("bqhd,bkhd->bhqk", queries, key_vals, preferred_element_type=F32)
        * score_scale
    )
    row_max = jnp.max(scores, axis=-1, keepdims=True)
    exp_scores = jnp.exp(scores - row_max)
    row_total = jnp.sum(exp_scores, axis=-1, keepdims=True)
    prob_vals = exp_scores / row_total
    prob_low = prob_vals.astype(BF16)
    attended = jnp.einsum("bhqk,bkhd->bqhd", prob_low, values_in, preferred_element_type=F32)
    attended = attended.reshape(tok_count, head_cols).astype(BF16)
    attended_other, cot_mine = lax.optimization_barrier((swap(attended), cot_mine))
    attended_all = in_order(plane, attended, attended_other, 1)
    middle = x_in + nn(attended_all, proj_full) + proj_bias
    normed2, inverse2 = norm_parts(middle)
    hidden2 = (normed2 * norm2_gain + norm2_bias).astype(BF16)

    send = tn(onehot, hidden2).astype(BF16).reshape(experts, slots, feat_dim)
    send = jnp.repeat(send, group_size, axis=0)
    cot_other = swap(cot_mine)
    arrived = lax.all_to_all(send, "dp", split_axis=0, concat_axis=0, tiled=True)
    arrived = arrived.reshape(-1, feat_dim)

    logits = nn(hidden2, router)
    chosen = [jnp.sum(jnp.where(pick[k], logits, 0.0), axis=1, keepdims=True) for k in range(2)]
    chosen_max = jnp.maximum(chosen[0], chosen[1])
    chosen_exp = [jnp.exp(chosen[k] - chosen_max) for k in range(2)]
    chosen_sum = chosen_exp[0] + chosen_exp[1]
    gate_vals = [chosen_exp[k] / chosen_sum for k in range(2)]
    gate_map = jnp.where(pick[0], gate_vals[0], 0.0) + jnp.where(pick[1], gate_vals[1], 0.0)
    grad_out = cotangent.astype(F32)
    row_grad = [(gate_vals[k] * grad_out).astype(BF16) for k in range(2)]
    out_bias_grad = tn(row_grad[0], pick_low[0]) + tn(row_grad[1], pick_low[1])

    note_rows = jnp.where(plane == 0, cot_mine, cot_other).reshape(sources, slots, half_dim)
    other_expert = note_rows[:, slots - 1, :slots].reshape(-1, 1).astype(jnp.int32)
    real_slot = (jnp.arange(sources * slots, dtype=jnp.int32)[:, None] % slots) < capacity
    row_logits = nn(arrived, router)
    own_logit = jnp.sum(
        jnp.where(expert_ids[None, :] == own_expert, row_logits, 0.0), axis=1, keepdims=True
    )
    other_logit = jnp.sum(
        jnp.where(expert_ids[None, :] == other_expert, row_logits, 0.0), axis=1, keepdims=True
    )
    top_logit = jnp.maximum(own_logit, other_logit)
    own_exp = jnp.exp(own_logit - top_logit)
    row_gate = own_exp / (own_exp + jnp.exp(other_logit - top_logit))
    row_gate = jnp.where(real_slot, row_gate, 0.0)
    cot_rows = in_order(plane, cot_mine, cot_other, 1)
    grad_rows = (row_gate * cot_rows.astype(F32)).astype(BF16)

    pre_act = nn(arrived, in_weight) + expert_in_bias[0]
    activ_vals, gelu_slope = gelu_parts(pre_act)
    activ_low = activ_vals.astype(BF16)
    act_grad = nt(grad_rows, out_weight) * gelu_slope
    in_bias_grad = jnp.sum(act_grad, axis=0)
    act_low = act_grad.astype(BF16)
    row_part = nt(act_low, in_weight)
    part_out = nn(activ_low, out_weight)

    inner = jnp.sum(cot_rows.astype(F32) * part_out, axis=1).reshape(sources, slots)
    inner_high = inner.astype(BF16)
    inner_low = (inner - inner_high.astype(F32)).astype(BF16)

    def widen(x):
        return jnp.pad(x, ((0, 0), (0, feat_dim - slots)))[:, None, :]

    row_send = row_part.astype(BF16).reshape(sources, slots, feat_dim)
    row_send = jnp.where(slot_ids[None, :, None] == slots - 1, widen(inner_high), row_send)
    row_send = jnp.where(slot_ids[None, :, None] == slots - 2, widen(inner_low), row_send)
    row_back = lax.all_to_all(row_send, "dp", split_axis=0, concat_axis=0, tiled=True)
    out_weight_grad = tn(activ_low, grad_rows)
    in_weight_grad = tn(arrived, act_low)
    row_back, out_weight_grad, in_weight_grad = lax.optimization_barrier(
        (row_back, out_weight_grad, in_weight_grad)
    )
    out_send = (row_gate * part_out).astype(BF16).reshape(sources, slots, feat_dim)
    out_send, row_back = lax.optimization_barrier((out_send, row_back))
    out_back = lax.all_to_all(out_send, "dp", split_axis=0, concat_axis=0, tiled=True)

    def over_group(x):
        if group_size == 1:
            return x
        shape = (experts, group_size) + x.shape[1:]
        return jnp.sum(x.reshape(shape).astype(F32), axis=1).astype(BF16)

    inner = row_back[:, slots - 2 :, :slots].astype(F32)
    inner = jnp.sum(inner.reshape(experts, 2 * group_size, slots), axis=1)
    inner = inner + swap(inner)
    gate_grad = []
    for k in range(2):
        found = exact(pick[k].astype(F32), inner)
        found = jnp.sum(jnp.where(rank_hot[k], found, 0.0), axis=1, keepdims=True)
        bias_row = exact(pick[k].astype(F32), expert_out_bias)
        gate_grad.append(found + jnp.sum(bias_row * grad_out, axis=1, keepdims=True))
    gate_mean = gate_vals[0] * gate_grad[0] + gate_vals[1] * gate_grad[1]
    chosen_grad = [gate_vals[k] * (gate_grad[k] - gate_mean) for k in range(2)]
    logit_grad = (
        jnp.where(pick[0], chosen_grad[0], 0.0) + jnp.where(pick[1], chosen_grad[1], 0.0)
    ).astype(BF16)
    row_home = nn(onehot, over_group(row_back).reshape(-1, feat_dim)).astype(BF16)
    row_home = row_home.astype(F32) + swap(row_home).astype(F32)
    hidden2_grad = row_home + nt(logit_grad, router)
    norm2_gain_grad = jnp.sum(hidden2_grad * normed2, axis=0)
    norm2_bias_grad = jnp.sum(hidden2_grad, axis=0)
    middle_grad = grad_out + norm_back(hidden2_grad * norm2_gain, normed2, inverse2)
    proj_bias_grad = jnp.sum(middle_grad, axis=0)
    middle_low = middle_grad.astype(BF16)

    bits = [1 << i for i in range(sources.bit_length() - 1)]
    orders = [bits, bits[:1] + bits[2:] + bits[1:2]]
    chunk = feat_dim // sources

    rows = jnp.arange(feat_dim, dtype=jnp.int32)[:, None]
    cols = jnp.arange(feat_dim, dtype=jnp.int32)[None, :]
    spot = cols // chunk
    piece = jnp.zeros_like(spot)
    for i in range(len(bits)):
        bit = jnp.where((me % 2 == 0) == (spot < sources // 2), orders[0][i], orders[1][i])
        piece = piece | jnp.where((spot >> (len(bits) - 1 - i)) & 1 == 1, bit, 0)
    mix = ((rows // chunk == (piece ^ me)) & (rows % chunk == cols % chunk)).astype(BF16)
    hidden1_mixed = nn(hidden1, mix).astype(BF16)
    proj_total = tn(nn(middle_low, mix).astype(BF16), attended)
    attended_grad = nt(middle_low, proj_weight).astype(BF16)
    attended_grad = attended_grad.reshape(images, SEQ, heads_here, HEAD)
    value_grad = jnp.einsum("bhqk,bqhd->bkhd", prob_low, attended_grad, preferred_element_type=F32)
    prob_grad = jnp.einsum("bqhd,bkhd->bhqk", attended_grad, values_in, preferred_element_type=F32)
    score_grad = prob_vals * (prob_grad - jnp.sum(prob_vals * prob_grad, axis=-1, keepdims=True))
    score_low = score_grad.astype(BF16)
    query_grad = (
        jnp.einsum("bhqk,bkhd->bqhd", score_low, key_vals, preferred_element_type=F32)
        * score_scale
    )
    key_grad = (
        jnp.einsum("bhqk,bqhd->bkhd", score_low, queries, preferred_element_type=F32)
        * score_scale
    )
    proj_low = [
        g.reshape(tok_count, head_cols).astype(BF16) for g in (query_grad, key_grad, value_grad)
    ]
    proj_low = jnp.concatenate(proj_low, axis=1)
    qkv_total = tn(hidden1_mixed, proj_low)
    qv_sums = jnp.sum(proj_low.astype(F32), axis=0)
    hidden1_part = sum(
        nt(proj_low[:, j * head_cols : (j + 1) * head_cols], qkv_weight[j]) for j in range(3)
    ).astype(BF16)
    hidden1_grad = hidden1_part.astype(F32) + swap(hidden1_part).astype(F32)
    norm1_gain_grad = jnp.sum(hidden1_grad * normed1, axis=0)
    norm1_bias_grad = jnp.sum(hidden1_grad, axis=0)
    input_grad = middle_grad + norm_back(hidden1_grad * norm1_gain, normed1, inverse1)

    small = jnp.concatenate(
        [
            tn(hidden2, logit_grad),
            out_bias_grad,
            norm2_gain_grad[:, None],
            norm2_bias_grad[:, None],
            proj_bias_grad[:, None],
        ],
        axis=1,
    )
    width = -(-small.shape[1] // 128) * 128
    small = jnp.pad(small, ((0, 0), (0, width - small.shape[1]))).astype(BF16)
    small = tn(mix, small)
    late = jnp.stack(
        [
            norm1_gain_grad,
            norm1_bias_grad,
            jnp.concatenate([qv_sums[:head_cols], qv_sums[2 * head_cols :]]),
        ]
    )
    for bit in bits:
        late = late + across(late, bit, sources)
    qv_bias_grad = late[2].reshape(2, head_cols)
    out_home = nn(onehot, over_group(out_back).reshape(-1, feat_dim)).astype(BF16)
    total = jnp.concatenate([qkv_total, proj_total, small], axis=1)
    total, out_home = lax.optimization_barrier((total, out_home))
    out_other = swap(out_home)
    total = halve(total, orders, 0, sources)
    total = halve(total, orders, 1, sources)
    total, out_other = lax.optimization_barrier((total, out_other))
    out_home = out_home.astype(F32) + out_other.astype(F32)
    output = (middle + (out_home + exact(gate_map, expert_out_bias))).astype(BF16)
    for turn in range(2, len(bits)):
        total = halve(total, orders, turn, sources)
    mine = total.astype(BF16)
    for turn in range(len(bits) - 1, 0, -1):
        mine = jnp.concatenate([mine, along(mine, orders, turn, sources)], axis=0)
    got = along(mine, orders, 0, sources)
    if chunk % 16 == 0:
        qkv_grad, proj_grad, router_grad, out_bias_grad, norm_grads = finish(
            me, mine, got, head_cols, experts, feat_dim, orders
        )
    else:
        whole = nn(mix, jnp.concatenate([mine, got], axis=0))
        qkv_grad = jnp.stack([whole[:, j * head_cols : (j + 1) * head_cols] for j in range(3)])
        proj_grad = whole[:, 3 * head_cols : 4 * head_cols].T
        router_grad = whole[:, 4 * head_cols : 4 * head_cols + experts]
        norm_grads = whole[:, 4 * head_cols + experts :].T
        out_bias_grad, norm_grads = norm_grads[:experts], norm_grads[experts:]
    norm2_gain_grad, norm2_bias_grad, proj_bias_grad = norm_grads[0], norm_grads[1], norm_grads[2]
    return (
        output,
        input_grad,
        late[0],
        late[1],
        qkv_grad,
        qv_bias_grad,
        proj_grad,
        proj_bias_grad,
        norm2_gain_grad,
        norm2_bias_grad,
        router_grad,
        in_weight_grad[None],
        in_bias_grad[None],
        out_weight_grad[None],
        out_bias_grad,
    )


def solution(mesh):
    return jax.shard_map(
        local,
        mesh=mesh,
        in_specs=(
            P("dp", None),
            P(),
            P(),
            P(None, None, "tensor"),
            P(None, "tensor"),
            P("tensor", None),
            P(),
            P(),
            P(),
            P(),
            P("dp", None, "tensor"),
            P("dp", "tensor"),
            P("dp", "tensor", None),
            P(),
            P("dp", None),
            P("dp", None),
        ),
        out_specs=(
            P("dp", None),
            P("dp", None),
            P(),
            P(),
            P(None, None, "tensor"),
            P(None, "tensor"),
            P("tensor", None),
            P(),
            P(),
            P(),
            P(),
            P("dp", None, "tensor"),
            P("dp", "tensor"),
            P("dp", "tensor", None),
            P(),
        ),
        check_vma=False,
    )
```

```python
import jax
import jax.numpy as jnp
from jax import lax
from jax.experimental import pallas as pl
from jax.experimental.pallas import tpu as pltpu
from jax.sharding import PartitionSpec as P

HEAD = 64
SEQ = 197
F32 = jnp.float32
BF16 = jnp.bfloat16

epsilon = 1e-06


def norm_parts(values):
    average = jnp.mean(values, axis=-1, keepdims=True)
    centred = values - average
    inverse = lax.rsqrt(jnp.mean(centred * centred, axis=-1, keepdims=True) + epsilon)
    return (centred * inverse, inverse)


def norm_back(inner_grad, normed, inverse):
    first_mean = jnp.mean(inner_grad, axis=-1, keepdims=True)
    second_mean = jnp.mean(inner_grad * normed, axis=-1, keepdims=True)
    return inverse * (inner_grad - first_mean - normed * second_mean)


def gelu_parts(pre_act):
    normal_cdf = 0.5 * (1.0 + lax.erf(pre_act * 0.7071067811865476))
    density = jnp.exp(-0.5 * pre_act * pre_act) * 0.3989422804014327
    return (pre_act * normal_cdf, normal_cdf + pre_act * density)


def dot(a, b, dims, out=F32):
    return lax.dot_general(a, b, (dims, ((), ())), preferred_element_type=out)


def nn(a, b):
    return dot(a, b, ((1,), (0,)))


def nt(a, b):
    return dot(a, b, ((1,), (1,)))


def tn(a, b):
    return dot(a, b, ((0,), (0,)))


def exact(a, b):
    return lax.dot_general(
        a,
        b,
        (((1,), (0,)), ((), ())),
        precision=lax.Precision.HIGHEST,
        preferred_element_type=F32,
    )


def swap(x):
    return lax.ppermute(x, "tensor", [(0, 1), (1, 0)])


def across(x, bit, count):
    return lax.ppermute(x, "dp", [(i, i ^ bit) for i in range(count)])


def in_order(plane, mine, other, axis):
    first = jnp.where(plane == 0, mine, other)
    second = jnp.where(plane == 0, other, mine)
    return jnp.concatenate([first, second], axis=axis)


def half_of(plane, x, which):
    width = x.shape[-1] // 2
    low, high = x[..., :width], x[..., width:]
    return jnp.where((plane == which), low, high)


def along(x, orders, turn, count):
    return lax.ppermute(x, "dp", [(i, i ^ orders[i & 1][turn]) for i in range(count)])


def halve(total, orders, turn, count):
    middle = total.shape[0] // 2
    return total[:middle] + along(total[middle:].astype(BF16), orders, turn, count).astype(F32)


def home_kernel(back_ref, onehot_ref, routes_ref, rank_ref, gates_ref, bias_dot_ref, home_ref, logit_ref, inner_ref):
    experts, slots, feat_dim = back_ref.shape
    tok_count = routes_ref.shape[0]
    home = nn(onehot_ref[...], back_ref[...].reshape(experts * slots, feat_dim))
    home_ref[...] = home.astype(BF16)
    for e in range(experts):
        inner_ref[0, e : e + 1, :] = back_ref[e, slots - 1 : slots, :slots].astype(F32)
        inner_ref[1, e : e + 1, :] = back_ref[e, slots - 2 : slots - 1, :slots].astype(F32)
    expert_ids = lax.broadcasted_iota(jnp.int32, (tok_count, experts), 1)
    slot_ids = lax.broadcasted_iota(jnp.int32, (tok_count, slots), 1)
    picks, inner_grads = [], []
    for k in range(2):
        pick = routes_ref[:, k : k + 1] == expert_ids
        hot = jnp.where(pick, 1.0, 0.0).astype(BF16)
        found = nn(hot, inner_ref[0].astype(BF16)) + nn(hot, inner_ref[1].astype(BF16))
        found = jnp.where(rank_ref[:, k : k + 1] == slot_ids, found, 0.0)
        own_bias = jnp.where(pick, bias_dot_ref[...], 0.0)
        inner_grads.append(
            jnp.sum(found, axis=1, keepdims=True) + jnp.sum(own_bias, axis=1, keepdims=True)
        )
        picks.append(pick)
    gates = [gates_ref[:, k : k + 1] for k in range(2)]
    mean = gates[0] * inner_grads[0] + gates[1] * inner_grads[1]
    logit_grad = 0.0
    for k in range(2):
        logit_grad = logit_grad + jnp.where(picks[k], gates[k] * (inner_grads[k] - mean), 0.0)
    logit_ref[...] = logit_grad.astype(BF16)


def home_rows(back, onehot, routes, rank, gates, bias_dot):
    experts, slots, feat_dim = back.shape
    tok_count = routes.shape[0]
    return pl.pallas_call(
        home_kernel,
        out_shape=(
            jax.ShapeDtypeStruct((tok_count, feat_dim), BF16),
            jax.ShapeDtypeStruct((tok_count, experts), BF16),
        ),
        scratch_shapes=[pltpu.VMEM((2, experts, slots), F32)],
        compiler_params=pltpu.CompilerParams(vmem_limit_bytes=24 << 20),
        cost_estimate=pl.CostEstimate(
            flops=2 * tok_count * feat_dim * experts * slots, bytes_accessed=2 << 20, transcendentals=0
        ),
        name="home_rows",
    )(back, onehot, routes, rank, gates, bias_dot)


def attention_grads_kernel(
    home_ref, other_ref, logit_ref, router_ref, cot_ref, normed_ref, inverse_ref, gain_ref, hidden2_ref, bias_grad_ref,
    proj_ref, projected_ref, lse_ref, attended_ref, hidden_ref, weight_ref, mix_ref,
    sent_ref, kept_ref, hidden_part_ref, sums_ref, middle_grad_ref, low_ref, back_ref, small_ref,
):
    head_cols = attended_ref.shape[1]
    experts = logit_ref.shape[1]
    scale = HEAD ** (-0.5)
    hidden_grad = home_ref[...].astype(F32) + other_ref[...].astype(F32) + nt(logit_ref[...], router_ref[...])
    normed = normed_ref[...]
    inner = hidden_grad * gain_ref[...]
    middle_grad = cot_ref[...].astype(F32) + norm_back(inner, normed, inverse_ref[...])
    middle_grad_ref[...] = middle_grad
    middle_low = middle_grad.astype(BF16)
    small_ref[...] = jnp.zeros_like(small_ref)
    small_ref[:experts, :] = tn(logit_ref[...], hidden2_ref[...])
    small_ref[experts : 2 * experts, :] = bias_grad_ref[...]
    small_ref[2 * experts : 2 * experts + 1, :] = jnp.sum(hidden_grad * normed, axis=0, keepdims=True)
    small_ref[2 * experts + 1 : 2 * experts + 2, :] = jnp.sum(hidden_grad, axis=0, keepdims=True)
    small_ref[2 * experts + 2 : 2 * experts + 3, :] = jnp.sum(middle_grad, axis=0, keepdims=True)
    back_ref[...] = nt(middle_low, proj_ref[...]).astype(BF16)
    for h in range(head_cols // HEAD):
        cols = slice(h * HEAD, (h + 1) * HEAD)
        queries, key_vals, values_in = (projected_ref[j, :, cols] for j in range(3))
        out_grad = back_ref[:, cols]
        prob_vals = jnp.exp(nt(queries, key_vals) * scale - lse_ref[:, h : h + 1])
        prob_low = prob_vals.astype(BF16)
        prob_grad = nt(out_grad, values_in)
        row = jnp.sum(prob_vals * prob_grad, axis=-1, keepdims=True)
        score_low = (prob_vals * (prob_grad - row)).astype(BF16)
        low_ref[:, h * HEAD : (h + 1) * HEAD] = (nn(score_low, key_vals) * scale).astype(BF16)
        start = head_cols + h * HEAD
        low_ref[:, start : start + HEAD] = (tn(score_low, queries) * scale).astype(BF16)
        start = start + head_cols
        low_ref[:, start : start + HEAD] = tn(prob_low, out_grad).astype(BF16)
    low = low_ref[...]
    half = kept_ref.shape[0]
    mixed_middle = nt(mix_ref[...], middle_low).astype(BF16)
    small = small_ref[...].astype(BF16)
    for part in range(2):
        rows = slice(part * half, (part + 1) * half)
        pieces = (
            nn(hidden_ref[rows, :], low),
            nn(mixed_middle[rows, :], attended_ref[...]),
            nt(mix_ref[rows, :], small),
        )
        first = 0
        for piece in pieces:
            last = first + piece.shape[1]
            if part == 0:
                kept_ref[:, first:last] = piece
            else:
                sent_ref[:, first:last] = piece.astype(BF16)
            first = last
    part = nt(low[:, :head_cols], weight_ref[0])
    part = part + nt(low[:, head_cols : 2 * head_cols], weight_ref[1])
    part = part + nt(low[:, 2 * head_cols :], weight_ref[2])
    hidden_part_ref[...] = part.astype(BF16)
    sums_ref[...] = jnp.sum(low.astype(F32), axis=0, keepdims=True)


def attention_grads(*operands):
    tok_count, feat_dim = operands[0].shape
    experts = operands[2].shape[1]
    head_cols = operands[10].shape[0]
    small = -(-(2 * experts + 3) // 128) * 128
    width = 4 * head_cols + small
    flops = 2 * tok_count * feat_dim * head_cols * 9 + 2 * feat_dim * feat_dim * (tok_count + small)
    return pl.pallas_call(
        attention_grads_kernel,
        out_shape=(
            jax.ShapeDtypeStruct((feat_dim // 2, width), BF16),
            jax.ShapeDtypeStruct((feat_dim // 2, width), F32),
            jax.ShapeDtypeStruct((tok_count, feat_dim), BF16),
            jax.ShapeDtypeStruct((1, 3 * head_cols), F32),
            jax.ShapeDtypeStruct((tok_count, feat_dim), F32),
        ),
        scratch_shapes=[
            pltpu.VMEM((tok_count, 3 * head_cols), BF16),
            pltpu.VMEM((tok_count, head_cols), BF16),
            pltpu.VMEM((small, feat_dim), F32),
        ],
        compiler_params=pltpu.CompilerParams(vmem_limit_bytes=40 << 20),
        cost_estimate=pl.CostEstimate(
            flops=flops, bytes_accessed=10 << 20, transcendentals=tok_count * tok_count * 6
        ),
        name="attention_grads",
    )(*operands)


def finish_kernel(head_cols, experts, orders, me_ref, mine, got, qkv_ref, proj_ref, router_ref, bias_ref, norm_ref, held_proj, held_small):
    me = me_ref[0]
    count = 1 << len(orders[0])
    feat_dim = qkv_ref.shape[1]
    chunk = feat_dim // count
    half = count // 2
    odd = me % 2
    width = held_small.shape[1]
    for spot in range(count):
        names = []
        for order in orders:
            names.append(sum(bit for i, bit in enumerate(order) if (spot >> (len(order) - 1 - i)) & 1))
        if spot >= half:
            names = names[::-1]
        name = names[0] + odd * (names[1] - names[0])
        start = pl.multiple_of((name ^ me) * chunk, chunk)
        source = mine if spot < half else got
        first = (spot % half) * chunk
        piece = source[first : first + chunk, :].astype(F32)
        for j in range(3):
            qkv_ref[j, pl.ds(start, chunk), :] = piece[:, j * head_cols : (j + 1) * head_cols]
        held_proj[pl.ds(start, chunk), :] = piece[:, 3 * head_cols : 4 * head_cols]
        held_small[pl.ds(start, chunk), :] = piece[:, 4 * head_cols :]
    proj_ref[...] = held_proj[...].T
    small = held_small[...]
    router_ref[...] = small[:, :experts]
    flat = small.T
    bias_ref[...] = flat[experts : 2 * experts]
    norm_ref[...] = flat[2 * experts : 2 * experts + 8]


def finish(me, mine, came, head_cols, experts, feat_dim, orders):
    width = mine.shape[1] - 4 * head_cols
    vmem = pl.BlockSpec(memory_space=pltpu.VMEM)
    return pl.pallas_call(
        lambda *refs: finish_kernel(head_cols, experts, orders, *refs),
        in_specs=[pl.BlockSpec(memory_space=pltpu.SMEM), vmem, vmem],
        out_specs=[vmem] * 5,
        out_shape=(
            jax.ShapeDtypeStruct((3, feat_dim, head_cols), F32),
            jax.ShapeDtypeStruct((head_cols, feat_dim), F32),
            jax.ShapeDtypeStruct((feat_dim, experts), F32),
            jax.ShapeDtypeStruct((experts, feat_dim), F32),
            jax.ShapeDtypeStruct((8, feat_dim), F32),
        ),
        scratch_shapes=[
            pltpu.VMEM((feat_dim, head_cols), F32),
            pltpu.VMEM((feat_dim, width), F32),
        ],
        compiler_params=pltpu.CompilerParams(vmem_limit_bytes=40 << 20),
        name="finish",
    )(me[None], mine, came)


def high_low(values):
    high = values.astype(BF16)
    return high, (values - high.astype(F32)).astype(BF16)


def local(
    inputs,
    norm1_gain,
    norm1_bias,
    qkv_weight,
    qv_bias,
    proj_weight,
    proj_bias,
    norm2_gain,
    norm2_bias,
    router,
    expert_in,
    expert_in_bias,
    expert_out,
    expert_out_bias,
    routes,
    cotangent,
):
    tok_count = inputs.shape[0]
    feat_dim = inputs.shape[1]
    half_dim = feat_dim // 2
    head_cols = qkv_weight.shape[2]
    heads_here = head_cols // HEAD
    images = tok_count // SEQ
    experts = router.shape[1]
    sources = lax.axis_size("dp")
    group_size = sources // experts
    capacity = max(2, (10 * tok_count + 3 * experts - 1) // (3 * experts))
    slots = (capacity + 3 + 15) // 16 * 16
    score_scale = HEAD ** (-0.5)
    plane = lax.axis_index("tensor")
    me = lax.axis_index("dp")
    own_expert = me // group_size
    in_weight, out_weight = expert_in[0], expert_out[0]

    expert_ids = jnp.arange(experts, dtype=jnp.int32)
    slot_ids = jnp.arange(slots, dtype=jnp.int32)
    all_ids = jnp.arange(experts * slots, dtype=jnp.int32)
    pick = [(routes[:, k : k + 1] == expert_ids[None, :]) for k in range(2)]
    named = (pick[0] | pick[1]).astype(BF16)
    before = (
        jnp.arange(tok_count)[:, None] > jnp.arange(tok_count)[None, :]
    ).astype(BF16)
    earlier = nn(before, named)
    rank = [
        jnp.sum(jnp.where(pick[k], earlier, 0.0), axis=1, keepdims=True).astype(jnp.int32)
        for k in range(2)
    ]
    place = [routes[:, k : k + 1] * slots + rank[k] for k in range(2)]
    onehot = ((place[0] == all_ids[None, :]) | (place[1] == all_ids[None, :])).astype(BF16)
    rank_hot = [(rank[k] == slot_ids[None, :]) for k in range(2)]
    pick_low = [pick[k].astype(BF16) for k in range(2)]
    partner = [
        jnp.where(rank_hot[k], routes[:, 1 - k : 2 - k].astype(F32), 0.0).astype(BF16)
        for k in range(2)
    ]
    partner_map = tn(pick_low[0], partner[0]) + tn(pick_low[1], partner[1])

    cot_half = half_of(plane, cotangent, 0)
    cot_send = tn(onehot, cot_half).astype(BF16).reshape(experts, slots, half_dim)
    note = jnp.pad(partner_map.astype(BF16), ((0, 0), (0, half_dim - slots)))[:, None, :]
    cot_send = jnp.where(slot_ids[None, :, None] == slots - 1, note, cot_send)
    cot_send = jnp.repeat(cot_send, group_size, axis=0)
    proj_other = swap(proj_weight)
    proj_full = in_order(plane, proj_weight, proj_other, 0)

    inputs, cot_send = lax.optimization_barrier((inputs, cot_send))
    cot_mine = lax.all_to_all(cot_send, "dp", split_axis=0, concat_axis=0, tiled=True)
    cot_mine = cot_mine.reshape(-1, half_dim)
    x_in = inputs.astype(F32)
    normed1, inverse1 = norm_parts(x_in)
    hidden1 = (normed1 * norm1_gain + norm1_bias).astype(BF16)
    projected = jnp.einsum("td,jde->jte", hidden1, qkv_weight, preferred_element_type=F32)
    bias_rows = jnp.stack([qv_bias[0], jnp.zeros_like(qv_bias[0]), qv_bias[1]])
    projected = (projected + bias_rows[:, None, :]).astype(BF16)
    heads_view = projected.reshape(3, images, SEQ, heads_here, HEAD)
    queries, key_vals, values_in = (heads_view[0], heads_view[1], heads_view[2])
    scores = (
        jnp.einsum("bqhd,bkhd->bhqk", queries, key_vals, preferred_element_type=F32)
        * score_scale
    )
    row_max = jnp.max(scores, axis=-1, keepdims=True)
    exp_scores = jnp.exp(scores - row_max)
    row_total = jnp.sum(exp_scores, axis=-1, keepdims=True)
    lse = (row_max + jnp.log(row_total)).reshape(heads_here, tok_count).T
    prob_low = (exp_scores / row_total).astype(BF16)
    attended = jnp.einsum("bhqk,bkhd->bqhd", prob_low, values_in, preferred_element_type=F32)
    attended = attended.reshape(tok_count, head_cols).astype(BF16)
    attended_other, cot_mine = lax.optimization_barrier((swap(attended), cot_mine))
    attended_all = in_order(plane, attended, attended_other, 1)
    middle = x_in + nn(attended_all, proj_full) + proj_bias
    normed2, inverse2 = norm_parts(middle)
    hidden2 = (normed2 * norm2_gain + norm2_bias).astype(BF16)

    send = tn(onehot, hidden2).astype(BF16).reshape(experts, slots, feat_dim)
    send = jnp.repeat(send, group_size, axis=0)
    cot_other = swap(cot_mine)
    arrived = lax.all_to_all(send, "dp", split_axis=0, concat_axis=0, tiled=True)
    arrived = arrived.reshape(-1, feat_dim)

    logits = nn(hidden2, router)
    chosen = [jnp.sum(jnp.where(pick[k], logits, 0.0), axis=1, keepdims=True) for k in range(2)]
    chosen_max = jnp.maximum(chosen[0], chosen[1])
    chosen_exp = [jnp.exp(chosen[k] - chosen_max) for k in range(2)]
    chosen_sum = chosen_exp[0] + chosen_exp[1]
    gate_vals = [chosen_exp[k] / chosen_sum for k in range(2)]
    gate_map = jnp.where(pick[0], gate_vals[0], 0.0) + jnp.where(pick[1], gate_vals[1], 0.0)
    grad_out = cotangent.astype(F32)
    row_grad = [(gate_vals[k] * grad_out).astype(BF16) for k in range(2)]
    out_bias_grad = tn(pick_low[0], row_grad[0]) + tn(pick_low[1], row_grad[1])

    note_rows = jnp.where(plane == 0, cot_mine, cot_other).reshape(sources, slots, half_dim)
    other_expert = note_rows[:, slots - 1, :slots].reshape(-1, 1).astype(jnp.int32)
    real_slot = (jnp.arange(sources * slots, dtype=jnp.int32)[:, None] % slots) < capacity
    row_logits = nn(arrived, router)
    own_logit = jnp.sum(
        jnp.where(expert_ids[None, :] == own_expert, row_logits, 0.0), axis=1, keepdims=True
    )
    other_logit = jnp.sum(
        jnp.where(expert_ids[None, :] == other_expert, row_logits, 0.0), axis=1, keepdims=True
    )
    top_logit = jnp.maximum(own_logit, other_logit)
    own_exp = jnp.exp(own_logit - top_logit)
    row_gate = own_exp / (own_exp + jnp.exp(other_logit - top_logit))
    row_gate = jnp.where(real_slot, row_gate, 0.0)
    cot_rows = in_order(plane, cot_mine, cot_other, 1)
    grad_rows = (row_gate * cot_rows.astype(F32)).astype(BF16)

    pre_act = nn(arrived, in_weight) + expert_in_bias[0]
    activ_vals, gelu_slope = gelu_parts(pre_act)
    activ_low = activ_vals.astype(BF16)
    part_out = nn(activ_low, out_weight)
    act_grad = nt(grad_rows, out_weight) * gelu_slope
    in_bias_grad = jnp.sum(act_grad, axis=0)
    act_low = act_grad.astype(BF16)
    row_part = nt(act_low, in_weight)

    inner = jnp.sum(cot_rows.astype(F32) * part_out, axis=1).reshape(sources, slots)
    inner = inner + swap(inner)
    inner_high = inner.astype(BF16)
    inner_low = (inner - inner_high.astype(F32)).astype(BF16)

    def widen(x):
        return jnp.pad(x, ((0, 0), (0, feat_dim - slots)))[:, None, :]

    row_send = row_part.astype(BF16).reshape(sources, slots, feat_dim)
    row_send = jnp.where(slot_ids[None, :, None] == slots - 1, widen(inner_high), row_send)
    row_send = jnp.where(slot_ids[None, :, None] == slots - 2, widen(inner_low), row_send)
    row_back = lax.all_to_all(row_send, "dp", split_axis=0, concat_axis=0, tiled=True)
    out_weight_grad = tn(activ_low, grad_rows)
    in_weight_grad = tn(arrived, act_low)
    bits = [1 << i for i in range(sources.bit_length() - 1)]
    orders = [bits, bits[:1] + bits[2:] + bits[1:2]]
    chunk = feat_dim // sources

    rows = jnp.arange(feat_dim, dtype=jnp.int32)[None, :]
    cols = jnp.arange(feat_dim, dtype=jnp.int32)[:, None]
    spot = cols // chunk
    piece = jnp.zeros_like(spot)
    for i in range(len(bits)):
        bit = jnp.where((me % 2 == 0) == (spot < sources // 2), orders[0][i], orders[1][i])
        piece = piece | jnp.where((spot >> (len(bits) - 1 - i)) & 1 == 1, bit, 0)
    mix_t = ((rows // chunk == (piece ^ me)) & (rows % chunk == cols % chunk)).astype(BF16)
    hidden1_t = nt(mix_t, hidden1).astype(BF16)
    bias_dot = lax.dot_general(
        grad_out,
        expert_out_bias,
        (((1,), (1,)), ((), ())),
        precision=lax.Precision.HIGHEST,
        preferred_element_type=F32,
    )
    rank_pair = jnp.concatenate(rank, axis=1)
    gate_pair = jnp.concatenate(gate_vals, axis=1)
    out_send = (row_gate * part_out).astype(BF16).reshape(sources, slots, feat_dim)
    ready = (
        out_weight_grad, in_weight_grad, in_bias_grad, out_send, mix_t, hidden1_t, bias_dot, rank_pair,
        gate_pair, onehot, out_bias_grad, normed2, inverse2, hidden2, lse, projected, gate_map,
    )
    row_back, ready = lax.optimization_barrier((row_back, ready))
    (
        out_weight_grad, in_weight_grad, in_bias_grad, out_send, mix_t, hidden1_t, bias_dot, rank_pair,
        gate_pair, onehot, out_bias_grad, normed2, inverse2, hidden2, lse, projected, gate_map,
    ) = ready

    def over_group(x):
        if group_size == 1:
            return x
        shape = (experts, group_size) + x.shape[1:]
        return jnp.sum(x.reshape(shape).astype(F32), axis=1).astype(BF16)

    row_home, logit_grad = home_rows(
        over_group(row_back),
        onehot,
        routes,
        rank_pair,
        gate_pair,
        bias_dot,
    )
    out_send, row_home = lax.optimization_barrier((out_send, row_home))
    row_other = swap(row_home)
    out_back = lax.all_to_all(out_send, "dp", split_axis=0, concat_axis=0, tiled=True)

    sent, kept, hidden1_part, qv_sums, middle_grad = attention_grads(
        row_home,
        row_other,
        logit_grad,
        router,
        cotangent,
        normed2,
        inverse2,
        norm2_gain[None],
        hidden2,
        out_bias_grad,
        proj_weight,
        projected,
        lse,
        attended,
        hidden1_t,
        qkv_weight,
        mix_t,
    )
    hidden1_grad = hidden1_part.astype(F32) + swap(hidden1_part).astype(F32)
    norm1_gain_grad = jnp.sum(hidden1_grad * normed1, axis=0)
    norm1_bias_grad = jnp.sum(hidden1_grad, axis=0)
    input_grad = middle_grad + norm_back(hidden1_grad * norm1_gain, normed1, inverse1)

    out_home = nn(onehot, over_group(out_back).reshape(-1, feat_dim)).astype(BF16)
    sent, out_home = lax.optimization_barrier((sent, out_home))
    out_other = swap(out_home)
    total = kept + along(sent, orders, 0, sources).astype(F32)
    total = halve(total, orders, 1, sources)
    total, out_other = lax.optimization_barrier((total, out_other))
    out_home = out_home.astype(F32) + out_other.astype(F32)
    output = (middle + (out_home + exact(gate_map, expert_out_bias))).astype(BF16)
    for turn in range(2, len(bits)):
        total = halve(total, orders, turn, sources)
    mine = total.astype(BF16)
    full = mine.shape[1]
    late = jnp.stack(
        [
            norm1_gain_grad,
            norm1_bias_grad,
            jnp.concatenate([qv_sums[0, :head_cols], qv_sums[0, 2 * head_cols :]]),
        ]
    )
    late = jnp.pad(late, ((0, 5), (0, 0)))
    for turn in range(len(bits) - 1, -1, -1):
        high, low = high_low(late)
        extra = jnp.pad(jnp.concatenate([high, low], axis=0), ((0, 0), (0, full - feat_dim)))
        came = along(jnp.concatenate([mine, extra], axis=0), orders, turn, sources)
        size = mine.shape[0]
        other = came[size : size + 8, :feat_dim].astype(F32) + came[size + 8 :, :feat_dim].astype(F32)
        late = (high.astype(F32) + low.astype(F32)) + other
        if turn > 0:
            mine = jnp.concatenate([mine, came[:size]], axis=0)
    got = came[:size]
    qv_bias_grad = late[2].reshape(2, head_cols)
    if chunk % 16 == 0:
        qkv_grad, proj_grad, router_grad, out_bias_grad, norm_grads = finish(
            me, mine, came, head_cols, experts, feat_dim, orders
        )
    else:
        whole = tn(mix_t, jnp.concatenate([mine, got], axis=0))
        qkv_grad = jnp.stack([whole[:, j * head_cols : (j + 1) * head_cols] for j in range(3)])
        proj_grad = whole[:, 3 * head_cols : 4 * head_cols].T
        router_grad = whole[:, 4 * head_cols : 4 * head_cols + experts]
        norm_grads = whole[:, 4 * head_cols + experts :].T
        out_bias_grad, norm_grads = norm_grads[:experts], norm_grads[experts:]
    norm2_gain_grad, norm2_bias_grad, proj_bias_grad = norm_grads[0], norm_grads[1], norm_grads[2]
    return (
        output,
        input_grad,
        late[0],
        late[1],
        qkv_grad,
        qv_bias_grad,
        proj_grad,
        proj_bias_grad,
        norm2_gain_grad,
        norm2_bias_grad,
        router_grad,
        in_weight_grad[None],
        in_bias_grad[None],
        out_weight_grad[None],
        out_bias_grad,
    )


def solution(mesh):
    return jax.shard_map(
        local,
        mesh=mesh,
        in_specs=(
            P("dp", None),
            P(),
            P(),
            P(None, None, "tensor"),
            P(None, "tensor"),
            P("tensor", None),
            P(),
            P(),
            P(),
            P(),
            P("dp", None, "tensor"),
            P("dp", "tensor"),
            P("dp", "tensor", None),
            P(),
            P("dp", None),
            P("dp", None),
        ),
        out_specs=(
            P("dp", None),
            P("dp", None),
            P(),
            P(),
            P(None, None, "tensor"),
            P(None, "tensor"),
            P("tensor", None),
            P(),
            P(),
            P(),
            P(),
            P("dp", None, "tensor"),
            P("dp", "tensor"),
            P("dp", "tensor", None),
            P(),
        ),
        check_vma=False,
    )
```

```python
import jax
import jax.numpy as jnp
from jax import lax
from jax.experimental import pallas as pl
from jax.experimental.pallas import tpu as pltpu
from jax.sharding import PartitionSpec as P

HEAD = 64
SEQ = 197
F32 = jnp.float32
BF16 = jnp.bfloat16

epsilon = 1e-06


def norm_parts(values):
    average = jnp.mean(values, axis=-1, keepdims=True)
    centred = values - average
    inverse = lax.rsqrt(jnp.mean(centred * centred, axis=-1, keepdims=True) + epsilon)
    return (centred * inverse, inverse)


def norm_back(inner_grad, normed, inverse):
    first_mean = jnp.mean(inner_grad, axis=-1, keepdims=True)
    second_mean = jnp.mean(inner_grad * normed, axis=-1, keepdims=True)
    return inverse * (inner_grad - first_mean - normed * second_mean)


def gelu_parts(pre_act):
    normal_cdf = 0.5 * (1.0 + lax.erf(pre_act * 0.7071067811865476))
    density = jnp.exp(-0.5 * pre_act * pre_act) * 0.3989422804014327
    return (pre_act * normal_cdf, normal_cdf + pre_act * density)


def dot(a, b, dims, out=F32):
    return lax.dot_general(a, b, (dims, ((), ())), preferred_element_type=out)


def nn(a, b):
    return dot(a, b, ((1,), (0,)))


def nt(a, b):
    return dot(a, b, ((1,), (1,)))


def tn(a, b):
    return dot(a, b, ((0,), (0,)))


def exact(a, b):
    return lax.dot_general(
        a,
        b,
        (((1,), (0,)), ((), ())),
        precision=lax.Precision.HIGHEST,
        preferred_element_type=F32,
    )


def swap(x):
    return lax.ppermute(x, "tensor", [(0, 1), (1, 0)])


def across(x, bit, count):
    return lax.ppermute(x, "dp", [(i, i ^ bit) for i in range(count)])


def in_order(plane, mine, other, axis):
    first = jnp.where(plane == 0, mine, other)
    second = jnp.where(plane == 0, other, mine)
    return jnp.concatenate([first, second], axis=axis)


def half_of(plane, x, which):
    width = x.shape[-1] // 2
    low, high = x[..., :width], x[..., width:]
    return jnp.where((plane == which), low, high)


def keep_half(total, came):
    middle = total.shape[0] // 2
    return total[:middle] + came.astype(F32)


def send_half(total, bit, count):
    return across(total[total.shape[0] // 2 :].astype(BF16), bit, count)


def home_kernel(back_ref, onehot_ref, facts_ref, home_ref, logit_ref, inner_ref):
    experts, slots, feat_dim = back_ref.shape
    tok_count = facts_ref.shape[0]
    home = nn(onehot_ref[...], back_ref[...].reshape(experts * slots, feat_dim))
    home_ref[...] = home.astype(BF16)
    for e in range(experts):
        inner_ref[0, e : e + 1, :] = back_ref[e, slots - 1 : slots, :slots].astype(F32)
        inner_ref[1, e : e + 1, :] = back_ref[e, slots - 2 : slots - 1, :slots].astype(F32)
    expert_ids = lax.broadcasted_iota(jnp.int32, (tok_count, experts), 1).astype(F32)
    slot_ids = lax.broadcasted_iota(jnp.int32, (tok_count, slots), 1).astype(F32)
    bias_dot = facts_ref[:, 16 : 16 + experts]
    picks, inner_grads = [], []
    for k in range(2):
        pick = facts_ref[:, k : k + 1] == expert_ids
        hot = jnp.where(pick, 1.0, 0.0).astype(BF16)
        found = nn(hot, inner_ref[0].astype(BF16)) + nn(hot, inner_ref[1].astype(BF16))
        found = jnp.where(facts_ref[:, k + 2 : k + 3] == slot_ids, found, 0.0)
        own_bias = jnp.where(pick, bias_dot, 0.0)
        inner_grads.append(
            jnp.sum(found, axis=1, keepdims=True) + jnp.sum(own_bias, axis=1, keepdims=True)
        )
        picks.append(pick)
    gates = [facts_ref[:, k + 4 : k + 5] for k in range(2)]
    mean = gates[0] * inner_grads[0] + gates[1] * inner_grads[1]
    logit_grad = 0.0
    for k in range(2):
        logit_grad = logit_grad + jnp.where(picks[k], gates[k] * (inner_grads[k] - mean), 0.0)
    logit_ref[...] = logit_grad.astype(BF16)


def home_rows(back, onehot, facts):
    experts, slots, feat_dim = back.shape
    tok_count = facts.shape[0]
    return pl.pallas_call(
        home_kernel,
        out_shape=(
            jax.ShapeDtypeStruct((tok_count, feat_dim), BF16),
            jax.ShapeDtypeStruct((tok_count, experts), BF16),
        ),
        scratch_shapes=[pltpu.VMEM((2, experts, slots), F32)],
        compiler_params=pltpu.CompilerParams(vmem_limit_bytes=60 << 20),
        cost_estimate=pl.CostEstimate(
            flops=2 * tok_count * feat_dim * experts * slots, bytes_accessed=2 << 20, transcendentals=0
        ),
        name="home_rows",
    )(back, onehot, facts)


def attention_grads_kernel(
    home_ref, other_ref, logit_ref, router_ref, cot_ref, normed_ref, facts_ref, gain_ref, hidden2_ref, bias_grad_ref,
    proj_ref, projected_ref, attended_ref, hidden_ref, weight_ref, mix_ref,
    sent_ref, kept_ref, hidden_part_ref, sums_ref, middle_grad_ref, low_ref, back_ref, small_ref,
):
    head_cols = attended_ref.shape[1]
    experts = logit_ref.shape[1]
    scale = HEAD ** (-0.5)
    hidden_grad = home_ref[...].astype(F32) + other_ref[...].astype(F32) + nt(logit_ref[...], router_ref[...])
    normed = normed_ref[...]
    inner = hidden_grad * gain_ref[...]
    middle_grad = cot_ref[...].astype(F32) + norm_back(inner, normed, facts_ref[:, 6:7])
    middle_grad_ref[...] = middle_grad
    middle_low = middle_grad.astype(BF16)
    small_ref[...] = jnp.zeros_like(small_ref)
    small_ref[:experts, :] = tn(logit_ref[...], hidden2_ref[...])
    small_ref[experts : 2 * experts, :] = bias_grad_ref[...]
    small_ref[2 * experts : 2 * experts + 1, :] = jnp.sum(hidden_grad * normed, axis=0, keepdims=True)
    small_ref[2 * experts + 1 : 2 * experts + 2, :] = jnp.sum(hidden_grad, axis=0, keepdims=True)
    small_ref[2 * experts + 2 : 2 * experts + 3, :] = jnp.sum(middle_grad, axis=0, keepdims=True)
    back_ref[...] = nt(middle_low, proj_ref[...]).astype(BF16)
    for h in range(head_cols // HEAD):
        cols = slice(h * HEAD, (h + 1) * HEAD)
        queries, key_vals, values_in = (projected_ref[j, :, cols] for j in range(3))
        out_grad = back_ref[:, cols]
        prob_vals = jnp.exp(nt(queries, key_vals) * scale - facts_ref[:, h + 8 : h + 9])
        prob_low = prob_vals.astype(BF16)
        prob_grad = nt(out_grad, values_in)
        row = jnp.sum(prob_vals * prob_grad, axis=-1, keepdims=True)
        score_low = (prob_vals * (prob_grad - row)).astype(BF16)
        low_ref[:, h * HEAD : (h + 1) * HEAD] = (nn(score_low, key_vals) * scale).astype(BF16)
        start = head_cols + h * HEAD
        low_ref[:, start : start + HEAD] = (tn(score_low, queries) * scale).astype(BF16)
        start = start + head_cols
        low_ref[:, start : start + HEAD] = tn(prob_low, out_grad).astype(BF16)
    low = low_ref[...]
    half = kept_ref.shape[0]
    mixed_middle = nt(mix_ref[1], middle_low).astype(BF16)
    small = small_ref[...].astype(BF16)
    for part in range(2):
        rows = slice(part * half, (part + 1) * half)
        pieces = (
            nn(hidden_ref[0, rows, :], low[:, : 2 * head_cols]),
            nt(mix_ref[0, rows, :], small),
            nn(hidden_ref[1, rows, :], low[:, 2 * head_cols :]),
            nn(mixed_middle[rows, :], attended_ref[...]),
        )
        first = 0
        for piece in pieces:
            last = first + piece.shape[1]
            if part == 0:
                kept_ref[:, first:last] = piece
            else:
                sent_ref[:, first:last] = piece.astype(BF16)
            first = last
    part = nt(low[:, :head_cols], weight_ref[0])
    part = part + nt(low[:, head_cols : 2 * head_cols], weight_ref[1])
    part = part + nt(low[:, 2 * head_cols :], weight_ref[2])
    hidden_part_ref[...] = part.astype(BF16)
    sums_ref[...] = jnp.sum(low.astype(F32), axis=0, keepdims=True)


def attention_grads(*operands):
    tok_count, feat_dim = operands[0].shape
    experts = operands[2].shape[1]
    head_cols = operands[10].shape[0]
    small = -(-(2 * experts + 3) // 128) * 128
    width = 4 * head_cols + small
    flops = 2 * tok_count * feat_dim * head_cols * 9 + 2 * feat_dim * feat_dim * (tok_count + small)
    return pl.pallas_call(
        attention_grads_kernel,
        out_shape=(
            jax.ShapeDtypeStruct((feat_dim // 2, width), BF16),
            jax.ShapeDtypeStruct((feat_dim // 2, width), F32),
            jax.ShapeDtypeStruct((tok_count, feat_dim), BF16),
            jax.ShapeDtypeStruct((1, 3 * head_cols), F32),
            jax.ShapeDtypeStruct((tok_count, feat_dim), F32),
        ),
        scratch_shapes=[
            pltpu.VMEM((tok_count, 3 * head_cols), BF16),
            pltpu.VMEM((tok_count, head_cols), BF16),
            pltpu.VMEM((small, feat_dim), F32),
        ],
        compiler_params=pltpu.CompilerParams(vmem_limit_bytes=60 << 20),
        cost_estimate=pl.CostEstimate(
            flops=flops, bytes_accessed=10 << 20, transcendentals=tok_count * tok_count * 6
        ),
        name="attention_grads",
    )(*operands)


def finish_kernel(head_cols, experts, orders, me_ref, mine, got, qkv_ref, proj_ref, router_ref, bias_ref, norm_ref, held_proj, held_small):
    me = me_ref[0]
    count = 1 << len(orders[0])
    feat_dim = qkv_ref.shape[1]
    chunk = feat_dim // count
    half = count // 2
    width = held_small.shape[1]
    split = 2 * head_cols + width
    for spot in range(count):
        starts = []
        for order in orders:
            name = sum(bit for i, bit in enumerate(order) if (spot >> (len(order) - 1 - i)) & 1)
            starts.append(pl.ds(pl.multiple_of((name ^ me) * chunk, chunk), chunk))
        source = mine if spot < half else got
        first = (spot % half) * chunk
        piece = source[first : first + chunk, :].astype(F32)
        qkv_ref[0, starts[0], :] = piece[:, :head_cols]
        qkv_ref[1, starts[0], :] = piece[:, head_cols : 2 * head_cols]
        held_small[starts[0], :] = piece[:, 2 * head_cols : split]
        qkv_ref[2, starts[1], :] = piece[:, split : split + head_cols]
        held_proj[starts[1], :] = piece[:, split + head_cols :]
    proj_ref[...] = held_proj[...].T
    small = held_small[...]
    router_ref[...] = small[:, :experts]
    flat = small.T
    bias_ref[...] = flat[experts : 2 * experts]
    norm_ref[...] = flat[2 * experts : 2 * experts + 8]


def finish(me, mine, came, head_cols, experts, feat_dim, orders):
    width = mine.shape[1] - 4 * head_cols
    vmem = pl.BlockSpec(memory_space=pltpu.VMEM)
    return pl.pallas_call(
        lambda *refs: finish_kernel(head_cols, experts, orders, *refs),
        in_specs=[pl.BlockSpec(memory_space=pltpu.SMEM), vmem, vmem],
        out_specs=[vmem] * 5,
        out_shape=(
            jax.ShapeDtypeStruct((3, feat_dim, head_cols), F32),
            jax.ShapeDtypeStruct((head_cols, feat_dim), F32),
            jax.ShapeDtypeStruct((feat_dim, experts), F32),
            jax.ShapeDtypeStruct((experts, feat_dim), F32),
            jax.ShapeDtypeStruct((8, feat_dim), F32),
        ),
        scratch_shapes=[
            pltpu.VMEM((feat_dim, head_cols), F32),
            pltpu.VMEM((feat_dim, width), F32),
        ],
        compiler_params=pltpu.CompilerParams(vmem_limit_bytes=60 << 20),
        name="finish",
    )(me[None], mine, came)


def high_low(values):
    high = values.astype(BF16)
    return high, (values - high.astype(F32)).astype(BF16)


def local(
    inputs,
    norm1_gain,
    norm1_bias,
    qkv_weight,
    qv_bias,
    proj_weight,
    proj_bias,
    norm2_gain,
    norm2_bias,
    router,
    expert_in,
    expert_in_bias,
    expert_out,
    expert_out_bias,
    routes,
    cotangent,
):
    tok_count = inputs.shape[0]
    feat_dim = inputs.shape[1]
    half_dim = feat_dim // 2
    head_cols = qkv_weight.shape[2]
    heads_here = head_cols // HEAD
    images = tok_count // SEQ
    experts = router.shape[1]
    sources = lax.axis_size("dp")
    group_size = sources // experts
    capacity = max(2, (10 * tok_count + 3 * experts - 1) // (3 * experts))
    slots = (capacity + 3 + 15) // 16 * 16
    score_scale = HEAD ** (-0.5)
    plane = lax.axis_index("tensor")
    me = lax.axis_index("dp")
    own_expert = me // group_size
    in_weight, out_weight = expert_in[0], expert_out[0]

    expert_ids = jnp.arange(experts, dtype=jnp.int32)
    slot_ids = jnp.arange(slots, dtype=jnp.int32)
    all_ids = jnp.arange(experts * slots, dtype=jnp.int32)
    pick = [(routes[:, k : k + 1] == expert_ids[None, :]) for k in range(2)]
    named = (pick[0] | pick[1]).astype(BF16)
    before = (
        jnp.arange(tok_count)[:, None] > jnp.arange(tok_count)[None, :]
    ).astype(BF16)
    earlier = nn(before, named)
    rank = [
        jnp.sum(jnp.where(pick[k], earlier, 0.0), axis=1, keepdims=True).astype(jnp.int32)
        for k in range(2)
    ]
    place = [routes[:, k : k + 1] * slots + rank[k] for k in range(2)]
    onehot = ((place[0] == all_ids[None, :]) | (place[1] == all_ids[None, :])).astype(BF16)
    rank_hot = [(rank[k] == slot_ids[None, :]) for k in range(2)]
    pick_low = [pick[k].astype(BF16) for k in range(2)]
    partner = [
        jnp.where(rank_hot[k], routes[:, 1 - k : 2 - k].astype(F32), 0.0).astype(BF16)
        for k in range(2)
    ]
    partner_map = tn(pick_low[0], partner[0]) + tn(pick_low[1], partner[1])

    cot_half = half_of(plane, cotangent, 0)
    cot_send = tn(onehot, cot_half).astype(BF16).reshape(experts, slots, half_dim)
    note = jnp.pad(partner_map.astype(BF16), ((0, 0), (0, half_dim - slots)))[:, None, :]
    cot_send = jnp.where(slot_ids[None, :, None] == slots - 1, note, cot_send)
    cot_send = jnp.repeat(cot_send, group_size, axis=0)
    proj_other = swap(proj_weight)
    proj_full = in_order(plane, proj_weight, proj_other, 0)

    inputs, cot_send = lax.optimization_barrier((inputs, cot_send))
    cot_mine = lax.all_to_all(cot_send, "dp", split_axis=0, concat_axis=0, tiled=True)
    cot_mine = cot_mine.reshape(-1, half_dim)
    x_in = inputs.astype(F32)
    normed1, inverse1 = norm_parts(x_in)
    hidden1 = (normed1 * norm1_gain + norm1_bias).astype(BF16)
    projected = jnp.einsum("td,jde->jte", hidden1, qkv_weight, preferred_element_type=F32)
    bias_rows = jnp.stack([qv_bias[0], jnp.zeros_like(qv_bias[0]), qv_bias[1]])
    projected = (projected + bias_rows[:, None, :]).astype(BF16)
    heads_view = projected.reshape(3, images, SEQ, heads_here, HEAD)
    queries, key_vals, values_in = (heads_view[0], heads_view[1], heads_view[2])
    scores = (
        jnp.einsum("bqhd,bkhd->bhqk", queries, key_vals, preferred_element_type=F32)
        * score_scale
    )
    row_max = jnp.max(scores, axis=-1, keepdims=True)
    exp_scores = jnp.exp(scores - row_max)
    row_total = jnp.sum(exp_scores, axis=-1, keepdims=True)
    lse = (row_max + jnp.log(row_total)).reshape(heads_here, tok_count).T
    prob_low = (exp_scores / row_total).astype(BF16)
    attended = jnp.einsum("bhqk,bkhd->bqhd", prob_low, values_in, preferred_element_type=F32)
    attended = attended.reshape(tok_count, head_cols).astype(BF16)
    attended_other, cot_mine = lax.optimization_barrier((swap(attended), cot_mine))
    attended_all = in_order(plane, attended, attended_other, 1)
    middle = x_in + nn(attended_all, proj_full) + proj_bias
    normed2, inverse2 = norm_parts(middle)
    hidden2 = (normed2 * norm2_gain + norm2_bias).astype(BF16)

    send = tn(onehot, hidden2).astype(BF16).reshape(experts, slots, feat_dim)
    send = jnp.repeat(send, group_size, axis=0)
    cot_other = swap(cot_mine)
    arrived = lax.all_to_all(send, "dp", split_axis=0, concat_axis=0, tiled=True)
    arrived = arrived.reshape(-1, feat_dim)

    logits = nn(hidden2, router)
    chosen = [jnp.sum(jnp.where(pick[k], logits, 0.0), axis=1, keepdims=True) for k in range(2)]
    chosen_max = jnp.maximum(chosen[0], chosen[1])
    chosen_exp = [jnp.exp(chosen[k] - chosen_max) for k in range(2)]
    chosen_sum = chosen_exp[0] + chosen_exp[1]
    gate_vals = [chosen_exp[k] / chosen_sum for k in range(2)]
    gate_map = jnp.where(pick[0], gate_vals[0], 0.0) + jnp.where(pick[1], gate_vals[1], 0.0)
    grad_out = cotangent.astype(F32)
    row_grad = [(gate_vals[k] * grad_out).astype(BF16) for k in range(2)]
    out_bias_grad = tn(pick_low[0], row_grad[0]) + tn(pick_low[1], row_grad[1])

    note_rows = jnp.where(plane == 0, cot_mine, cot_other).reshape(sources, slots, half_dim)
    other_expert = note_rows[:, slots - 1, :slots].reshape(-1, 1).astype(jnp.int32)
    real_slot = (jnp.arange(sources * slots, dtype=jnp.int32)[:, None] % slots) < capacity
    row_logits = nn(arrived, router)
    own_logit = jnp.sum(
        jnp.where(expert_ids[None, :] == own_expert, row_logits, 0.0), axis=1, keepdims=True
    )
    other_logit = jnp.sum(
        jnp.where(expert_ids[None, :] == other_expert, row_logits, 0.0), axis=1, keepdims=True
    )
    top_logit = jnp.maximum(own_logit, other_logit)
    own_exp = jnp.exp(own_logit - top_logit)
    row_gate = own_exp / (own_exp + jnp.exp(other_logit - top_logit))
    row_gate = jnp.where(real_slot, row_gate, 0.0)
    cot_rows = in_order(plane, cot_mine, cot_other, 1)
    grad_rows = (row_gate * cot_rows.astype(F32)).astype(BF16)

    pre_act = nn(arrived, in_weight) + expert_in_bias[0]
    activ_vals, gelu_slope = gelu_parts(pre_act)
    activ_low = activ_vals.astype(BF16)
    part_out = nn(activ_low, out_weight)
    act_grad = nt(grad_rows, out_weight) * gelu_slope
    in_bias_grad = jnp.sum(act_grad, axis=0)
    act_low = act_grad.astype(BF16)
    row_part = nt(act_low, in_weight)

    inner = jnp.sum(cot_rows.astype(F32) * part_out, axis=1).reshape(sources, slots)
    inner = inner + swap(inner)
    inner_high = inner.astype(BF16)
    inner_low = (inner - inner_high.astype(F32)).astype(BF16)

    def widen(x):
        return jnp.pad(x, ((0, 0), (0, feat_dim - slots)))[:, None, :]

    row_send = row_part.astype(BF16).reshape(sources, slots, feat_dim)
    row_send = jnp.where(slot_ids[None, :, None] == slots - 1, widen(inner_high), row_send)
    row_send = jnp.where(slot_ids[None, :, None] == slots - 2, widen(inner_low), row_send)
    row_back = lax.all_to_all(row_send, "dp", split_axis=0, concat_axis=0, tiled=True)
    out_weight_grad = tn(activ_low, grad_rows)
    in_weight_grad = tn(arrived, act_low)
    bits = [1 << i for i in range(sources.bit_length() - 1)]
    orders = [bits, bits[:1] + bits[2:] + bits[1:2]]
    chunk = feat_dim // sources

    rows = jnp.arange(feat_dim, dtype=jnp.int32)[None, :]
    cols = jnp.arange(feat_dim, dtype=jnp.int32)[:, None]
    spot = cols // chunk
    mix_t = []
    for order in orders:
        piece = jnp.zeros_like(spot)
        for i, bit in enumerate(order):
            piece = piece | jnp.where((spot >> (len(bits) - 1 - i)) & 1 == 1, bit, 0)
        mix_t.append(
            ((rows // chunk == (piece ^ me)) & (rows % chunk == cols % chunk)).astype(BF16)
        )
    mix_t = jnp.stack(mix_t)
    hidden1_t = jnp.einsum("jqd,td->jqt", mix_t, hidden1, preferred_element_type=F32).astype(BF16)
    bias_dot = lax.dot_general(
        grad_out,
        expert_out_bias,
        (((1,), (1,)), ((), ())),
        precision=lax.Precision.HIGHEST,
        preferred_element_type=F32,
    )
    facts = [routes.astype(F32)] + [r.astype(F32) for r in rank] + gate_vals + [inverse2]
    facts = jnp.concatenate(facts, axis=1)
    facts = jnp.concatenate([facts, jnp.zeros_like(facts[:, :1]), lse], axis=1)
    facts = jnp.pad(facts, ((0, 0), (0, 16 - facts.shape[1])))
    facts = jnp.pad(jnp.concatenate([facts, bias_dot], axis=1), ((0, 0), (0, 112 - experts)))
    ready = (
        out_weight_grad, in_weight_grad, in_bias_grad, mix_t, hidden1_t, facts, onehot,
        out_bias_grad, normed2, hidden2, projected, attended, router, gate_map,
    )
    row_back, ready = lax.optimization_barrier((row_back, ready))
    (
        out_weight_grad, in_weight_grad, in_bias_grad, mix_t, hidden1_t, facts, onehot,
        out_bias_grad, normed2, hidden2, projected, attended, router, gate_map,
    ) = ready

    def over_group(x):
        if group_size == 1:
            return x
        shape = (experts, group_size) + x.shape[1:]
        return jnp.sum(x.reshape(shape).astype(F32), axis=1).astype(BF16)

    row_home, logit_grad = home_rows(
        over_group(row_back),
        onehot,
        facts,
    )
    part_out, row_home = lax.optimization_barrier((part_out, row_home))
    out_send = (row_gate * part_out).astype(BF16).reshape(sources, slots, feat_dim)
    row_other = swap(row_home)
    out_back = lax.all_to_all(out_send, "dp", split_axis=0, concat_axis=0, tiled=True)

    sent, kept, hidden1_part, qv_sums, middle_grad = attention_grads(
        row_home,
        row_other,
        logit_grad,
        router,
        cotangent,
        normed2,
        facts,
        norm2_gain[None],
        hidden2,
        out_bias_grad,
        proj_weight,
        projected,
        attended,
        hidden1_t,
        qkv_weight,
        mix_t,
    )
    hidden1_grad = hidden1_part.astype(F32) + swap(hidden1_part).astype(F32)
    norm1_gain_grad = jnp.sum(hidden1_grad * normed1, axis=0)
    norm1_bias_grad = jnp.sum(hidden1_grad, axis=0)
    input_grad = middle_grad + norm_back(hidden1_grad * norm1_gain, normed1, inverse1)

    split = sent.shape[1] - 2 * head_cols
    sent, out_back = lax.optimization_barrier((sent, out_back))
    came = across(sent, bits[0], sources)
    total = kept + came.astype(F32)
    totals = [total[:, :split], total[:, split:]]
    out_home = nn(onehot, over_group(out_back).reshape(-1, feat_dim)).astype(BF16)
    for turn in range(1, len(bits)):
        totals, out_home = lax.optimization_barrier((totals, out_home))
        if turn == 2:
            out_other = swap(out_home)
        cames = [send_half(t, order[turn], sources) for t, order in zip(totals, orders)]
        totals = [keep_half(t, c) for t, c in zip(totals, cames)]
    totals, out_other = lax.optimization_barrier((totals, out_other))
    out_home = out_home.astype(F32) + out_other.astype(F32)
    output = (middle + (out_home + exact(gate_map, expert_out_bias))).astype(BF16)
    mine = [t.astype(BF16) for t in totals]
    late = jnp.stack(
        [
            norm1_gain_grad,
            norm1_bias_grad,
            jnp.concatenate([qv_sums[0, :head_cols], qv_sums[0, 2 * head_cols :]]),
        ]
    )
    late = jnp.pad(late, ((0, 5), (0, 0)))

    def late_rows(late):
        high, low = high_low(late)
        both = jnp.pad(jnp.concatenate([high, low], axis=0), ((0, 0), (0, split - feat_dim)))
        return high.astype(F32) + low.astype(F32), both

    def late_sum(own, came):
        came = came[:, :feat_dim].astype(F32)
        return own + (came[:8] + came[8:])

    size = chunk
    for turn in range(len(bits) - 1, 0, -1):
        own, both = late_rows(late)
        first, second = lax.optimization_barrier(
            (jnp.concatenate([mine[0], both], axis=0), mine[1])
        )
        came = across(first, orders[0][turn], sources)
        came_b = across(second, orders[1][turn], sources)
        late = late_sum(own, came[size:])
        mine = [
            jnp.concatenate([mine[0], came[:size]], axis=0),
            jnp.concatenate([mine[1], came_b], axis=0),
        ]
        size = 2 * size
    own, both = late_rows(late)
    mine = jnp.concatenate(mine, axis=1)
    both = jnp.pad(both, ((0, 0), (0, 2 * head_cols)))
    came = across(jnp.concatenate([mine, both], axis=0), bits[0], sources)
    late = late_sum(own, came[size:])
    qv_bias_grad = late[2].reshape(2, head_cols)
    if chunk % 16 == 0:
        qkv_grad, proj_grad, router_grad, out_bias_grad, norm_grads = finish(
            me, mine, came, head_cols, experts, feat_dim, orders
        )
    else:
        whole = jnp.concatenate([mine, came[:size]], axis=0)
        first, second = tn(mix_t[0], whole[:, :split]), tn(mix_t[1], whole[:, split:])
        qkv_grad = jnp.stack(
            [first[:, :head_cols], first[:, head_cols : 2 * head_cols], second[:, :head_cols]]
        )
        proj_grad = second[:, head_cols:].T
        router_grad = first[:, 2 * head_cols : 2 * head_cols + experts]
        norm_grads = first[:, 2 * head_cols + experts :].T
        out_bias_grad, norm_grads = norm_grads[:experts], norm_grads[experts:]
    norm2_gain_grad, norm2_bias_grad, proj_bias_grad = norm_grads[0], norm_grads[1], norm_grads[2]
    return (
        output,
        input_grad,
        late[0],
        late[1],
        qkv_grad,
        qv_bias_grad,
        proj_grad,
        proj_bias_grad,
        norm2_gain_grad,
        norm2_bias_grad,
        router_grad,
        in_weight_grad[None],
        in_bias_grad[None],
        out_weight_grad[None],
        out_bias_grad,
    )


def solution(mesh):
    return jax.shard_map(
        local,
        mesh=mesh,
        in_specs=(
            P("dp", None),
            P(),
            P(),
            P(None, None, "tensor"),
            P(None, "tensor"),
            P("tensor", None),
            P(),
            P(),
            P(),
            P(),
            P("dp", None, "tensor"),
            P("dp", "tensor"),
            P("dp", "tensor", None),
            P(),
            P("dp", None),
            P("dp", None),
        ),
        out_specs=(
            P("dp", None),
            P("dp", None),
            P(),
            P(),
            P(None, None, "tensor"),
            P(None, "tensor"),
            P("tensor", None),
            P(),
            P(),
            P(),
            P(),
            P("dp", None, "tensor"),
            P("dp", "tensor"),
            P("dp", "tensor", None),
            P(),
        ),
        check_vma=False,
    )
```

```python
import jax
import jax.numpy as jnp
from jax import lax
from jax.experimental import pallas as pl
from jax.experimental.pallas import tpu as pltpu
from jax.sharding import PartitionSpec as P

HEAD = 64
SEQ = 197
F32 = jnp.float32
BF16 = jnp.bfloat16

epsilon = 1e-06


def norm_parts(values):
    average = jnp.mean(values, axis=-1, keepdims=True)
    centred = values - average
    inverse = lax.rsqrt(jnp.mean(centred * centred, axis=-1, keepdims=True) + epsilon)
    return (centred * inverse, inverse)


def norm_back(inner_grad, normed, inverse):
    first_mean = jnp.mean(inner_grad, axis=-1, keepdims=True)
    second_mean = jnp.mean(inner_grad * normed, axis=-1, keepdims=True)
    return inverse * (inner_grad - first_mean - normed * second_mean)


def gelu_parts(pre_act):
    normal_cdf = 0.5 * (1.0 + lax.erf(pre_act * 0.7071067811865476))
    density = jnp.exp(-0.5 * pre_act * pre_act) * 0.3989422804014327
    return (pre_act * normal_cdf, normal_cdf + pre_act * density)


def dot(a, b, dims, out=F32):
    return lax.dot_general(a, b, (dims, ((), ())), preferred_element_type=out)


def nn(a, b):
    return dot(a, b, ((1,), (0,)))


def nt(a, b):
    return dot(a, b, ((1,), (1,)))


def tn(a, b):
    return dot(a, b, ((0,), (0,)))


def exact(a, b):
    return lax.dot_general(
        a,
        b,
        (((1,), (0,)), ((), ())),
        precision=lax.Precision.HIGHEST,
        preferred_element_type=F32,
    )


def swap(x):
    return lax.ppermute(x, "tensor", [(0, 1), (1, 0)])


def across(x, bit, count):
    return lax.ppermute(x, "dp", [(i, i ^ bit) for i in range(count)])


def in_order(plane, mine, other, axis):
    first = jnp.where(plane == 0, mine, other)
    second = jnp.where(plane == 0, other, mine)
    return jnp.concatenate([first, second], axis=axis)


def half_of(plane, x, which):
    width = x.shape[-1] // 2
    low, high = x[..., :width], x[..., width:]
    return jnp.where((plane == which), low, high)


def keep_half(total, came):
    middle = total.shape[0] // 2
    return total[:middle] + came.astype(F32)


def send_half(total, bit, count):
    return across(total[total.shape[0] // 2 :].astype(BF16), bit, count)


def expert_kernel(
    capacity, slots, own_ref, arrived_ref, cot_ref, other_ref, router_ref, in_ref, bias_ref, out_ref,
    activ_ref, slope_ref, grad_rows_ref, row_ref, out_rows_ref, bias_grad_ref, gate_ref, row_sum, out_sum,
):
    step = pl.program_id(0)
    count = arrived_ref.shape[0]
    experts = router_ref.shape[1]

    @pl.when(step == 0)
    def _():
        logits = nn(arrived_ref[...], router_ref[...])
        ids = lax.broadcasted_iota(jnp.int32, (count, experts), 1)
        own = jnp.sum(jnp.where(ids == own_ref[0], logits, 0.0), axis=1, keepdims=True)
        other = jnp.sum(jnp.where(ids.astype(F32) == other_ref[...], logits, 0.0), axis=1, keepdims=True)
        top = jnp.maximum(own, other)
        own, other = jnp.exp(own - top), jnp.exp(other - top)
        spot = lax.broadcasted_iota(jnp.int32, (count, 1), 0) % slots
        gate = jnp.where(spot < capacity, own / (own + other), 0.0)
        gate_ref[...] = jnp.broadcast_to(gate, gate_ref.shape)
        grad_rows_ref[...] = (gate * cot_ref[...].astype(F32)).astype(BF16)
        row_sum[...] = jnp.zeros_like(row_sum)
        out_sum[...] = jnp.zeros_like(out_sum)

    pre_act = nn(arrived_ref[...], in_ref[...]) + bias_ref[...]
    activ, slope = gelu_parts(pre_act)
    activ = activ.astype(BF16)
    activ_ref[...] = activ
    grad = nt(grad_rows_ref[...], out_ref[...]) * slope
    bias_grad_ref[...] = jnp.sum(grad, axis=0, keepdims=True)
    grad = grad.astype(BF16)
    slope_ref[...] = grad
    row_sum[...] += nt(grad, in_ref[...])
    out_sum[...] += nn(activ, out_ref[...])

    @pl.when(step == pl.num_programs(0) - 1)
    def _():
        inner = jnp.sum(cot_ref[...].astype(F32) * out_sum[...], axis=1, keepdims=True)
        inner = jnp.broadcast_to(inner, gate_ref.shape).T
        out_rows_ref[...] = (gate_ref[:, :1] * out_sum[...]).astype(BF16)
        spot = lax.broadcasted_iota(jnp.int32, (slots, 128), 0)
        row_ref[...] = row_sum[...].astype(BF16)
        for source in range(count // slots):
            first = source * slots
            line = inner[:1, first : first + slots]
            line = jnp.concatenate([line, jnp.zeros((1, 128 - slots), F32)], axis=1)
            high = line.astype(BF16).astype(F32)
            tail = row_sum[first + slots - 16 : first + slots, :128]
            place = lax.broadcasted_iota(jnp.int32, tail.shape, 0)
            tail = jnp.where(place == 15, high, jnp.where(place == 14, line - high, tail))
            row_ref[first + slots - 16 : first + slots, :128] = tail.astype(BF16)


def expert_rows(own, arrived, cot_rows, other, router, in_weight, in_bias, out_weight, capacity, slots):
    count, feat_dim = arrived.shape
    hidden = in_weight.shape[1]
    block = 512 if hidden % 512 == 0 else hidden
    whole = lambda shape: pl.BlockSpec(shape, lambda i: (0, 0))
    return pl.pallas_call(
        lambda *refs: expert_kernel(capacity, slots, *refs),
        grid=(hidden // block,),
        in_specs=[
            pl.BlockSpec(memory_space=pltpu.SMEM),
            whole((count, feat_dim)),
            whole((count, feat_dim)),
            whole((count, 1)),
            whole(router.shape),
            pl.BlockSpec((feat_dim, block), lambda i: (0, i)),
            pl.BlockSpec((1, block), lambda i: (0, i)),
            pl.BlockSpec((block, feat_dim), lambda i: (i, 0)),
        ],
        out_specs=[
            pl.BlockSpec((count, block), lambda i: (0, i)),
            pl.BlockSpec((count, block), lambda i: (0, i)),
            whole((count, feat_dim)),
            whole((count, feat_dim)),
            whole((count, feat_dim)),
            pl.BlockSpec((1, block), lambda i: (0, i)),
        ],
        out_shape=(
            jax.ShapeDtypeStruct((count, hidden), BF16),
            jax.ShapeDtypeStruct((count, hidden), BF16),
            jax.ShapeDtypeStruct((count, feat_dim), BF16),
            jax.ShapeDtypeStruct((count, feat_dim), BF16),
            jax.ShapeDtypeStruct((count, feat_dim), BF16),
            jax.ShapeDtypeStruct((1, hidden), F32),
        ),
        scratch_shapes=[
            pltpu.VMEM((count, 128), F32),
            pltpu.VMEM((count, feat_dim), F32),
            pltpu.VMEM((count, feat_dim), F32),
        ],
        compiler_params=pltpu.CompilerParams(vmem_limit_bytes=60 << 20),
        cost_estimate=pl.CostEstimate(
            flops=8 * count * feat_dim * hidden, bytes_accessed=12 << 20, transcendentals=2 * count * hidden
        ),
        name="expert_rows",
    )(own[None], arrived, cot_rows, other, router, in_weight, in_bias, out_weight)


def expert_rows_plain(own, arrived, cot_rows, other, router, in_weight, in_bias, out_weight, capacity, slots):
    count, feat_dim = arrived.shape
    logits = nn(arrived, router)
    ids = jnp.arange(router.shape[1], dtype=jnp.int32)[None, :]
    own = jnp.sum(jnp.where(ids == own, logits, 0.0), axis=1, keepdims=True)
    other = jnp.sum(jnp.where(ids.astype(F32) == other, logits, 0.0), axis=1, keepdims=True)
    top = jnp.maximum(own, other)
    own, other = jnp.exp(own - top), jnp.exp(other - top)
    spot = jnp.arange(count, dtype=jnp.int32)[:, None] % slots
    gate = jnp.where(spot < capacity, own / (own + other), 0.0)
    grad_rows = (gate * cot_rows.astype(F32)).astype(BF16)
    activ, slope = gelu_parts(nn(arrived, in_weight) + in_bias)
    activ = activ.astype(BF16)
    grad = nt(grad_rows, out_weight) * slope
    bias_grad = jnp.sum(grad, axis=0, keepdims=True)
    grad = grad.astype(BF16)
    part_out = nn(activ, out_weight)
    inner = jnp.sum(cot_rows.astype(F32) * part_out, axis=1).reshape(-1, slots)
    high, low = high_low(jnp.pad(inner, ((0, 0), (0, feat_dim - slots)))[:, None, :])
    rows = nt(grad, in_weight).astype(BF16).reshape(-1, slots, feat_dim)
    rows = jnp.concatenate([rows[:, : slots - 2], low, high], axis=1).reshape(count, feat_dim)
    return activ, grad, grad_rows, rows, (gate * part_out).astype(BF16), bias_grad


def home_kernel(back_ref, onehot_ref, facts_ref, home_ref, inner_ref):
    experts, slots, feat_dim = back_ref.shape
    tok_count = facts_ref.shape[0]
    home = nn(onehot_ref[...], back_ref[...].reshape(experts * slots, feat_dim))
    home_ref[:tok_count, :] = home.astype(BF16)
    for e in range(experts):
        inner_ref[0, e : e + 1, :] = back_ref[e, slots - 1 : slots, :slots].astype(F32)
        inner_ref[1, e : e + 1, :] = back_ref[e, slots - 2 : slots - 1, :slots].astype(F32)
    expert_ids = lax.broadcasted_iota(jnp.int32, (tok_count, experts), 1).astype(F32)
    slot_ids = lax.broadcasted_iota(jnp.int32, (tok_count, slots), 1).astype(F32)
    lanes = lax.broadcasted_iota(jnp.int32, (tok_count, 128), 1)
    table = jnp.zeros((tok_count, 128), F32)
    for k in range(2):
        hot = jnp.where(facts_ref[:, k : k + 1] == expert_ids, 1.0, 0.0).astype(BF16)
        found = nn(hot, inner_ref[0].astype(BF16)) + nn(hot, inner_ref[1].astype(BF16))
        found = jnp.where(facts_ref[:, k + 2 : k + 3] == slot_ids, found, 0.0)
        found = jnp.sum(found, axis=1, keepdims=True)
        high = found.astype(BF16).astype(F32)
        table = jnp.where(lanes == 2 * k, high, jnp.where(lanes == 2 * k + 1, found - high, table))
    home_ref[tok_count + 3 : tok_count + 11, :tok_count] = table.T[:8, :].astype(BF16)


def home_rows(back, onehot, facts):
    experts, slots, feat_dim = back.shape
    tok_count = facts.shape[0]
    return pl.pallas_call(
        home_kernel,
        out_shape=jax.ShapeDtypeStruct((tok_count + 11, feat_dim), BF16),
        scratch_shapes=[pltpu.VMEM((2, experts, slots), F32)],
        compiler_params=pltpu.CompilerParams(vmem_limit_bytes=16 << 20),
        cost_estimate=pl.CostEstimate(
            flops=2 * tok_count * feat_dim * experts * slots, bytes_accessed=2 << 20, transcendentals=0
        ),
        name="home_rows",
    )(back, onehot, facts)


def attention_grads_kernel(
    home_ref, other_ref, router_ref, cot_ref, normed_ref, facts_ref, gain_ref, hidden2_ref, bias_grad_ref,
    proj_ref, projected_ref, attended_ref, hidden_ref, weight_ref, mix_ref,
    sent_ref, kept_ref, hidden_part_ref, sums_ref, middle_grad_ref, low_ref, back_ref, small_ref, logit_ref,
):
    head_cols = attended_ref.shape[1]
    experts = router_ref.shape[1]
    tok_count = cot_ref.shape[0]
    scale = HEAD ** (-0.5)
    lines = slice(tok_count + 3, tok_count + 11)
    inner = home_ref[lines, :tok_count].astype(F32) + other_ref[lines, :tok_count].astype(F32)
    inner = inner.T
    bias_dot = facts_ref[:, 16 : 16 + experts]
    expert_ids = lax.broadcasted_iota(jnp.int32, (tok_count, experts), 1).astype(F32)
    picks = [facts_ref[:, k : k + 1] == expert_ids for k in range(2)]
    gates = [facts_ref[:, k + 4 : k + 5] for k in range(2)]
    inner_grads = []
    for k in range(2):
        own_bias = jnp.sum(jnp.where(picks[k], bias_dot, 0.0), axis=1, keepdims=True)
        inner_grads.append(inner[:, 2 * k : 2 * k + 1] + inner[:, 2 * k + 1 : 2 * k + 2] + own_bias)
    mean = gates[0] * inner_grads[0] + gates[1] * inner_grads[1]
    logit_grad = 0.0
    for k in range(2):
        logit_grad = logit_grad + jnp.where(picks[k], gates[k] * (inner_grads[k] - mean), 0.0)
    logit_ref[...] = logit_grad.astype(BF16)
    hidden_grad = home_ref[:tok_count, :].astype(F32) + other_ref[:tok_count, :].astype(F32)
    hidden_grad = hidden_grad + nt(logit_ref[...], router_ref[...])
    normed = normed_ref[...]
    inner = hidden_grad * gain_ref[...]
    middle_grad = cot_ref[...].astype(F32) + norm_back(inner, normed, facts_ref[:, 6:7])
    middle_grad_ref[...] = middle_grad
    middle_low = middle_grad.astype(BF16)
    small_ref[...] = jnp.zeros_like(small_ref)
    small_ref[:experts, :] = tn(logit_ref[...], hidden2_ref[...])
    small_ref[experts : 2 * experts, :] = bias_grad_ref[...]
    small_ref[2 * experts : 2 * experts + 1, :] = jnp.sum(hidden_grad * normed, axis=0, keepdims=True)
    small_ref[2 * experts + 1 : 2 * experts + 2, :] = jnp.sum(hidden_grad, axis=0, keepdims=True)
    small_ref[2 * experts + 2 : 2 * experts + 3, :] = jnp.sum(middle_grad, axis=0, keepdims=True)
    back_ref[...] = nt(middle_low, proj_ref[...]).astype(BF16)
    for h in range(head_cols // HEAD):
        cols = slice(h * HEAD, (h + 1) * HEAD)
        queries, key_vals, values_in = (projected_ref[j, :, cols] for j in range(3))
        out_grad = back_ref[:, cols]
        prob_vals = jnp.exp(nt(queries, key_vals) * scale - facts_ref[:, h + 8 : h + 9])
        prob_low = prob_vals.astype(BF16)
        prob_grad = nt(out_grad, values_in)
        row = jnp.sum(prob_vals * prob_grad, axis=-1, keepdims=True)
        score_low = (prob_vals * (prob_grad - row)).astype(BF16)
        low_ref[:, h * HEAD : (h + 1) * HEAD] = (nn(score_low, key_vals) * scale).astype(BF16)
        start = head_cols + h * HEAD
        low_ref[:, start : start + HEAD] = (tn(score_low, queries) * scale).astype(BF16)
        start = start + head_cols
        low_ref[:, start : start + HEAD] = tn(prob_low, out_grad).astype(BF16)
    low = low_ref[...]
    half = kept_ref.shape[0]
    mixed_middle = nt(mix_ref[1], middle_low).astype(BF16)
    small = small_ref[...].astype(BF16)
    for part in range(2):
        rows = slice(part * half, (part + 1) * half)
        pieces = (
            nn(hidden_ref[0, rows, :], low[:, : 2 * head_cols]),
            nt(mix_ref[0, rows, :], small),
            nn(hidden_ref[1, rows, :], low[:, 2 * head_cols :]),
            nn(mixed_middle[rows, :], attended_ref[...]),
        )
        first = 0
        for piece in pieces:
            last = first + piece.shape[1]
            if part == 0:
                kept_ref[:, first:last] = piece
            else:
                sent_ref[:, first:last] = piece.astype(BF16)
            first = last
    part = nt(low[:, :head_cols], weight_ref[0])
    part = part + nt(low[:, head_cols : 2 * head_cols], weight_ref[1])
    part = part + nt(low[:, 2 * head_cols :], weight_ref[2])
    hidden_part_ref[...] = part.astype(BF16)
    sums_ref[...] = jnp.sum(low.astype(F32), axis=0, keepdims=True)


def attention_grads(*operands):
    tok_count, feat_dim = operands[3].shape
    experts = operands[2].shape[1]
    head_cols = operands[9].shape[0]
    small = -(-(2 * experts + 3) // 128) * 128
    width = 4 * head_cols + small
    flops = 2 * tok_count * feat_dim * head_cols * 9 + 2 * feat_dim * feat_dim * (tok_count + small)
    return pl.pallas_call(
        attention_grads_kernel,
        out_shape=(
            jax.ShapeDtypeStruct((feat_dim // 2, width), BF16),
            jax.ShapeDtypeStruct((feat_dim // 2, width), F32),
            jax.ShapeDtypeStruct((tok_count, feat_dim), BF16),
            jax.ShapeDtypeStruct((1, 3 * head_cols), F32),
            jax.ShapeDtypeStruct((tok_count, feat_dim), F32),
        ),
        scratch_shapes=[
            pltpu.VMEM((tok_count, 3 * head_cols), BF16),
            pltpu.VMEM((tok_count, head_cols), BF16),
            pltpu.VMEM((small, feat_dim), F32),
            pltpu.VMEM((tok_count, experts), BF16),
        ],
        compiler_params=pltpu.CompilerParams(vmem_limit_bytes=60 << 20),
        cost_estimate=pl.CostEstimate(
            flops=flops, bytes_accessed=10 << 20, transcendentals=tok_count * tok_count * 6
        ),
        name="attention_grads",
    )(*operands)


def finish_kernel(head_cols, experts, orders, me_ref, mine, mine_b, got, got_b, qkv_ref, proj_ref, router_ref, bias_ref, norm_ref, held_proj, held_small):
    me = me_ref[0]
    count = 1 << len(orders[0])
    feat_dim = qkv_ref.shape[1]
    chunk = feat_dim // count
    half = count // 2
    for spot in range(count):
        starts = []
        for order in orders:
            name = sum(bit for i, bit in enumerate(order) if (spot >> (len(order) - 1 - i)) & 1)
            starts.append(pl.ds(pl.multiple_of((name ^ me) * chunk, chunk), chunk))
        source, source_b = (mine, mine_b) if spot < half else (got, got_b)
        first = (spot % half) * chunk
        piece = source[first : first + chunk, :].astype(F32)
        qkv_ref[0, starts[0], :] = piece[:, :head_cols]
        qkv_ref[1, starts[0], :] = piece[:, head_cols : 2 * head_cols]
        held_small[starts[0], :] = piece[:, 2 * head_cols :]
        piece = source_b[first : first + chunk, :].astype(F32)
        qkv_ref[2, starts[1], :] = piece[:, :head_cols]
        held_proj[starts[1], :] = piece[:, head_cols:]
    proj_ref[...] = held_proj[...].T
    small = held_small[...]
    flat = small.T
    router_ref[...] = flat[:experts]
    bias_ref[...] = flat[experts : 2 * experts]
    norm_ref[...] = flat[2 * experts : 2 * experts + 8]


def finish(me, mine, mine_b, came, came_b, head_cols, experts, feat_dim, orders):
    width = mine.shape[1] - 2 * head_cols
    vmem = pl.BlockSpec(memory_space=pltpu.VMEM)
    return pl.pallas_call(
        lambda *refs: finish_kernel(head_cols, experts, orders, *refs),
        in_specs=[pl.BlockSpec(memory_space=pltpu.SMEM)] + [vmem] * 4,
        out_specs=[vmem] * 5,
        out_shape=(
            jax.ShapeDtypeStruct((3, feat_dim, head_cols), F32),
            jax.ShapeDtypeStruct((head_cols, feat_dim), F32),
            jax.ShapeDtypeStruct((experts, feat_dim), F32),
            jax.ShapeDtypeStruct((experts, feat_dim), F32),
            jax.ShapeDtypeStruct((8, feat_dim), F32),
        ),
        scratch_shapes=[
            pltpu.VMEM((feat_dim, head_cols), F32),
            pltpu.VMEM((feat_dim, width), F32),
        ],
        compiler_params=pltpu.CompilerParams(vmem_limit_bytes=40 << 20),
        name="finish",
    )(me[None], mine, mine_b, came, came_b)


def high_low(values):
    high = values.astype(BF16)
    return high, (values - high.astype(F32)).astype(BF16)


def local(
    inputs,
    norm1_gain,
    norm1_bias,
    qkv_weight,
    qv_bias,
    proj_weight,
    proj_bias,
    norm2_gain,
    norm2_bias,
    router,
    expert_in,
    expert_in_bias,
    expert_out,
    expert_out_bias,
    routes,
    cotangent,
):
    tok_count = inputs.shape[0]
    feat_dim = inputs.shape[1]
    half_dim = feat_dim // 2
    head_cols = qkv_weight.shape[2]
    heads_here = head_cols // HEAD
    images = tok_count // SEQ
    experts = router.shape[1]
    sources = lax.axis_size("dp")
    group_size = sources // experts
    capacity = max(2, (10 * tok_count + 3 * experts - 1) // (3 * experts))
    slots = (capacity + 3 + 15) // 16 * 16
    score_scale = HEAD ** (-0.5)
    plane = lax.axis_index("tensor")
    me = lax.axis_index("dp")
    own_expert = me // group_size
    in_weight, out_weight = expert_in[0], expert_out[0]

    expert_ids = jnp.arange(experts, dtype=jnp.int32)
    slot_ids = jnp.arange(slots, dtype=jnp.int32)
    all_ids = jnp.arange(experts * slots, dtype=jnp.int32)
    pick = [(routes[:, k : k + 1] == expert_ids[None, :]) for k in range(2)]
    named = (pick[0] | pick[1]).astype(BF16)
    before = (
        jnp.arange(tok_count)[:, None] > jnp.arange(tok_count)[None, :]
    ).astype(BF16)
    earlier = nn(before, named)
    rank = [
        jnp.sum(jnp.where(pick[k], earlier, 0.0), axis=1, keepdims=True).astype(jnp.int32)
        for k in range(2)
    ]
    place = [routes[:, k : k + 1] * slots + rank[k] for k in range(2)]
    onehot = ((place[0] == all_ids[None, :]) | (place[1] == all_ids[None, :])).astype(BF16)
    rank_hot = [(rank[k] == slot_ids[None, :]) for k in range(2)]
    pick_low = [pick[k].astype(BF16) for k in range(2)]
    partner = [
        jnp.where(rank_hot[k], routes[:, 1 - k : 2 - k].astype(F32), 0.0).astype(BF16)
        for k in range(2)
    ]
    partner_map = tn(pick_low[0], partner[0]) + tn(pick_low[1], partner[1])

    cot_half = half_of(plane, cotangent, 0)
    cot_send = tn(onehot, cot_half).astype(BF16).reshape(experts, slots, half_dim)
    note = jnp.pad(partner_map.astype(BF16), ((0, 0), (0, half_dim - slots)))[:, None, :]
    cot_send = jnp.where(slot_ids[None, :, None] == slots - 1, note, cot_send)
    cot_send = jnp.repeat(cot_send, group_size, axis=0)
    proj_other = swap(proj_weight)
    proj_full = in_order(plane, proj_weight, proj_other, 0)

    inputs, cot_send = lax.optimization_barrier((inputs, cot_send))
    cot_mine = lax.all_to_all(cot_send, "dp", split_axis=0, concat_axis=0, tiled=True)
    cot_mine = cot_mine.reshape(-1, half_dim)
    x_in = inputs.astype(F32)
    normed1, inverse1 = norm_parts(x_in)
    hidden1 = (normed1 * norm1_gain + norm1_bias).astype(BF16)
    projected = jnp.einsum("td,jde->jte", hidden1, qkv_weight, preferred_element_type=F32)
    bias_rows = jnp.stack([qv_bias[0], jnp.zeros_like(qv_bias[0]), qv_bias[1]])
    projected = (projected + bias_rows[:, None, :]).astype(BF16)
    heads_view = projected.reshape(3, images, SEQ, heads_here, HEAD)
    queries, key_vals, values_in = (heads_view[0], heads_view[1], heads_view[2])
    scores = (
        jnp.einsum("bqhd,bkhd->bhqk", queries, key_vals, preferred_element_type=F32)
        * score_scale
    )
    row_max = jnp.max(scores, axis=-1, keepdims=True)
    exp_scores = jnp.exp(scores - row_max)
    row_total = jnp.sum(exp_scores, axis=-1, keepdims=True)
    lse = (row_max + jnp.log(row_total)).reshape(heads_here, tok_count).T
    prob_low = (exp_scores / row_total).astype(BF16)
    attended = jnp.einsum("bhqk,bkhd->bqhd", prob_low, values_in, preferred_element_type=F32)
    attended = attended.reshape(tok_count, head_cols).astype(BF16)
    attended_other, cot_mine = lax.optimization_barrier((swap(attended), cot_mine))
    attended_all = in_order(plane, attended, attended_other, 1)
    middle = x_in + nn(attended_all, proj_full) + proj_bias
    normed2, inverse2 = norm_parts(middle)
    hidden2 = (normed2 * norm2_gain + norm2_bias).astype(BF16)

    send = tn(onehot, hidden2).astype(BF16).reshape(experts, slots, feat_dim)
    send = jnp.repeat(send, group_size, axis=0)
    cot_other = swap(cot_mine)
    arrived = lax.all_to_all(send, "dp", split_axis=0, concat_axis=0, tiled=True)
    arrived = arrived.reshape(-1, feat_dim)

    logits = nn(hidden2, router)
    chosen = [jnp.sum(jnp.where(pick[k], logits, 0.0), axis=1, keepdims=True) for k in range(2)]
    chosen_max = jnp.maximum(chosen[0], chosen[1])
    chosen_exp = [jnp.exp(chosen[k] - chosen_max) for k in range(2)]
    chosen_sum = chosen_exp[0] + chosen_exp[1]
    gate_vals = [chosen_exp[k] / chosen_sum for k in range(2)]
    gate_map = jnp.where(pick[0], gate_vals[0], 0.0) + jnp.where(pick[1], gate_vals[1], 0.0)
    grad_out = cotangent.astype(F32)
    row_grad = [(gate_vals[k] * grad_out).astype(BF16) for k in range(2)]
    out_bias_grad = tn(pick_low[0], row_grad[0]) + tn(pick_low[1], row_grad[1])

    note_rows = jnp.where(plane == 0, cot_mine, cot_other).reshape(sources, slots, half_dim)
    other_expert = note_rows[:, slots - 1, :slots].reshape(-1, 1).astype(F32)
    cot_rows = in_order(plane, cot_mine, cot_other, 1)
    activ_low, act_low, grad_rows, row_send, out_send, in_bias_grad = (
        expert_rows if sources * slots <= 1024 else expert_rows_plain
    )(
        own_expert, arrived, cot_rows, other_expert, router, in_weight, expert_in_bias, out_weight, capacity, slots
    )
    row_send = row_send.reshape(sources, slots, feat_dim)
    row_back = lax.all_to_all(row_send, "dp", split_axis=0, concat_axis=0, tiled=True)
    out_weight_grad = tn(activ_low, grad_rows)
    in_weight_grad = tn(arrived, act_low)
    bits = [1 << i for i in range(sources.bit_length() - 1)]
    orders = [bits, bits[:1] + bits[2:] + bits[1:2]]
    chunk = feat_dim // sources

    rows = jnp.arange(feat_dim, dtype=jnp.int32)[None, :]
    cols = jnp.arange(feat_dim, dtype=jnp.int32)[:, None]
    spot = cols // chunk
    mix_t = []
    for order in orders:
        piece = jnp.zeros_like(spot)
        for i, bit in enumerate(order):
            piece = piece | jnp.where((spot >> (len(bits) - 1 - i)) & 1 == 1, bit, 0)
        mix_t.append(
            ((rows // chunk == (piece ^ me)) & (rows % chunk == cols % chunk)).astype(BF16)
        )
    mix_t = jnp.stack(mix_t)
    hidden1_t = jnp.einsum("jqd,td->jqt", mix_t, hidden1, preferred_element_type=F32).astype(BF16)
    bias_dot = lax.dot_general(
        grad_out,
        expert_out_bias,
        (((1,), (1,)), ((), ())),
        precision=lax.Precision.HIGHEST,
        preferred_element_type=F32,
    )
    facts = [routes.astype(F32)] + [r.astype(F32) for r in rank] + gate_vals + [inverse2]
    facts = jnp.concatenate(facts, axis=1)
    facts = jnp.concatenate([facts, jnp.zeros_like(facts[:, :1]), lse], axis=1)
    facts = jnp.pad(facts, ((0, 0), (0, 16 - facts.shape[1])))
    facts = jnp.pad(jnp.concatenate([facts, bias_dot], axis=1), ((0, 0), (0, 112 - experts)))
    ready = (
        out_weight_grad, in_weight_grad, in_bias_grad, mix_t, hidden1_t, facts, onehot,
        out_bias_grad, normed2, hidden2, projected, attended, router, gate_map,
    )
    row_back, ready = lax.optimization_barrier((row_back, ready))
    (
        out_weight_grad, in_weight_grad, in_bias_grad, mix_t, hidden1_t, facts, onehot,
        out_bias_grad, normed2, hidden2, projected, attended, router, gate_map,
    ) = ready

    def over_group(x):
        if group_size == 1:
            return x
        shape = (experts, group_size) + x.shape[1:]
        return jnp.sum(x.reshape(shape).astype(F32), axis=1).astype(BF16)

    row_home = home_rows(
        over_group(row_back),
        onehot,
        facts,
    )
    out_send, row_home = lax.optimization_barrier((out_send, row_home))
    out_send = out_send.reshape(sources, slots, feat_dim)
    row_other = swap(row_home)
    out_back = lax.all_to_all(out_send, "dp", split_axis=0, concat_axis=0, tiled=True)

    sent, kept, hidden1_part, qv_sums, middle_grad = attention_grads(
        row_home,
        row_other,
        router,
        cotangent,
        normed2,
        facts,
        norm2_gain[None],
        hidden2,
        out_bias_grad,
        proj_weight,
        projected,
        attended,
        hidden1_t,
        qkv_weight,
        mix_t,
    )
    hidden1_grad = hidden1_part.astype(F32) + swap(hidden1_part).astype(F32)
    norm1_gain_grad = jnp.sum(hidden1_grad * normed1, axis=0)
    norm1_bias_grad = jnp.sum(hidden1_grad, axis=0)
    input_grad = middle_grad + norm_back(hidden1_grad * norm1_gain, normed1, inverse1)

    split = sent.shape[1] - 2 * head_cols
    sent, out_back = lax.optimization_barrier((sent, out_back))
    came = across(sent, bits[0], sources)
    total = kept + came.astype(F32)
    totals = [total[:, :split], total[:, split:]]
    out_home = nn(onehot, over_group(out_back).reshape(-1, feat_dim)).astype(BF16)
    for turn in range(1, len(bits)):
        totals, out_home = lax.optimization_barrier((totals, out_home))
        if turn == 2:
            out_other = swap(out_home)
        cames = [send_half(t, order[turn], sources) for t, order in zip(totals, orders)]
        totals = [keep_half(t, c) for t, c in zip(totals, cames)]
    totals, out_other = lax.optimization_barrier((totals, out_other))
    out_home = out_home.astype(F32) + out_other.astype(F32)
    output = (middle + (out_home + exact(gate_map, expert_out_bias))).astype(BF16)
    mine = [t.astype(BF16) for t in totals]
    late = jnp.stack(
        [
            norm1_gain_grad,
            norm1_bias_grad,
            jnp.concatenate([qv_sums[0, :head_cols], qv_sums[0, 2 * head_cols :]]),
        ]
    )
    late = jnp.pad(late, ((0, 5), (0, 0)))

    def late_rows(late):
        high, low = high_low(late)
        both = jnp.pad(jnp.concatenate([high, low], axis=0), ((0, 0), (0, split - feat_dim)))
        return high.astype(F32) + low.astype(F32), both

    def late_sum(own, came):
        came = came[:, :feat_dim].astype(F32)
        return own + (came[:8] + came[8:])

    size = chunk
    for turn in range(len(bits) - 1, 0, -1):
        own, both = late_rows(late)
        first, second = lax.optimization_barrier(
            (jnp.concatenate([mine[0], both], axis=0), mine[1])
        )
        came = across(first, orders[0][turn], sources)
        came_b = across(second, orders[1][turn], sources)
        late = late_sum(own, came[size:])
        mine = [
            jnp.concatenate([mine[0], came[:size]], axis=0),
            jnp.concatenate([mine[1], came_b], axis=0),
        ]
        size = 2 * size
    own, both = late_rows(late)
    first, second, input_grad, output = lax.optimization_barrier(
        (jnp.concatenate([mine[0], both], axis=0), mine[1], input_grad, output)
    )
    came = across(first, bits[0], sources)
    came_b = across(second, bits[0], sources)
    late = late_sum(own, came[size:])
    qv_bias_grad = late[2].reshape(2, head_cols)
    if chunk % 16 == 0:
        qkv_grad, proj_grad, router_grad, out_bias_grad, norm_grads = finish(
            me, first, second, came, came_b, head_cols, experts, feat_dim, orders
        )
        router_grad = router_grad.T
    else:
        first = tn(mix_t[0], jnp.concatenate([mine[0], came[:size]], axis=0))
        second = tn(mix_t[1], jnp.concatenate([mine[1], came_b], axis=0))
        qkv_grad = jnp.stack(
            [first[:, :head_cols], first[:, head_cols : 2 * head_cols], second[:, :head_cols]]
        )
        proj_grad = second[:, head_cols:].T
        router_grad = first[:, 2 * head_cols : 2 * head_cols + experts]
        norm_grads = first[:, 2 * head_cols + experts :].T
        out_bias_grad, norm_grads = norm_grads[:experts], norm_grads[experts:]
    norm2_gain_grad, norm2_bias_grad, proj_bias_grad = norm_grads[0], norm_grads[1], norm_grads[2]
    return (
        output,
        input_grad,
        late[0],
        late[1],
        qkv_grad,
        qv_bias_grad,
        proj_grad,
        proj_bias_grad,
        norm2_gain_grad,
        norm2_bias_grad,
        router_grad,
        in_weight_grad[None],
        in_bias_grad,
        out_weight_grad[None],
        out_bias_grad,
    )


def solution(mesh):
    return jax.shard_map(
        local,
        mesh=mesh,
        in_specs=(
            P("dp", None),
            P(),
            P(),
            P(None, None, "tensor"),
            P(None, "tensor"),
            P("tensor", None),
            P(),
            P(),
            P(),
            P(),
            P("dp", None, "tensor"),
            P("dp", "tensor"),
            P("dp", "tensor", None),
            P(),
            P("dp", None),
            P("dp", None),
        ),
        out_specs=(
            P("dp", None),
            P("dp", None),
            P(),
            P(),
            P(None, None, "tensor"),
            P(None, "tensor"),
            P("tensor", None),
            P(),
            P(),
            P(),
            P(),
            P("dp", None, "tensor"),
            P("dp", "tensor"),
            P("dp", "tensor", None),
            P(),
        ),
        check_vma=False,
    )
```

```python
import jax
import jax.numpy as jnp
from jax import lax
from jax.experimental import pallas as pl
from jax.experimental.pallas import tpu as pltpu
from jax.sharding import PartitionSpec as P

HEAD = 64
SEQ = 197
F32 = jnp.float32
BF16 = jnp.bfloat16

epsilon = 1e-06


def norm_parts(values):
    average = jnp.mean(values, axis=-1, keepdims=True)
    centred = values - average
    inverse = lax.rsqrt(jnp.mean(centred * centred, axis=-1, keepdims=True) + epsilon)
    return (centred * inverse, inverse)


def norm_back(inner_grad, normed, inverse):
    first_mean = jnp.mean(inner_grad, axis=-1, keepdims=True)
    second_mean = jnp.mean(inner_grad * normed, axis=-1, keepdims=True)
    return inverse * (inner_grad - first_mean - normed * second_mean)


def gelu_parts(pre_act):
    normal_cdf = 0.5 * (1.0 + lax.erf(pre_act * 0.7071067811865476))
    density = jnp.exp(-0.5 * pre_act * pre_act) * 0.3989422804014327
    return (pre_act * normal_cdf, normal_cdf + pre_act * density)


def dot(a, b, dims, out=F32):
    return lax.dot_general(a, b, (dims, ((), ())), preferred_element_type=out)


def nn(a, b):
    return dot(a, b, ((1,), (0,)))


def nt(a, b):
    return dot(a, b, ((1,), (1,)))


def tn(a, b):
    return dot(a, b, ((0,), (0,)))


def exact(a, b):
    return lax.dot_general(
        a,
        b,
        (((1,), (0,)), ((), ())),
        precision=lax.Precision.HIGHEST,
        preferred_element_type=F32,
    )


def swap(x):
    return lax.ppermute(x, "tensor", [(0, 1), (1, 0)])


def across(x, bit, count):
    return lax.ppermute(x, "dp", [(i, i ^ bit) for i in range(count)])


def in_order(plane, mine, other, axis):
    first = jnp.where(plane == 0, mine, other)
    second = jnp.where(plane == 0, other, mine)
    return jnp.concatenate([first, second], axis=axis)


def half_of(plane, x, which):
    width = x.shape[-1] // 2
    low, high = x[..., :width], x[..., width:]
    return jnp.where((plane == which), low, high)


def keep_half(total, came):
    middle = total.shape[0] // 2
    return total[:middle] + came.astype(F32)


def send_half(total, bit, count):
    return across(total[total.shape[0] // 2 :].astype(BF16), bit, count)


def expert_kernel(
    capacity, slots, own_ref, arrived_ref, cot_ref, other_ref, router_ref, in_ref, bias_ref, out_ref,
    activ_ref, slope_ref, grad_rows_ref, row_ref, out_rows_ref, bias_grad_ref, gate_ref, row_sum, out_sum,
):
    step = pl.program_id(0)
    count = arrived_ref.shape[0]
    experts = router_ref.shape[1]

    @pl.when(step == 0)
    def _():
        logits = nn(arrived_ref[...], router_ref[...])
        ids = lax.broadcasted_iota(jnp.int32, (count, experts), 1)
        own = jnp.sum(jnp.where(ids == own_ref[0], logits, 0.0), axis=1, keepdims=True)
        other = jnp.sum(jnp.where(ids.astype(F32) == other_ref[...], logits, 0.0), axis=1, keepdims=True)
        top = jnp.maximum(own, other)
        own, other = jnp.exp(own - top), jnp.exp(other - top)
        spot = lax.broadcasted_iota(jnp.int32, (count, 1), 0) % slots
        gate = jnp.where(spot < capacity, own / (own + other), 0.0)
        gate_ref[...] = jnp.broadcast_to(gate, gate_ref.shape)
        grad_rows_ref[...] = (gate * cot_ref[...].astype(F32)).astype(BF16)
        row_sum[...] = jnp.zeros_like(row_sum)
        out_sum[...] = jnp.zeros_like(out_sum)

    pre_act = nn(arrived_ref[...], in_ref[...]) + bias_ref[...]
    activ, slope = gelu_parts(pre_act)
    activ = activ.astype(BF16)
    activ_ref[...] = activ
    grad = nt(grad_rows_ref[...], out_ref[...]) * slope
    bias_grad_ref[...] = jnp.sum(grad, axis=0, keepdims=True)
    grad = grad.astype(BF16)
    slope_ref[...] = grad
    row_sum[...] += nt(grad, in_ref[...])
    out_sum[...] += nn(activ, out_ref[...])

    @pl.when(step == pl.num_programs(0) - 1)
    def _():
        inner = jnp.sum(cot_ref[...].astype(F32) * out_sum[...], axis=1, keepdims=True)
        inner = jnp.broadcast_to(inner, gate_ref.shape).T
        out_rows_ref[...] = (gate_ref[:, :1] * out_sum[...]).astype(BF16)
        spot = lax.broadcasted_iota(jnp.int32, (slots, 128), 0)
        row_ref[...] = row_sum[...].astype(BF16)
        for source in range(count // slots):
            first = source * slots
            line = inner[:1, first : first + slots]
            line = jnp.concatenate([line, jnp.zeros((1, 128 - slots), F32)], axis=1)
            high = line.astype(BF16).astype(F32)
            tail = row_sum[first + slots - 16 : first + slots, :128]
            place = lax.broadcasted_iota(jnp.int32, tail.shape, 0)
            tail = jnp.where(place == 15, high, jnp.where(place == 14, line - high, tail))
            row_ref[first + slots - 16 : first + slots, :128] = tail.astype(BF16)


def expert_rows(own, arrived, cot_rows, other, router, in_weight, in_bias, out_weight, capacity, slots):
    count, feat_dim = arrived.shape
    hidden = in_weight.shape[1]
    block = 512 if hidden % 512 == 0 else hidden
    whole = lambda shape: pl.BlockSpec(shape, lambda i: (0, 0))
    return pl.pallas_call(
        lambda *refs: expert_kernel(capacity, slots, *refs),
        grid=(hidden // block,),
        in_specs=[
            pl.BlockSpec(memory_space=pltpu.SMEM),
            whole((count, feat_dim)),
            whole((count, feat_dim)),
            whole((count, 1)),
            whole(router.shape),
            pl.BlockSpec((feat_dim, block), lambda i: (0, i)),
            pl.BlockSpec((1, block), lambda i: (0, i)),
            pl.BlockSpec((block, feat_dim), lambda i: (i, 0)),
        ],
        out_specs=[
            pl.BlockSpec((count, block), lambda i: (0, i)),
            pl.BlockSpec((count, block), lambda i: (0, i)),
            whole((count, feat_dim)),
            whole((count, feat_dim)),
            whole((count, feat_dim)),
            pl.BlockSpec((1, block), lambda i: (0, i)),
        ],
        out_shape=(
            jax.ShapeDtypeStruct((count, hidden), BF16),
            jax.ShapeDtypeStruct((count, hidden), BF16),
            jax.ShapeDtypeStruct((count, feat_dim), BF16),
            jax.ShapeDtypeStruct((count, feat_dim), BF16),
            jax.ShapeDtypeStruct((count, feat_dim), BF16),
            jax.ShapeDtypeStruct((1, hidden), F32),
        ),
        scratch_shapes=[
            pltpu.VMEM((count, 128), F32),
            pltpu.VMEM((count, feat_dim), F32),
            pltpu.VMEM((count, feat_dim), F32),
        ],
        compiler_params=pltpu.CompilerParams(vmem_limit_bytes=60 << 20),
        cost_estimate=pl.CostEstimate(
            flops=8 * count * feat_dim * hidden, bytes_accessed=12 << 20, transcendentals=2 * count * hidden
        ),
        name="expert_rows",
    )(own[None], arrived, cot_rows, other, router, in_weight, in_bias, out_weight)


def expert_rows_plain(own, arrived, cot_rows, other, router, in_weight, in_bias, out_weight, capacity, slots):
    count, feat_dim = arrived.shape
    logits = nn(arrived, router)
    ids = jnp.arange(router.shape[1], dtype=jnp.int32)[None, :]
    own = jnp.sum(jnp.where(ids == own, logits, 0.0), axis=1, keepdims=True)
    other = jnp.sum(jnp.where(ids.astype(F32) == other, logits, 0.0), axis=1, keepdims=True)
    top = jnp.maximum(own, other)
    own, other = jnp.exp(own - top), jnp.exp(other - top)
    spot = jnp.arange(count, dtype=jnp.int32)[:, None] % slots
    gate = jnp.where(spot < capacity, own / (own + other), 0.0)
    grad_rows = (gate * cot_rows.astype(F32)).astype(BF16)
    activ, slope = gelu_parts(nn(arrived, in_weight) + in_bias)
    activ = activ.astype(BF16)
    grad = nt(grad_rows, out_weight) * slope
    bias_grad = jnp.sum(grad, axis=0, keepdims=True)
    grad = grad.astype(BF16)
    part_out = nn(activ, out_weight)
    inner = jnp.sum(cot_rows.astype(F32) * part_out, axis=1).reshape(-1, slots)
    high, low = high_low(jnp.pad(inner, ((0, 0), (0, feat_dim - slots)))[:, None, :])
    rows = nt(grad, in_weight).astype(BF16).reshape(-1, slots, feat_dim)
    rows = jnp.concatenate([rows[:, : slots - 2], low, high], axis=1).reshape(count, feat_dim)
    return activ, grad, grad_rows, rows, (gate * part_out).astype(BF16), bias_grad


def home_kernel(back_ref, onehot_ref, facts_ref, home_ref, inner_ref):
    experts, slots, feat_dim = back_ref.shape
    tok_count = facts_ref.shape[0]
    home = nn(onehot_ref[...], back_ref[...].reshape(experts * slots, feat_dim))
    home_ref[:tok_count, :] = home.astype(BF16)
    for e in range(experts):
        inner_ref[0, e : e + 1, :] = back_ref[e, slots - 1 : slots, :slots].astype(F32)
        inner_ref[1, e : e + 1, :] = back_ref[e, slots - 2 : slots - 1, :slots].astype(F32)
    expert_ids = lax.broadcasted_iota(jnp.int32, (tok_count, experts), 1).astype(F32)
    slot_ids = lax.broadcasted_iota(jnp.int32, (tok_count, slots), 1).astype(F32)
    lanes = lax.broadcasted_iota(jnp.int32, (tok_count, 128), 1)
    table = jnp.zeros((tok_count, 128), F32)
    for k in range(2):
        hot = jnp.where(facts_ref[:, k : k + 1] == expert_ids, 1.0, 0.0).astype(BF16)
        found = nn(hot, inner_ref[0].astype(BF16)) + nn(hot, inner_ref[1].astype(BF16))
        found = jnp.where(facts_ref[:, k + 2 : k + 3] == slot_ids, found, 0.0)
        found = jnp.sum(found, axis=1, keepdims=True)
        high = found.astype(BF16).astype(F32)
        table = jnp.where(lanes == 2 * k, high, jnp.where(lanes == 2 * k + 1, found - high, table))
    home_ref[tok_count + 3 : tok_count + 11, :tok_count] = table.T[:8, :].astype(BF16)


def home_rows(back, onehot, facts):
    experts, slots, feat_dim = back.shape
    tok_count = facts.shape[0]
    return pl.pallas_call(
        home_kernel,
        out_shape=jax.ShapeDtypeStruct((tok_count + 11, feat_dim), BF16),
        scratch_shapes=[pltpu.VMEM((2, experts, slots), F32)],
        compiler_params=pltpu.CompilerParams(vmem_limit_bytes=16 << 20),
        cost_estimate=pl.CostEstimate(
            flops=2 * tok_count * feat_dim * experts * slots, bytes_accessed=2 << 20, transcendentals=0
        ),
        name="home_rows",
    )(back, onehot, facts)


def attention_grads_kernel(
    home_ref, other_ref, router_ref, cot_ref, normed_ref, facts_ref, gain_ref, hidden2_ref, bias_grad_ref,
    proj_ref, projected_ref, attended_ref, hidden_ref, weight_ref, mix_ref,
    sent_ref, kept_ref, hidden_part_ref, sums_ref, middle_grad_ref, low_ref, back_ref, small_ref, logit_ref,
):
    head_cols = attended_ref.shape[1]
    experts = router_ref.shape[1]
    tok_count = cot_ref.shape[0]
    scale = HEAD ** (-0.5)
    lines = slice(tok_count + 3, tok_count + 11)
    inner = home_ref[lines, :tok_count].astype(F32) + other_ref[lines, :tok_count].astype(F32)
    inner = inner.T
    bias_dot = facts_ref[:, 16 : 16 + experts]
    expert_ids = lax.broadcasted_iota(jnp.int32, (tok_count, experts), 1).astype(F32)
    picks = [facts_ref[:, k : k + 1] == expert_ids for k in range(2)]
    gates = [facts_ref[:, k + 4 : k + 5] for k in range(2)]
    inner_grads = []
    for k in range(2):
        own_bias = jnp.sum(jnp.where(picks[k], bias_dot, 0.0), axis=1, keepdims=True)
        inner_grads.append(inner[:, 2 * k : 2 * k + 1] + inner[:, 2 * k + 1 : 2 * k + 2] + own_bias)
    mean = gates[0] * inner_grads[0] + gates[1] * inner_grads[1]
    logit_grad = 0.0
    for k in range(2):
        logit_grad = logit_grad + jnp.where(picks[k], gates[k] * (inner_grads[k] - mean), 0.0)
    logit_ref[...] = logit_grad.astype(BF16)
    hidden_grad = home_ref[:tok_count, :].astype(F32) + other_ref[:tok_count, :].astype(F32)
    hidden_grad = hidden_grad + nt(logit_ref[...], router_ref[...])
    normed = normed_ref[...]
    inner = hidden_grad * gain_ref[...]
    middle_grad = cot_ref[...].astype(F32) + norm_back(inner, normed, facts_ref[:, 6:7])
    middle_grad_ref[...] = middle_grad
    middle_low = middle_grad.astype(BF16)
    small_ref[...] = jnp.zeros_like(small_ref)
    small_ref[:experts, :] = tn(logit_ref[...], hidden2_ref[...])
    small_ref[experts : 2 * experts, :] = bias_grad_ref[...]
    small_ref[2 * experts : 2 * experts + 1, :] = jnp.sum(hidden_grad * normed, axis=0, keepdims=True)
    small_ref[2 * experts + 1 : 2 * experts + 2, :] = jnp.sum(hidden_grad, axis=0, keepdims=True)
    small_ref[2 * experts + 2 : 2 * experts + 3, :] = jnp.sum(middle_grad, axis=0, keepdims=True)
    back_ref[...] = nt(middle_low, proj_ref[...]).astype(BF16)
    for h in range(head_cols // HEAD):
        cols = slice(h * HEAD, (h + 1) * HEAD)
        queries, key_vals, values_in = (projected_ref[j, :, cols] for j in range(3))
        out_grad = back_ref[:, cols]
        prob_vals = jnp.exp(nt(queries, key_vals) * scale - facts_ref[:, h + 8 : h + 9])
        prob_low = prob_vals.astype(BF16)
        prob_grad = nt(out_grad, values_in)
        row = jnp.sum(prob_vals * prob_grad, axis=-1, keepdims=True)
        score_low = (prob_vals * (prob_grad - row)).astype(BF16)
        low_ref[:, h * HEAD : (h + 1) * HEAD] = (nn(score_low, key_vals) * scale).astype(BF16)
        start = head_cols + h * HEAD
        low_ref[:, start : start + HEAD] = (tn(score_low, queries) * scale).astype(BF16)
        start = start + head_cols
        low_ref[:, start : start + HEAD] = tn(prob_low, out_grad).astype(BF16)
    low = low_ref[...]
    half = kept_ref.shape[0]
    mixed_middle = nt(mix_ref[1], middle_low).astype(BF16)
    small = small_ref[...].astype(BF16)
    for part in range(2):
        rows = slice(part * half, (part + 1) * half)
        pieces = (
            nn(hidden_ref[0, rows, :], low[:, : 2 * head_cols]),
            nt(mix_ref[0, rows, :], small),
            nn(hidden_ref[1, rows, :], low[:, 2 * head_cols :]),
            nn(mixed_middle[rows, :], attended_ref[...]),
        )
        first = 0
        for piece in pieces:
            last = first + piece.shape[1]
            if part == 0:
                kept_ref[:, first:last] = piece
            else:
                sent_ref[:, first:last] = piece.astype(BF16)
            first = last
    part = nt(low[:, :head_cols], weight_ref[0])
    part = part + nt(low[:, head_cols : 2 * head_cols], weight_ref[1])
    part = part + nt(low[:, 2 * head_cols :], weight_ref[2])
    hidden_part_ref[...] = part.astype(BF16)
    sums_ref[...] = jnp.sum(low.astype(F32), axis=0, keepdims=True)


def attention_grads(*operands):
    tok_count, feat_dim = operands[3].shape
    experts = operands[2].shape[1]
    head_cols = operands[9].shape[0]
    small = -(-(2 * experts + 3) // 128) * 128
    width = 4 * head_cols + small
    flops = 2 * tok_count * feat_dim * head_cols * 9 + 2 * feat_dim * feat_dim * (tok_count + small)
    return pl.pallas_call(
        attention_grads_kernel,
        out_shape=(
            jax.ShapeDtypeStruct((feat_dim // 2, width), BF16),
            jax.ShapeDtypeStruct((feat_dim // 2, width), F32),
            jax.ShapeDtypeStruct((tok_count, feat_dim), BF16),
            jax.ShapeDtypeStruct((1, 3 * head_cols), F32),
            jax.ShapeDtypeStruct((tok_count, feat_dim), F32),
        ),
        scratch_shapes=[
            pltpu.VMEM((tok_count, 3 * head_cols), BF16),
            pltpu.VMEM((tok_count, head_cols), BF16),
            pltpu.VMEM((small, feat_dim), F32),
            pltpu.VMEM((tok_count, experts), BF16),
        ],
        compiler_params=pltpu.CompilerParams(vmem_limit_bytes=60 << 20),
        cost_estimate=pl.CostEstimate(
            flops=flops, bytes_accessed=10 << 20, transcendentals=tok_count * tok_count * 6
        ),
        name="attention_grads",
    )(*operands)


def finish_kernel(head_cols, experts, orders, me_ref, mine, mine_b, got, got_b, qkv_ref, proj_ref, router_ref, bias_ref, norm_ref, held_proj, held_small):
    me = me_ref[0]
    count = 1 << len(orders[0])
    feat_dim = qkv_ref.shape[1]
    chunk = feat_dim // count
    half = count // 2
    for spot in range(count):
        starts = []
        for order in orders:
            name = sum(bit for i, bit in enumerate(order) if (spot >> (len(order) - 1 - i)) & 1)
            starts.append(pl.ds(pl.multiple_of((name ^ me) * chunk, chunk), chunk))
        source, source_b = (mine, mine_b) if spot < half else (got, got_b)
        first = (spot % half) * chunk
        piece = source[first : first + chunk, :].astype(F32)
        qkv_ref[0, starts[0], :] = piece[:, :head_cols]
        qkv_ref[1, starts[0], :] = piece[:, head_cols : 2 * head_cols]
        held_small[starts[0], :] = piece[:, 2 * head_cols :]
        piece = source_b[first : first + chunk, :].astype(F32)
        qkv_ref[2, starts[1], :] = piece[:, :head_cols]
        held_proj[starts[1], :] = piece[:, head_cols:]
    proj_ref[...] = held_proj[...].T
    small = held_small[...]
    flat = small.T
    router_ref[...] = flat[:experts]
    bias_ref[...] = flat[experts : 2 * experts]
    norm_ref[...] = flat[2 * experts : 2 * experts + 8]


def finish(me, mine, mine_b, came, came_b, head_cols, experts, feat_dim, orders):
    width = mine.shape[1] - 2 * head_cols
    vmem = pl.BlockSpec(memory_space=pltpu.VMEM)
    return pl.pallas_call(
        lambda *refs: finish_kernel(head_cols, experts, orders, *refs),
        in_specs=[pl.BlockSpec(memory_space=pltpu.SMEM)] + [vmem] * 4,
        out_specs=[vmem] * 5,
        out_shape=(
            jax.ShapeDtypeStruct((3, feat_dim, head_cols), F32),
            jax.ShapeDtypeStruct((head_cols, feat_dim), F32),
            jax.ShapeDtypeStruct((experts, feat_dim), F32),
            jax.ShapeDtypeStruct((experts, feat_dim), F32),
            jax.ShapeDtypeStruct((8, feat_dim), F32),
        ),
        scratch_shapes=[
            pltpu.VMEM((feat_dim, head_cols), F32),
            pltpu.VMEM((feat_dim, width), F32),
        ],
        compiler_params=pltpu.CompilerParams(vmem_limit_bytes=40 << 20),
        name="finish",
    )(me[None], mine, mine_b, came, came_b)


def high_low(values):
    high = values.astype(BF16)
    return high, (values - high.astype(F32)).astype(BF16)


def local(
    inputs,
    norm1_gain,
    norm1_bias,
    qkv_weight,
    qv_bias,
    proj_weight,
    proj_bias,
    norm2_gain,
    norm2_bias,
    router,
    expert_in,
    expert_in_bias,
    expert_out,
    expert_out_bias,
    routes,
    cotangent,
):
    tok_count = inputs.shape[0]
    feat_dim = inputs.shape[1]
    half_dim = feat_dim // 2
    head_cols = qkv_weight.shape[2]
    heads_here = head_cols // HEAD
    images = tok_count // SEQ
    experts = router.shape[1]
    sources = lax.axis_size("dp")
    group_size = sources // experts
    capacity = max(2, (10 * tok_count + 3 * experts - 1) // (3 * experts))
    slots = (capacity + 3 + 15) // 16 * 16
    score_scale = HEAD ** (-0.5)
    plane = lax.axis_index("tensor")
    me = lax.axis_index("dp")
    own_expert = me // group_size
    in_weight, out_weight = expert_in[0], expert_out[0]

    expert_ids = jnp.arange(experts, dtype=jnp.int32)
    slot_ids = jnp.arange(slots, dtype=jnp.int32)
    all_ids = jnp.arange(experts * slots, dtype=jnp.int32)
    pick = [(routes[:, k : k + 1] == expert_ids[None, :]) for k in range(2)]
    named = (pick[0] | pick[1]).astype(BF16)
    before = (
        jnp.arange(tok_count)[:, None] > jnp.arange(tok_count)[None, :]
    ).astype(BF16)
    earlier = nn(before, named)
    rank = [
        jnp.sum(jnp.where(pick[k], earlier, 0.0), axis=1, keepdims=True).astype(jnp.int32)
        for k in range(2)
    ]
    place = [routes[:, k : k + 1] * slots + rank[k] for k in range(2)]
    onehot = ((place[0] == all_ids[None, :]) | (place[1] == all_ids[None, :])).astype(BF16)
    rank_hot = [(rank[k] == slot_ids[None, :]) for k in range(2)]
    pick_low = [pick[k].astype(BF16) for k in range(2)]
    partner = [
        jnp.where(rank_hot[k], routes[:, 1 - k : 2 - k].astype(F32), 0.0).astype(BF16)
        for k in range(2)
    ]
    partner_map = tn(pick_low[0], partner[0]) + tn(pick_low[1], partner[1])

    cot_send = tn(onehot, cotangent).astype(BF16).reshape(experts, slots, feat_dim)
    note = jnp.pad(partner_map.astype(BF16), ((0, 0), (0, feat_dim - slots)))[:, None, :]
    cot_send = jnp.where(slot_ids[None, :, None] == slots - 1, note, cot_send)
    cot_send = jnp.repeat(cot_send, group_size, axis=0)
    proj_other = swap(proj_weight)
    proj_full = in_order(plane, proj_weight, proj_other, 0)

    inputs, cot_send = lax.optimization_barrier((inputs, cot_send))
    cot_rows = lax.all_to_all(cot_send, "dp", split_axis=0, concat_axis=0, tiled=True)
    x_in = inputs.astype(F32)
    normed1, inverse1 = norm_parts(x_in)
    hidden1 = (normed1 * norm1_gain + norm1_bias).astype(BF16)
    projected = jnp.einsum("td,jde->jte", hidden1, qkv_weight, preferred_element_type=F32)
    bias_rows = jnp.stack([qv_bias[0], jnp.zeros_like(qv_bias[0]), qv_bias[1]])
    projected = (projected + bias_rows[:, None, :]).astype(BF16)
    projected, proj_full = lax.optimization_barrier((projected, proj_full))
    heads_view = projected.reshape(3, images, SEQ, heads_here, HEAD)
    queries, key_vals, values_in = (heads_view[0], heads_view[1], heads_view[2])
    scores = (
        jnp.einsum("bqhd,bkhd->bhqk", queries, key_vals, preferred_element_type=F32)
        * score_scale
    )
    row_max = jnp.max(scores, axis=-1, keepdims=True)
    exp_scores = jnp.exp(scores - row_max)
    row_total = jnp.sum(exp_scores, axis=-1, keepdims=True)
    lse = (row_max + jnp.log(row_total)).reshape(heads_here, tok_count).T
    prob_low = (exp_scores / row_total).astype(BF16)
    attended = jnp.einsum("bhqk,bkhd->bqhd", prob_low, values_in, preferred_element_type=F32)
    attended = attended.reshape(tok_count, head_cols).astype(BF16)
    attended_all = in_order(plane, attended, swap(attended), 1)
    attended_all, cot_rows = lax.optimization_barrier((attended_all, cot_rows))
    middle = x_in + nn(attended_all, proj_full) + proj_bias
    normed2, inverse2 = norm_parts(middle)
    hidden2 = (normed2 * norm2_gain + norm2_bias).astype(BF16)

    send = tn(onehot, hidden2).astype(BF16).reshape(experts, slots, feat_dim)
    send = jnp.repeat(send, group_size, axis=0)
    arrived = lax.all_to_all(send, "dp", split_axis=0, concat_axis=0, tiled=True)
    arrived = arrived.reshape(-1, feat_dim)

    logits = nn(hidden2, router)
    chosen = [jnp.sum(jnp.where(pick[k], logits, 0.0), axis=1, keepdims=True) for k in range(2)]
    chosen_max = jnp.maximum(chosen[0], chosen[1])
    chosen_exp = [jnp.exp(chosen[k] - chosen_max) for k in range(2)]
    chosen_sum = chosen_exp[0] + chosen_exp[1]
    gate_vals = [chosen_exp[k] / chosen_sum for k in range(2)]
    gate_map = jnp.where(pick[0], gate_vals[0], 0.0) + jnp.where(pick[1], gate_vals[1], 0.0)
    grad_out = cotangent.astype(F32)
    row_grad = [(gate_vals[k] * grad_out).astype(BF16) for k in range(2)]
    out_bias_grad = tn(pick_low[0], row_grad[0]) + tn(pick_low[1], row_grad[1])

    other_expert = cot_rows[:, slots - 1, :slots].reshape(-1, 1).astype(F32)
    cot_rows = cot_rows.reshape(-1, feat_dim)
    bits = [1 << i for i in range(sources.bit_length() - 1)]
    orders = [bits, bits[:1] + bits[2:] + bits[1:2]]
    chunk = feat_dim // sources

    rows = jnp.arange(feat_dim, dtype=jnp.int32)[None, :]
    cols = jnp.arange(feat_dim, dtype=jnp.int32)[:, None]
    spot = cols // chunk
    mix_t = []
    for order in orders:
        piece = jnp.zeros_like(spot)
        for i, bit in enumerate(order):
            piece = piece | jnp.where((spot >> (len(bits) - 1 - i)) & 1 == 1, bit, 0)
        mix_t.append(
            ((rows // chunk == (piece ^ me)) & (rows % chunk == cols % chunk)).astype(BF16)
        )
    mix_t = jnp.stack(mix_t)
    hidden1_t = jnp.einsum("jqd,td->jqt", mix_t, hidden1, preferred_element_type=F32).astype(BF16)
    bias_dot = lax.dot_general(
        grad_out,
        expert_out_bias,
        (((1,), (1,)), ((), ())),
        precision=lax.Precision.HIGHEST,
        preferred_element_type=F32,
    )
    facts = [routes.astype(F32)] + [r.astype(F32) for r in rank] + gate_vals + [inverse2]
    facts = jnp.concatenate(facts, axis=1)
    facts = jnp.concatenate([facts, jnp.zeros_like(facts[:, :1]), lse], axis=1)
    facts = jnp.pad(facts, ((0, 0), (0, 16 - facts.shape[1])))
    facts = jnp.pad(jnp.concatenate([facts, bias_dot], axis=1), ((0, 0), (0, 112 - experts)))
    ready = (
        mix_t, hidden1_t, facts, onehot, out_bias_grad, normed2, hidden2, projected, attended, router, gate_map,
        other_expert,
    )
    arrived, ready = lax.optimization_barrier((arrived, ready))
    (
        mix_t, hidden1_t, facts, onehot, out_bias_grad, normed2, hidden2, projected, attended, router, gate_map,
        other_expert,
    ) = ready
    activ_low, act_low, grad_rows, row_send, out_send, in_bias_grad = (
        expert_rows if sources * slots <= 1024 else expert_rows_plain
    )(
        own_expert, arrived, cot_rows, other_expert, router, in_weight, expert_in_bias, out_weight, capacity, slots
    )
    row_send = row_send.reshape(sources, slots, feat_dim)
    row_back = lax.all_to_all(row_send, "dp", split_axis=0, concat_axis=0, tiled=True)
    out_weight_grad = tn(activ_low, grad_rows)
    in_weight_grad = tn(arrived, act_low)
    out_send, out_weight_grad, in_weight_grad = lax.optimization_barrier(
        (out_send, out_weight_grad, in_weight_grad)
    )
    def over_group(x):
        if group_size == 1:
            return x
        shape = (experts, group_size) + x.shape[1:]
        return jnp.sum(x.reshape(shape).astype(F32), axis=1).astype(BF16)

    row_home = home_rows(
        over_group(row_back),
        onehot,
        facts,
    )
    out_send = out_send.reshape(sources, slots, feat_dim)
    row_other = swap(row_home)
    out_back = lax.all_to_all(out_send, "dp", split_axis=0, concat_axis=0, tiled=True)

    sent, kept, hidden1_part, qv_sums, middle_grad = attention_grads(
        row_home,
        row_other,
        router,
        cotangent,
        normed2,
        facts,
        norm2_gain[None],
        hidden2,
        out_bias_grad,
        proj_weight,
        projected,
        attended,
        hidden1_t,
        qkv_weight,
        mix_t,
    )
    hidden1_other = swap(hidden1_part)
    split = sent.shape[1] - 2 * head_cols
    sent, out_back = lax.optimization_barrier((sent, out_back))
    came = across(sent, bits[0], sources)
    total = kept + came.astype(F32)
    totals = [total[:, :split], total[:, split:]]
    out_home = nn(onehot, over_group(out_back).reshape(-1, feat_dim)).astype(BF16)
    for turn in range(1, len(bits)):
        totals, out_home = lax.optimization_barrier((totals, out_home))
        if turn == len(bits) - 1:
            out_other = swap(out_home)
        if turn == 2:
            totals, hidden1_other = lax.optimization_barrier((totals, hidden1_other))
        cames = [send_half(t, order[turn], sources) for t, order in zip(totals, orders)]
        totals = [keep_half(t, c) for t, c in zip(totals, cames)]
    hidden1_grad = hidden1_part.astype(F32) + hidden1_other.astype(F32)
    norm1_gain_grad = jnp.sum(hidden1_grad * normed1, axis=0)
    norm1_bias_grad = jnp.sum(hidden1_grad, axis=0)
    input_grad = middle_grad + norm_back(hidden1_grad * norm1_gain, normed1, inverse1)
    bias_home = exact(gate_map, expert_out_bias)
    mine = [t.astype(BF16) for t in totals]
    late = jnp.stack(
        [
            norm1_gain_grad,
            norm1_bias_grad,
            jnp.concatenate([qv_sums[0, :head_cols], qv_sums[0, 2 * head_cols :]]),
        ]
    )
    late = jnp.pad(late, ((0, 5), (0, 0)))

    def late_rows(late):
        high, low = high_low(late)
        both = jnp.pad(jnp.concatenate([high, low], axis=0), ((0, 0), (0, split - feat_dim)))
        return high.astype(F32) + low.astype(F32), both

    def late_sum(own, came):
        came = came[:, :feat_dim].astype(F32)
        return own + (came[:8] + came[8:])

    size = chunk
    for turn in range(len(bits) - 1, 0, -1):
        own, both = late_rows(late)
        first, second = jnp.concatenate([mine[0], both], axis=0), mine[1]
        if turn == 1:
            first, second, out_other = lax.optimization_barrier((first, second, out_other))
        else:
            first, second = lax.optimization_barrier((first, second))
        came = across(first, orders[0][turn], sources)
        came_b = across(second, orders[1][turn], sources)
        late = late_sum(own, came[size:])
        mine = [
            jnp.concatenate([mine[0], came[:size]], axis=0),
            jnp.concatenate([mine[1], came_b], axis=0),
        ]
        size = 2 * size
    out_home = out_home.astype(F32) + out_other.astype(F32)
    output = (middle + (out_home + bias_home)).astype(BF16)
    own, both = late_rows(late)
    first, second, input_grad, output = lax.optimization_barrier(
        (jnp.concatenate([mine[0], both], axis=0), mine[1], input_grad, output)
    )
    came = across(first, bits[0], sources)
    came_b = across(second, bits[0], sources)
    late = late_sum(own, came[size:])
    qv_bias_grad = late[2].reshape(2, head_cols)
    if chunk % 16 == 0:
        qkv_grad, proj_grad, router_grad, out_bias_grad, norm_grads = finish(
            me, first, second, came, came_b, head_cols, experts, feat_dim, orders
        )
        router_grad = router_grad.T
    else:
        first = tn(mix_t[0], jnp.concatenate([mine[0], came[:size]], axis=0))
        second = tn(mix_t[1], jnp.concatenate([mine[1], came_b], axis=0))
        qkv_grad = jnp.stack(
            [first[:, :head_cols], first[:, head_cols : 2 * head_cols], second[:, :head_cols]]
        )
        proj_grad = second[:, head_cols:].T
        router_grad = first[:, 2 * head_cols : 2 * head_cols + experts]
        norm_grads = first[:, 2 * head_cols + experts :].T
        out_bias_grad, norm_grads = norm_grads[:experts], norm_grads[experts:]
    norm2_gain_grad, norm2_bias_grad, proj_bias_grad = norm_grads[0], norm_grads[1], norm_grads[2]
    return (
        output,
        input_grad,
        late[0],
        late[1],
        qkv_grad,
        qv_bias_grad,
        proj_grad,
        proj_bias_grad,
        norm2_gain_grad,
        norm2_bias_grad,
        router_grad,
        in_weight_grad[None],
        in_bias_grad,
        out_weight_grad[None],
        out_bias_grad,
    )


def solution(mesh):
    return jax.shard_map(
        local,
        mesh=mesh,
        in_specs=(
            P("dp", None),
            P(),
            P(),
            P(None, None, "tensor"),
            P(None, "tensor"),
            P("tensor", None),
            P(),
            P(),
            P(),
            P(),
            P("dp", None, "tensor"),
            P("dp", "tensor"),
            P("dp", "tensor", None),
            P(),
            P("dp", None),
            P("dp", None),
        ),
        out_specs=(
            P("dp", None),
            P("dp", None),
            P(),
            P(),
            P(None, None, "tensor"),
            P(None, "tensor"),
            P("tensor", None),
            P(),
            P(),
            P(),
            P(),
            P("dp", None, "tensor"),
            P("dp", "tensor"),
            P("dp", "tensor", None),
            P(),
        ),
        check_vma=False,
    )
```

```python
import jax
import jax.numpy as jnp
from jax import lax
from jax.experimental import pallas as pl
from jax.experimental.pallas import tpu as pltpu
from jax.sharding import PartitionSpec as P

HEAD = 64
SEQ = 197
F32 = jnp.float32
BF16 = jnp.bfloat16

epsilon = 1e-06


def norm_parts(values):
    average = jnp.mean(values, axis=-1, keepdims=True)
    centred = values - average
    inverse = lax.rsqrt(jnp.mean(centred * centred, axis=-1, keepdims=True) + epsilon)
    return (centred * inverse, inverse)


def norm_back(inner_grad, normed, inverse):
    first_mean = jnp.mean(inner_grad, axis=-1, keepdims=True)
    second_mean = jnp.mean(inner_grad * normed, axis=-1, keepdims=True)
    return inverse * (inner_grad - first_mean - normed * second_mean)


def gelu_parts(pre_act):
    normal_cdf = 0.5 * (1.0 + lax.erf(pre_act * 0.7071067811865476))
    density = jnp.exp(-0.5 * pre_act * pre_act) * 0.3989422804014327
    return (pre_act * normal_cdf, normal_cdf + pre_act * density)


def dot(a, b, dims, out=F32):
    return lax.dot_general(a, b, (dims, ((), ())), preferred_element_type=out)


def nn(a, b):
    return dot(a, b, ((1,), (0,)))


def nt(a, b):
    return dot(a, b, ((1,), (1,)))


def tn(a, b):
    return dot(a, b, ((0,), (0,)))


def exact(a, b):
    return lax.dot_general(
        a,
        b,
        (((1,), (0,)), ((), ())),
        precision=lax.Precision.HIGHEST,
        preferred_element_type=F32,
    )


def swap(x):
    return lax.ppermute(x, "tensor", [(0, 1), (1, 0)])


def across(x, bit, count):
    return lax.ppermute(x, "dp", [(i, i ^ bit) for i in range(count)])


def in_order(plane, mine, other, axis):
    first = jnp.where(plane == 0, mine, other)
    second = jnp.where(plane == 0, other, mine)
    return jnp.concatenate([first, second], axis=axis)


def half_of(plane, x, which):
    width = x.shape[-1] // 2
    low, high = x[..., :width], x[..., width:]
    return jnp.where((plane == which), low, high)


def keep_half(total, came):
    middle = total.shape[0] // 2
    return total[:middle] + came.astype(F32)


def expert_kernel(
    capacity, slots, own_ref, arrived_ref, cot_ref, other_ref, router_ref, in_ref, bias_ref, out_ref,
    activ_ref, slope_ref, grad_rows_ref, row_ref, out_rows_ref, bias_grad_ref, gate_ref, row_sum, out_sum,
):
    step = pl.program_id(0)
    count = arrived_ref.shape[0]
    experts = router_ref.shape[1]

    @pl.when(step == 0)
    def _():
        logits = nn(arrived_ref[...], router_ref[...])
        ids = lax.broadcasted_iota(jnp.int32, (count, experts), 1)
        own = jnp.sum(jnp.where(ids == own_ref[0], logits, 0.0), axis=1, keepdims=True)
        other = jnp.sum(jnp.where(ids.astype(F32) == other_ref[...], logits, 0.0), axis=1, keepdims=True)
        top = jnp.maximum(own, other)
        own, other = jnp.exp(own - top), jnp.exp(other - top)
        spot = lax.broadcasted_iota(jnp.int32, (count, 1), 0) % slots
        gate = jnp.where(spot < capacity, own / (own + other), 0.0)
        gate_ref[...] = jnp.broadcast_to(gate, gate_ref.shape)
        grad_rows_ref[...] = (gate * cot_ref[...].astype(F32)).astype(BF16)
        row_sum[...] = jnp.zeros_like(row_sum)
        out_sum[...] = jnp.zeros_like(out_sum)

    pre_act = nn(arrived_ref[...], in_ref[...]) + bias_ref[...]
    activ, slope = gelu_parts(pre_act)
    activ = activ.astype(BF16)
    activ_ref[...] = activ
    grad = nt(grad_rows_ref[...], out_ref[...]) * slope
    bias_grad_ref[...] = jnp.sum(grad, axis=0, keepdims=True)
    grad = grad.astype(BF16)
    slope_ref[...] = grad
    row_sum[...] += nt(grad, in_ref[...])
    out_sum[...] += nn(activ, out_ref[...])

    @pl.when(step == pl.num_programs(0) - 1)
    def _():
        inner = jnp.sum(cot_ref[...].astype(F32) * out_sum[...], axis=1, keepdims=True)
        inner = jnp.broadcast_to(inner, gate_ref.shape).T
        out_rows_ref[...] = (gate_ref[:, :1] * out_sum[...]).astype(BF16)
        spot = lax.broadcasted_iota(jnp.int32, (slots, 128), 0)
        row_ref[...] = row_sum[...].astype(BF16)
        for source in range(count // slots):
            first = source * slots
            line = inner[:1, first : first + slots]
            line = jnp.concatenate([line, jnp.zeros((1, 128 - slots), F32)], axis=1)
            high = line.astype(BF16).astype(F32)
            tail = row_sum[first + slots - 16 : first + slots, :128]
            place = lax.broadcasted_iota(jnp.int32, tail.shape, 0)
            tail = jnp.where(place == 15, high, jnp.where(place == 14, line - high, tail))
            row_ref[first + slots - 16 : first + slots, :128] = tail.astype(BF16)


def expert_rows(own, arrived, cot_rows, other, router, in_weight, in_bias, out_weight, capacity, slots):
    count, feat_dim = arrived.shape
    hidden = in_weight.shape[1]
    block = 512 if hidden % 512 == 0 else hidden
    whole = lambda shape: pl.BlockSpec(shape, lambda i: (0, 0))
    return pl.pallas_call(
        lambda *refs: expert_kernel(capacity, slots, *refs),
        grid=(hidden // block,),
        in_specs=[
            pl.BlockSpec(memory_space=pltpu.SMEM),
            whole((count, feat_dim)),
            whole((count, feat_dim)),
            whole((count, 1)),
            whole(router.shape),
            pl.BlockSpec((feat_dim, block), lambda i: (0, i)),
            pl.BlockSpec((1, block), lambda i: (0, i)),
            pl.BlockSpec((block, feat_dim), lambda i: (i, 0)),
        ],
        out_specs=[
            pl.BlockSpec((count, block), lambda i: (0, i)),
            pl.BlockSpec((count, block), lambda i: (0, i)),
            whole((count, feat_dim)),
            whole((count, feat_dim)),
            whole((count, feat_dim)),
            pl.BlockSpec((1, block), lambda i: (0, i)),
        ],
        out_shape=(
            jax.ShapeDtypeStruct((count, hidden), BF16),
            jax.ShapeDtypeStruct((count, hidden), BF16),
            jax.ShapeDtypeStruct((count, feat_dim), BF16),
            jax.ShapeDtypeStruct((count, feat_dim), BF16),
            jax.ShapeDtypeStruct((count, feat_dim), BF16),
            jax.ShapeDtypeStruct((1, hidden), F32),
        ),
        scratch_shapes=[
            pltpu.VMEM((count, 128), F32),
            pltpu.VMEM((count, feat_dim), F32),
            pltpu.VMEM((count, feat_dim), F32),
        ],
        compiler_params=pltpu.CompilerParams(vmem_limit_bytes=60 << 20),
        cost_estimate=pl.CostEstimate(
            flops=8 * count * feat_dim * hidden, bytes_accessed=12 << 20, transcendentals=2 * count * hidden
        ),
        name="expert_rows",
    )(own[None], arrived, cot_rows, other, router, in_weight, in_bias, out_weight)


def expert_rows_plain(own, arrived, cot_rows, other, router, in_weight, in_bias, out_weight, capacity, slots):
    count, feat_dim = arrived.shape
    logits = nn(arrived, router)
    ids = jnp.arange(router.shape[1], dtype=jnp.int32)[None, :]
    own = jnp.sum(jnp.where(ids == own, logits, 0.0), axis=1, keepdims=True)
    other = jnp.sum(jnp.where(ids.astype(F32) == other, logits, 0.0), axis=1, keepdims=True)
    top = jnp.maximum(own, other)
    own, other = jnp.exp(own - top), jnp.exp(other - top)
    spot = jnp.arange(count, dtype=jnp.int32)[:, None] % slots
    gate = jnp.where(spot < capacity, own / (own + other), 0.0)
    grad_rows = (gate * cot_rows.astype(F32)).astype(BF16)
    activ, slope = gelu_parts(nn(arrived, in_weight) + in_bias)
    activ = activ.astype(BF16)
    grad = nt(grad_rows, out_weight) * slope
    bias_grad = jnp.sum(grad, axis=0, keepdims=True)
    grad = grad.astype(BF16)
    part_out = nn(activ, out_weight)
    inner = jnp.sum(cot_rows.astype(F32) * part_out, axis=1).reshape(-1, slots)
    high, low = high_low(jnp.pad(inner, ((0, 0), (0, feat_dim - slots)))[:, None, :])
    rows = nt(grad, in_weight).astype(BF16).reshape(-1, slots, feat_dim)
    rows = jnp.concatenate([rows[:, : slots - 2], low, high], axis=1).reshape(count, feat_dim)
    return activ, grad, grad_rows, rows, (gate * part_out).astype(BF16), bias_grad


def home_kernel(back_ref, onehot_ref, facts_ref, home_ref, inner_ref):
    experts, slots, feat_dim = back_ref.shape
    tok_count = facts_ref.shape[0]
    home = nn(onehot_ref[...], back_ref[...].reshape(experts * slots, feat_dim))
    home_ref[:tok_count, :] = home.astype(BF16)
    for e in range(experts):
        inner_ref[0, e : e + 1, :] = back_ref[e, slots - 1 : slots, :slots].astype(F32)
        inner_ref[1, e : e + 1, :] = back_ref[e, slots - 2 : slots - 1, :slots].astype(F32)
    expert_ids = lax.broadcasted_iota(jnp.int32, (tok_count, experts), 1).astype(F32)
    slot_ids = lax.broadcasted_iota(jnp.int32, (tok_count, slots), 1).astype(F32)
    lanes = lax.broadcasted_iota(jnp.int32, (tok_count, 128), 1)
    table = jnp.zeros((tok_count, 128), F32)
    for k in range(2):
        hot = jnp.where(facts_ref[:, k : k + 1] == expert_ids, 1.0, 0.0).astype(BF16)
        found = nn(hot, inner_ref[0].astype(BF16)) + nn(hot, inner_ref[1].astype(BF16))
        found = jnp.where(facts_ref[:, k + 2 : k + 3] == slot_ids, found, 0.0)
        found = jnp.sum(found, axis=1, keepdims=True)
        high = found.astype(BF16).astype(F32)
        table = jnp.where(lanes == 2 * k, high, jnp.where(lanes == 2 * k + 1, found - high, table))
    home_ref[tok_count + 3 : tok_count + 11, :tok_count] = table.T[:8, :].astype(BF16)


def home_rows(back, onehot, facts):
    experts, slots, feat_dim = back.shape
    tok_count = facts.shape[0]
    return pl.pallas_call(
        home_kernel,
        out_shape=jax.ShapeDtypeStruct((tok_count + 11, feat_dim), BF16),
        scratch_shapes=[pltpu.VMEM((2, experts, slots), F32)],
        compiler_params=pltpu.CompilerParams(vmem_limit_bytes=16 << 20),
        cost_estimate=pl.CostEstimate(
            flops=2 * tok_count * feat_dim * experts * slots, bytes_accessed=2 << 20, transcendentals=0
        ),
        name="home_rows",
    )(back, onehot, facts)


def attention_grads_kernel(
    home_ref, other_ref, router_ref, cot_ref, normed_ref, facts_ref, gain_ref, hidden2_ref, bias_grad_ref,
    proj_ref, projected_ref, attended_ref, hidden_ref, weight_ref, mix_ref,
    sent_ref, kept_ref, hidden_part_ref, sums_ref, middle_grad_ref, low_ref, back_ref, small_ref, logit_ref,
):
    head_cols = attended_ref.shape[1]
    experts = router_ref.shape[1]
    tok_count = cot_ref.shape[0]
    scale = HEAD ** (-0.5)
    lines = slice(tok_count + 3, tok_count + 11)
    inner = home_ref[lines, :tok_count].astype(F32) + other_ref[lines, :tok_count].astype(F32)
    inner = inner.T
    bias_dot = facts_ref[:, 16 : 16 + experts]
    expert_ids = lax.broadcasted_iota(jnp.int32, (tok_count, experts), 1).astype(F32)
    picks = [facts_ref[:, k : k + 1] == expert_ids for k in range(2)]
    gates = [facts_ref[:, k + 4 : k + 5] for k in range(2)]
    inner_grads = []
    for k in range(2):
        own_bias = jnp.sum(jnp.where(picks[k], bias_dot, 0.0), axis=1, keepdims=True)
        inner_grads.append(inner[:, 2 * k : 2 * k + 1] + inner[:, 2 * k + 1 : 2 * k + 2] + own_bias)
    mean = gates[0] * inner_grads[0] + gates[1] * inner_grads[1]
    logit_grad = 0.0
    for k in range(2):
        logit_grad = logit_grad + jnp.where(picks[k], gates[k] * (inner_grads[k] - mean), 0.0)
    logit_ref[...] = logit_grad.astype(BF16)
    hidden_grad = home_ref[:tok_count, :].astype(F32) + other_ref[:tok_count, :].astype(F32)
    hidden_grad = hidden_grad + nt(logit_ref[...], router_ref[...])
    normed = normed_ref[...]
    inner = hidden_grad * gain_ref[...]
    middle_grad = cot_ref[...].astype(F32) + norm_back(inner, normed, facts_ref[:, 6:7])
    middle_grad_ref[...] = middle_grad
    middle_low = middle_grad.astype(BF16)
    small_ref[...] = jnp.zeros_like(small_ref)
    small_ref[:experts, :] = tn(logit_ref[...], hidden2_ref[...])
    small_ref[experts : 2 * experts, :] = bias_grad_ref[...]
    small_ref[2 * experts : 2 * experts + 1, :] = jnp.sum(hidden_grad * normed, axis=0, keepdims=True)
    small_ref[2 * experts + 1 : 2 * experts + 2, :] = jnp.sum(hidden_grad, axis=0, keepdims=True)
    small_ref[2 * experts + 2 : 2 * experts + 3, :] = jnp.sum(middle_grad, axis=0, keepdims=True)
    back_ref[...] = nt(middle_low, proj_ref[...]).astype(BF16)
    for h in range(head_cols // HEAD):
        cols = slice(h * HEAD, (h + 1) * HEAD)
        queries, key_vals, values_in = (projected_ref[j, :, cols] for j in range(3))
        out_grad = back_ref[:, cols]
        prob_vals = jnp.exp(nt(queries, key_vals) * scale - facts_ref[:, h + 8 : h + 9])
        prob_low = prob_vals.astype(BF16)
        prob_grad = nt(out_grad, values_in)
        row = jnp.sum(prob_vals * prob_grad, axis=-1, keepdims=True)
        score_low = (prob_vals * (prob_grad - row)).astype(BF16)
        low_ref[:, h * HEAD : (h + 1) * HEAD] = (nn(score_low, key_vals) * scale).astype(BF16)
        start = head_cols + h * HEAD
        low_ref[:, start : start + HEAD] = (tn(score_low, queries) * scale).astype(BF16)
        start = start + head_cols
        low_ref[:, start : start + HEAD] = tn(prob_low, out_grad).astype(BF16)
    low = low_ref[...]
    half = kept_ref.shape[0]
    mixed_middle = nt(mix_ref[1], middle_low).astype(BF16)
    small = small_ref[...].astype(BF16)
    for part in range(2):
        rows = slice(part * half, (part + 1) * half)
        pieces = (
            nn(hidden_ref[0, rows, :], low[:, : 2 * head_cols]),
            nt(mix_ref[0, rows, :], small),
            nn(hidden_ref[1, rows, :], low[:, 2 * head_cols :]),
            nn(mixed_middle[rows, :], attended_ref[...]),
        )
        first = 0
        for piece in pieces:
            last = first + piece.shape[1]
            if part == 0:
                kept_ref[:, first:last] = piece
            else:
                sent_ref[:, first:last] = piece.astype(BF16)
            first = last
    part = nt(low[:, :head_cols], weight_ref[0])
    part = part + nt(low[:, head_cols : 2 * head_cols], weight_ref[1])
    part = part + nt(low[:, 2 * head_cols :], weight_ref[2])
    hidden_part_ref[...] = part.astype(BF16)
    sums_ref[...] = jnp.sum(low.astype(F32), axis=0, keepdims=True)


def attention_grads(*operands):
    tok_count, feat_dim = operands[3].shape
    experts = operands[2].shape[1]
    head_cols = operands[9].shape[0]
    small = -(-(2 * experts + 3) // 128) * 128
    width = 4 * head_cols + small
    flops = 2 * tok_count * feat_dim * head_cols * 9 + 2 * feat_dim * feat_dim * (tok_count + small)
    return pl.pallas_call(
        attention_grads_kernel,
        out_shape=(
            jax.ShapeDtypeStruct((feat_dim // 2, width), BF16),
            jax.ShapeDtypeStruct((feat_dim // 2, width), F32),
            jax.ShapeDtypeStruct((tok_count, feat_dim), BF16),
            jax.ShapeDtypeStruct((1, 3 * head_cols), F32),
            jax.ShapeDtypeStruct((tok_count, feat_dim), F32),
        ),
        scratch_shapes=[
            pltpu.VMEM((tok_count, 3 * head_cols), BF16),
            pltpu.VMEM((tok_count, head_cols), BF16),
            pltpu.VMEM((small, feat_dim), F32),
            pltpu.VMEM((tok_count, experts), BF16),
        ],
        compiler_params=pltpu.CompilerParams(vmem_limit_bytes=60 << 20),
        cost_estimate=pl.CostEstimate(
            flops=flops, bytes_accessed=10 << 20, transcendentals=tok_count * tok_count * 6
        ),
        name="attention_grads",
    )(*operands)


def finish_kernel(head_cols, experts, orders, me_ref, mine, mine_b, got, got_b, qkv_ref, proj_ref, router_ref, bias_ref, norm_ref, held_proj, held_small):
    me = me_ref[0]
    count = 1 << len(orders[0])
    feat_dim = qkv_ref.shape[1]
    chunk = feat_dim // count
    half = count // 2
    for spot in range(count):
        starts = []
        for order in orders:
            name = sum(bit for i, bit in enumerate(order) if (spot >> (len(order) - 1 - i)) & 1)
            starts.append(pl.ds(pl.multiple_of((name ^ me) * chunk, chunk), chunk))
        source, source_b = (mine, mine_b) if spot < half else (got, got_b)
        first = (spot % half) * chunk
        piece = source[first : first + chunk, :].astype(F32)
        qkv_ref[0, starts[0], :] = piece[:, :head_cols]
        qkv_ref[1, starts[0], :] = piece[:, head_cols : 2 * head_cols]
        held_small[starts[0], :] = piece[:, 2 * head_cols :]
        piece = source_b[first : first + chunk, :].astype(F32)
        qkv_ref[2, starts[1], :] = piece[:, :head_cols]
        held_proj[starts[1], :] = piece[:, head_cols:]
    proj_ref[...] = held_proj[...].T
    small = held_small[...]
    flat = small.T
    router_ref[...] = flat[:experts]
    bias_ref[...] = flat[experts : 2 * experts]
    norm_ref[...] = flat[2 * experts : 2 * experts + 8]


def finish(me, mine, mine_b, came, came_b, head_cols, experts, feat_dim, orders):
    width = mine.shape[1] - 2 * head_cols
    vmem = pl.BlockSpec(memory_space=pltpu.VMEM)
    return pl.pallas_call(
        lambda *refs: finish_kernel(head_cols, experts, orders, *refs),
        in_specs=[pl.BlockSpec(memory_space=pltpu.SMEM)] + [vmem] * 4,
        out_specs=[vmem] * 5,
        out_shape=(
            jax.ShapeDtypeStruct((3, feat_dim, head_cols), F32),
            jax.ShapeDtypeStruct((head_cols, feat_dim), F32),
            jax.ShapeDtypeStruct((experts, feat_dim), F32),
            jax.ShapeDtypeStruct((experts, feat_dim), F32),
            jax.ShapeDtypeStruct((8, feat_dim), F32),
        ),
        scratch_shapes=[
            pltpu.VMEM((feat_dim, head_cols), F32),
            pltpu.VMEM((feat_dim, width), F32),
        ],
        compiler_params=pltpu.CompilerParams(vmem_limit_bytes=40 << 20),
        name="finish",
    )(me[None], mine, mine_b, came, came_b)


def high_low(values):
    high = values.astype(BF16)
    return high, (values - high.astype(F32)).astype(BF16)


def local(
    inputs,
    norm1_gain,
    norm1_bias,
    qkv_weight,
    qv_bias,
    proj_weight,
    proj_bias,
    norm2_gain,
    norm2_bias,
    router,
    expert_in,
    expert_in_bias,
    expert_out,
    expert_out_bias,
    routes,
    cotangent,
):
    tok_count = inputs.shape[0]
    feat_dim = inputs.shape[1]
    half_dim = feat_dim // 2
    head_cols = qkv_weight.shape[2]
    heads_here = head_cols // HEAD
    images = tok_count // SEQ
    experts = router.shape[1]
    sources = lax.axis_size("dp")
    group_size = sources // experts
    capacity = max(2, (10 * tok_count + 3 * experts - 1) // (3 * experts))
    slots = (capacity + 3 + 15) // 16 * 16
    score_scale = HEAD ** (-0.5)
    plane = lax.axis_index("tensor")
    me = lax.axis_index("dp")
    own_expert = me // group_size
    in_weight, out_weight = expert_in[0], expert_out[0]

    expert_ids = jnp.arange(experts, dtype=jnp.int32)
    slot_ids = jnp.arange(slots, dtype=jnp.int32)
    all_ids = jnp.arange(experts * slots, dtype=jnp.int32)
    pick = [(routes[:, k : k + 1] == expert_ids[None, :]) for k in range(2)]
    named = (pick[0] | pick[1]).astype(BF16)
    before = (
        jnp.arange(tok_count)[:, None] > jnp.arange(tok_count)[None, :]
    ).astype(BF16)
    earlier = nn(before, named)
    rank = [
        jnp.sum(jnp.where(pick[k], earlier, 0.0), axis=1, keepdims=True).astype(jnp.int32)
        for k in range(2)
    ]
    place = [routes[:, k : k + 1] * slots + rank[k] for k in range(2)]
    onehot = ((place[0] == all_ids[None, :]) | (place[1] == all_ids[None, :])).astype(BF16)
    rank_hot = [(rank[k] == slot_ids[None, :]) for k in range(2)]
    pick_low = [pick[k].astype(BF16) for k in range(2)]
    partner = [
        jnp.where(rank_hot[k], routes[:, 1 - k : 2 - k].astype(F32), 0.0).astype(BF16)
        for k in range(2)
    ]
    partner_map = tn(pick_low[0], partner[0]) + tn(pick_low[1], partner[1])

    cot_half = half_of(plane, cotangent, 0)
    cot_send = tn(onehot, cot_half).astype(BF16).reshape(experts, slots, half_dim)
    note = jnp.pad(partner_map.astype(BF16), ((0, 0), (0, half_dim - slots)))[:, None, :]
    cot_send = jnp.where(slot_ids[None, :, None] == slots - 1, note, cot_send)
    cot_send = jnp.repeat(cot_send, group_size, axis=0)
    proj_other = swap(proj_weight)
    proj_full = in_order(plane, proj_weight, proj_other, 0)

    inputs, cot_send = lax.optimization_barrier((inputs, cot_send))
    cot_mine = lax.all_to_all(cot_send, "dp", split_axis=0, concat_axis=0, tiled=True)
    x_in = inputs.astype(F32)
    normed1, inverse1 = norm_parts(x_in)
    hidden1 = (normed1 * norm1_gain + norm1_bias).astype(BF16)
    projected = jnp.einsum("td,jde->jte", hidden1, qkv_weight, preferred_element_type=F32)
    bias_rows = jnp.stack([qv_bias[0], jnp.zeros_like(qv_bias[0]), qv_bias[1]])
    projected = (projected + bias_rows[:, None, :]).astype(BF16)
    projected, proj_full = lax.optimization_barrier((projected, proj_full))
    heads_view = projected.reshape(3, images, SEQ, heads_here, HEAD)
    queries, key_vals, values_in = (heads_view[0], heads_view[1], heads_view[2])
    scores = (
        jnp.einsum("bqhd,bkhd->bhqk", queries, key_vals, preferred_element_type=F32)
        * score_scale
    )
    row_max = jnp.max(scores, axis=-1, keepdims=True)
    exp_scores = jnp.exp(scores - row_max)
    row_total = jnp.sum(exp_scores, axis=-1, keepdims=True)
    lse = (row_max + jnp.log(row_total)).reshape(heads_here, tok_count).T
    prob_low = (exp_scores / row_total).astype(BF16)
    attended = jnp.einsum("bhqk,bkhd->bqhd", prob_low, values_in, preferred_element_type=F32)
    attended = attended.reshape(tok_count, head_cols).astype(BF16)
    attended_all = in_order(plane, attended, swap(attended), 1)
    attended_all, cot_mine = lax.optimization_barrier((attended_all, cot_mine))
    cot_other = swap(cot_mine)
    middle = x_in + nn(attended_all, proj_full) + proj_bias
    normed2, inverse2 = norm_parts(middle)
    hidden2 = (normed2 * norm2_gain + norm2_bias).astype(BF16)

    send = tn(onehot, hidden2).astype(BF16).reshape(experts, slots, feat_dim)
    send = jnp.repeat(send, group_size, axis=0)
    arrived = lax.all_to_all(send, "dp", split_axis=0, concat_axis=0, tiled=True)
    arrived = arrived.reshape(-1, feat_dim)

    logits = nn(hidden2, router)
    chosen = [jnp.sum(jnp.where(pick[k], logits, 0.0), axis=1, keepdims=True) for k in range(2)]
    chosen_max = jnp.maximum(chosen[0], chosen[1])
    chosen_exp = [jnp.exp(chosen[k] - chosen_max) for k in range(2)]
    chosen_sum = chosen_exp[0] + chosen_exp[1]
    gate_vals = [chosen_exp[k] / chosen_sum for k in range(2)]
    gate_map = jnp.where(pick[0], gate_vals[0], 0.0) + jnp.where(pick[1], gate_vals[1], 0.0)
    grad_out = cotangent.astype(F32)
    row_grad = [(gate_vals[k] * grad_out).astype(BF16) for k in range(2)]
    out_bias_grad = tn(pick_low[0], row_grad[0]) + tn(pick_low[1], row_grad[1])

    other_expert = cot_mine[:, slots - 1, :slots].reshape(-1, 1).astype(F32)
    cot_rows = in_order(plane, cot_mine, cot_other, 2).reshape(-1, feat_dim)
    bits = [1 << i for i in range(sources.bit_length() - 1)]
    orders = [bits, bits[:1] + bits[2:] + bits[1:2]]
    chunk = feat_dim // sources

    rows = jnp.arange(feat_dim, dtype=jnp.int32)[None, :]
    cols = jnp.arange(feat_dim, dtype=jnp.int32)[:, None]
    spot = cols // chunk
    mix_t = []
    for order in orders:
        piece = jnp.zeros_like(spot)
        for i, bit in enumerate(order):
            piece = piece | jnp.where((spot >> (len(bits) - 1 - i)) & 1 == 1, bit, 0)
        mix_t.append(
            ((rows // chunk == (piece ^ me)) & (rows % chunk == cols % chunk)).astype(BF16)
        )
    mix_t = jnp.stack(mix_t)
    hidden1_t = jnp.einsum("jqd,td->jqt", mix_t, hidden1, preferred_element_type=F32).astype(BF16)
    bias_dot = lax.dot_general(
        grad_out,
        expert_out_bias,
        (((1,), (1,)), ((), ())),
        precision=lax.Precision.HIGHEST,
        preferred_element_type=F32,
    )
    facts = [routes.astype(F32)] + [r.astype(F32) for r in rank] + gate_vals + [inverse2]
    facts = jnp.concatenate(facts, axis=1)
    facts = jnp.concatenate([facts, jnp.zeros_like(facts[:, :1]), lse], axis=1)
    facts = jnp.pad(facts, ((0, 0), (0, 16 - facts.shape[1])))
    facts = jnp.pad(jnp.concatenate([facts, bias_dot], axis=1), ((0, 0), (0, 112 - experts)))
    ready = (
        mix_t, hidden1_t, facts, onehot, out_bias_grad, normed2, hidden2, projected, attended, gate_map,
        cot_rows,
    )
    arrived, ready = lax.optimization_barrier((arrived, ready))
    (
        mix_t, hidden1_t, facts, onehot, out_bias_grad, normed2, hidden2, projected, attended, gate_map,
        cot_rows,
    ) = ready
    activ_low, act_low, grad_rows, row_send, out_send, in_bias_grad = (
        expert_rows if sources * slots <= 1024 else expert_rows_plain
    )(
        own_expert, arrived, cot_rows, other_expert, router, in_weight, expert_in_bias, out_weight, capacity, slots
    )
    row_send = row_send.reshape(sources, slots, feat_dim)
    row_back = lax.all_to_all(row_send, "dp", split_axis=0, concat_axis=0, tiled=True)
    out_weight_grad = tn(activ_low, grad_rows)
    in_weight_grad = tn(arrived, act_low)
    out_send, out_weight_grad, in_weight_grad = lax.optimization_barrier(
        (out_send, out_weight_grad, in_weight_grad)
    )
    def over_group(x):
        if group_size == 1:
            return x
        shape = (experts, group_size) + x.shape[1:]
        return jnp.sum(x.reshape(shape).astype(F32), axis=1).astype(BF16)

    row_home = home_rows(
        over_group(row_back),
        onehot,
        facts,
    )
    out_send = out_send.reshape(sources, slots, feat_dim)
    row_other = swap(row_home)
    out_back = lax.all_to_all(out_send, "dp", split_axis=0, concat_axis=0, tiled=True)

    sent, kept, hidden1_part, qv_sums, middle_grad = attention_grads(
        row_home,
        row_other,
        router,
        cotangent,
        normed2,
        facts,
        norm2_gain[None],
        hidden2,
        out_bias_grad,
        proj_weight,
        projected,
        attended,
        hidden1_t,
        qkv_weight,
        mix_t,
    )
    hidden1_other = swap(hidden1_part)
    split = sent.shape[1] - 2 * head_cols
    sent, out_back = lax.optimization_barrier((sent, out_back))
    came = across(sent, bits[0], sources)
    total = kept + came.astype(F32)
    totals = [total[:, :split], total[:, split:]]
    out_home = nn(onehot, over_group(out_back).reshape(-1, feat_dim)).astype(BF16)
    for turn in range(1, len(bits)):
        totals, out_home = lax.optimization_barrier((totals, out_home))
        if turn == len(bits) - 1:
            out_other = swap(out_home)
        if turn == 2:
            totals, hidden1_other = lax.optimization_barrier((totals, hidden1_other))
        sends = lax.optimization_barrier([t[t.shape[0] // 2 :].astype(BF16) for t in totals])
        cames = [across(t, order[turn], sources) for t, order in zip(sends, orders)]
        totals = [keep_half(t, c) for t, c in zip(totals, cames)]
    hidden1_grad = hidden1_part.astype(F32) + hidden1_other.astype(F32)
    norm1_gain_grad = jnp.sum(hidden1_grad * normed1, axis=0)
    norm1_bias_grad = jnp.sum(hidden1_grad, axis=0)
    input_grad = middle_grad + norm_back(hidden1_grad * norm1_gain, normed1, inverse1)
    bias_home = exact(gate_map, expert_out_bias)
    mine = [t.astype(BF16) for t in totals]
    late = jnp.stack(
        [
            norm1_gain_grad,
            norm1_bias_grad,
            jnp.concatenate([qv_sums[0, :head_cols], qv_sums[0, 2 * head_cols :]]),
        ]
    )
    late = jnp.pad(late, ((0, 5), (0, 0)))

    def late_rows(late):
        high, low = high_low(late)
        both = jnp.pad(jnp.concatenate([high, low], axis=0), ((0, 0), (0, split - feat_dim)))
        return high.astype(F32) + low.astype(F32), both

    def late_sum(own, came):
        came = came[:, :feat_dim].astype(F32)
        return own + (came[:8] + came[8:])

    size = chunk
    for turn in range(len(bits) - 1, 0, -1):
        own, both = late_rows(late)
        first, second = jnp.concatenate([mine[0], both], axis=0), mine[1]
        if turn == 1:
            first, second, out_other = lax.optimization_barrier((first, second, out_other))
        else:
            first, second = lax.optimization_barrier((first, second))
        came = across(first, orders[0][turn], sources)
        came_b = across(second, orders[1][turn], sources)
        late = late_sum(own, came[size:])
        mine = [
            jnp.concatenate([mine[0], came[:size]], axis=0),
            jnp.concatenate([mine[1], came_b], axis=0),
        ]
        size = 2 * size
    out_home = out_home.astype(F32) + out_other.astype(F32)
    output = (middle + (out_home + bias_home)).astype(BF16)
    own, both = late_rows(late)
    first, second, input_grad, output = lax.optimization_barrier(
        (jnp.concatenate([mine[0], both], axis=0), mine[1], input_grad, output)
    )
    came = across(first, bits[0], sources)
    came_b = across(second, bits[0], sources)
    late = late_sum(own, came[size:])
    qv_bias_grad = late[2].reshape(2, head_cols)
    if chunk % 16 == 0:
        qkv_grad, proj_grad, router_grad, out_bias_grad, norm_grads = finish(
            me, first, second, came, came_b, head_cols, experts, feat_dim, orders
        )
        router_grad = router_grad.T
    else:
        first = tn(mix_t[0], jnp.concatenate([mine[0], came[:size]], axis=0))
        second = tn(mix_t[1], jnp.concatenate([mine[1], came_b], axis=0))
        qkv_grad = jnp.stack(
            [first[:, :head_cols], first[:, head_cols : 2 * head_cols], second[:, :head_cols]]
        )
        proj_grad = second[:, head_cols:].T
        router_grad = first[:, 2 * head_cols : 2 * head_cols + experts]
        norm_grads = first[:, 2 * head_cols + experts :].T
        out_bias_grad, norm_grads = norm_grads[:experts], norm_grads[experts:]
    norm2_gain_grad, norm2_bias_grad, proj_bias_grad = norm_grads[0], norm_grads[1], norm_grads[2]
    return (
        output,
        input_grad,
        late[0],
        late[1],
        qkv_grad,
        qv_bias_grad,
        proj_grad,
        proj_bias_grad,
        norm2_gain_grad,
        norm2_bias_grad,
        router_grad,
        in_weight_grad[None],
        in_bias_grad,
        out_weight_grad[None],
        out_bias_grad,
    )


def solution(mesh):
    return jax.shard_map(
        local,
        mesh=mesh,
        in_specs=(
            P("dp", None),
            P(),
            P(),
            P(None, None, "tensor"),
            P(None, "tensor"),
            P("tensor", None),
            P(),
            P(),
            P(),
            P(),
            P("dp", None, "tensor"),
            P("dp", "tensor"),
            P("dp", "tensor", None),
            P(),
            P("dp", None),
            P("dp", None),
        ),
        out_specs=(
            P("dp", None),
            P("dp", None),
            P(),
            P(),
            P(None, None, "tensor"),
            P(None, "tensor"),
            P("tensor", None),
            P(),
            P(),
            P(),
            P(),
            P("dp", None, "tensor"),
            P("dp", "tensor"),
            P("dp", "tensor", None),
            P(),
        ),
        check_vma=False,
    )
```

```python
import jax
import jax.numpy as jnp
from jax import lax
from jax.experimental import pallas as pl
from jax.experimental.pallas import tpu as pltpu
from jax.sharding import PartitionSpec as P

HEAD = 64
SEQ = 197
F32 = jnp.float32
BF16 = jnp.bfloat16

epsilon = 1e-06


def norm_parts(values):
    average = jnp.mean(values, axis=-1, keepdims=True)
    centred = values - average
    inverse = lax.rsqrt(jnp.mean(centred * centred, axis=-1, keepdims=True) + epsilon)
    return (centred * inverse, inverse)


def norm_back(inner_grad, normed, inverse):
    first_mean = jnp.mean(inner_grad, axis=-1, keepdims=True)
    second_mean = jnp.mean(inner_grad * normed, axis=-1, keepdims=True)
    return inverse * (inner_grad - first_mean - normed * second_mean)


def gelu_parts(pre_act):
    normal_cdf = 0.5 * (1.0 + lax.erf(pre_act * 0.7071067811865476))
    density = jnp.exp(-0.5 * pre_act * pre_act) * 0.3989422804014327
    return (pre_act * normal_cdf, normal_cdf + pre_act * density)


def dot(a, b, dims, out=F32):
    return lax.dot_general(a, b, (dims, ((), ())), preferred_element_type=out)


def nn(a, b):
    return dot(a, b, ((1,), (0,)))


def nt(a, b):
    return dot(a, b, ((1,), (1,)))


def tn(a, b):
    return dot(a, b, ((0,), (0,)))


def exact(a, b):
    return lax.dot_general(
        a,
        b,
        (((1,), (0,)), ((), ())),
        precision=lax.Precision.HIGHEST,
        preferred_element_type=F32,
    )


def swap(x):
    return lax.ppermute(x, "tensor", [(0, 1), (1, 0)])


def across(x, bit, count):
    return lax.ppermute(x, "dp", [(i, i ^ bit) for i in range(count)])


def in_order(plane, mine, other, axis):
    first = jnp.where(plane == 0, mine, other)
    second = jnp.where(plane == 0, other, mine)
    return jnp.concatenate([first, second], axis=axis)


def half_of(plane, x, which):
    width = x.shape[-1] // 2
    low, high = x[..., :width], x[..., width:]
    return jnp.where((plane == which), low, high)


def keep_half(total, came):
    middle = total.shape[0] // 2
    return total[:middle] + came.astype(F32)


def expert_kernel(
    capacity, slots, own_ref, arrived_ref, cot_ref, other_ref, router_ref, in_ref, bias_ref, out_ref,
    activ_ref, slope_ref, grad_rows_ref, row_ref, out_rows_ref, bias_grad_ref, gate_ref, row_sum, out_sum,
):
    step = pl.program_id(0)
    count = arrived_ref.shape[0]
    experts = router_ref.shape[1]

    @pl.when(step == 0)
    def _():
        logits = nn(arrived_ref[...], router_ref[...])
        ids = lax.broadcasted_iota(jnp.int32, (count, experts), 1)
        own = jnp.sum(jnp.where(ids == own_ref[0], logits, 0.0), axis=1, keepdims=True)
        other = jnp.sum(jnp.where(ids.astype(F32) == other_ref[...], logits, 0.0), axis=1, keepdims=True)
        top = jnp.maximum(own, other)
        own, other = jnp.exp(own - top), jnp.exp(other - top)
        spot = lax.broadcasted_iota(jnp.int32, (count, 1), 0) % slots
        gate = jnp.where(spot < capacity, own / (own + other), 0.0)
        gate_ref[...] = jnp.broadcast_to(gate, gate_ref.shape)
        grad_rows_ref[...] = (gate * cot_ref[...].astype(F32)).astype(BF16)
        row_sum[...] = jnp.zeros_like(row_sum)
        out_sum[...] = jnp.zeros_like(out_sum)

    pre_act = nn(arrived_ref[...], in_ref[...]) + bias_ref[...]
    activ, slope = gelu_parts(pre_act)
    activ = activ.astype(BF16)
    activ_ref[...] = activ
    grad = nt(grad_rows_ref[...], out_ref[...]) * slope
    bias_grad_ref[...] = jnp.sum(grad, axis=0, keepdims=True)
    grad = grad.astype(BF16)
    slope_ref[...] = grad
    row_sum[...] += nt(grad, in_ref[...])
    out_sum[...] += nn(activ, out_ref[...])

    @pl.when(step == pl.num_programs(0) - 1)
    def _():
        inner = jnp.sum(cot_ref[...].astype(F32) * out_sum[...], axis=1, keepdims=True)
        inner = jnp.broadcast_to(inner, gate_ref.shape).T
        out_rows_ref[...] = (gate_ref[:, :1] * out_sum[...]).astype(BF16)
        spot = lax.broadcasted_iota(jnp.int32, (slots, 128), 0)
        row_ref[...] = row_sum[...].astype(BF16)
        for source in range(count // slots):
            first = source * slots
            line = inner[:1, first : first + slots]
            line = jnp.concatenate([line, jnp.zeros((1, 128 - slots), F32)], axis=1)
            high = line.astype(BF16).astype(F32)
            tail = row_sum[first + slots - 16 : first + slots, :128]
            place = lax.broadcasted_iota(jnp.int32, tail.shape, 0)
            tail = jnp.where(place == 15, high, jnp.where(place == 14, line - high, tail))
            row_ref[first + slots - 16 : first + slots, :128] = tail.astype(BF16)


def expert_rows(own, arrived, cot_rows, other, router, in_weight, in_bias, out_weight, capacity, slots):
    count, feat_dim = arrived.shape
    hidden = in_weight.shape[1]
    block = 512 if hidden % 512 == 0 else hidden
    whole = lambda shape: pl.BlockSpec(shape, lambda i: (0, 0))
    return pl.pallas_call(
        lambda *refs: expert_kernel(capacity, slots, *refs),
        grid=(hidden // block,),
        in_specs=[
            pl.BlockSpec(memory_space=pltpu.SMEM),
            whole((count, feat_dim)),
            whole((count, feat_dim)),
            whole((count, 1)),
            whole(router.shape),
            pl.BlockSpec((feat_dim, block), lambda i: (0, i)),
            pl.BlockSpec((1, block), lambda i: (0, i)),
            pl.BlockSpec((block, feat_dim), lambda i: (i, 0)),
        ],
        out_specs=[
            pl.BlockSpec((count, block), lambda i: (0, i)),
            pl.BlockSpec((count, block), lambda i: (0, i)),
            whole((count, feat_dim)),
            whole((count, feat_dim)),
            whole((count, feat_dim)),
            pl.BlockSpec((1, block), lambda i: (0, i)),
        ],
        out_shape=(
            jax.ShapeDtypeStruct((count, hidden), BF16),
            jax.ShapeDtypeStruct((count, hidden), BF16),
            jax.ShapeDtypeStruct((count, feat_dim), BF16),
            jax.ShapeDtypeStruct((count, feat_dim), BF16),
            jax.ShapeDtypeStruct((count, feat_dim), BF16),
            jax.ShapeDtypeStruct((1, hidden), F32),
        ),
        scratch_shapes=[
            pltpu.VMEM((count, 128), F32),
            pltpu.VMEM((count, feat_dim), F32),
            pltpu.VMEM((count, feat_dim), F32),
        ],
        compiler_params=pltpu.CompilerParams(vmem_limit_bytes=60 << 20),
        cost_estimate=pl.CostEstimate(
            flops=8 * count * feat_dim * hidden, bytes_accessed=12 << 20, transcendentals=2 * count * hidden
        ),
        name="expert_rows",
    )(own[None], arrived, cot_rows, other, router, in_weight, in_bias, out_weight)


def expert_rows_plain(own, arrived, cot_rows, other, router, in_weight, in_bias, out_weight, capacity, slots):
    count, feat_dim = arrived.shape
    logits = nn(arrived, router)
    ids = jnp.arange(router.shape[1], dtype=jnp.int32)[None, :]
    own = jnp.sum(jnp.where(ids == own, logits, 0.0), axis=1, keepdims=True)
    other = jnp.sum(jnp.where(ids.astype(F32) == other, logits, 0.0), axis=1, keepdims=True)
    top = jnp.maximum(own, other)
    own, other = jnp.exp(own - top), jnp.exp(other - top)
    spot = jnp.arange(count, dtype=jnp.int32)[:, None] % slots
    gate = jnp.where(spot < capacity, own / (own + other), 0.0)
    grad_rows = (gate * cot_rows.astype(F32)).astype(BF16)
    activ, slope = gelu_parts(nn(arrived, in_weight) + in_bias)
    activ = activ.astype(BF16)
    grad = nt(grad_rows, out_weight) * slope
    bias_grad = jnp.sum(grad, axis=0, keepdims=True)
    grad = grad.astype(BF16)
    part_out = nn(activ, out_weight)
    inner = jnp.sum(cot_rows.astype(F32) * part_out, axis=1).reshape(-1, slots)
    high, low = high_low(jnp.pad(inner, ((0, 0), (0, feat_dim - slots)))[:, None, :])
    rows = nt(grad, in_weight).astype(BF16).reshape(-1, slots, feat_dim)
    rows = jnp.concatenate([rows[:, : slots - 2], low, high], axis=1).reshape(count, feat_dim)
    return activ, grad, grad_rows, rows, (gate * part_out).astype(BF16), bias_grad


def home_kernel(back_ref, onehot_ref, facts_ref, home_ref, inner_ref):
    experts, slots, feat_dim = back_ref.shape
    tok_count = facts_ref.shape[0]
    home = nn(onehot_ref[...], back_ref[...].reshape(experts * slots, feat_dim))
    home_ref[:tok_count, :] = home.astype(BF16)
    for e in range(experts):
        inner_ref[0, e : e + 1, :] = back_ref[e, slots - 1 : slots, :slots].astype(F32)
        inner_ref[1, e : e + 1, :] = back_ref[e, slots - 2 : slots - 1, :slots].astype(F32)
    expert_ids = lax.broadcasted_iota(jnp.int32, (tok_count, experts), 1).astype(F32)
    slot_ids = lax.broadcasted_iota(jnp.int32, (tok_count, slots), 1).astype(F32)
    lanes = lax.broadcasted_iota(jnp.int32, (tok_count, 128), 1)
    table = jnp.zeros((tok_count, 128), F32)
    for k in range(2):
        hot = jnp.where(facts_ref[:, k : k + 1] == expert_ids, 1.0, 0.0).astype(BF16)
        found = nn(hot, inner_ref[0].astype(BF16)) + nn(hot, inner_ref[1].astype(BF16))
        found = jnp.where(facts_ref[:, k + 2 : k + 3] == slot_ids, found, 0.0)
        found = jnp.sum(found, axis=1, keepdims=True)
        high = found.astype(BF16).astype(F32)
        table = jnp.where(lanes == 2 * k, high, jnp.where(lanes == 2 * k + 1, found - high, table))
    home_ref[tok_count + 3 : tok_count + 11, :tok_count] = table.T[:8, :].astype(BF16)


def home_rows(back, onehot, facts):
    experts, slots, feat_dim = back.shape
    tok_count = facts.shape[0]
    return pl.pallas_call(
        home_kernel,
        out_shape=jax.ShapeDtypeStruct((tok_count + 11, feat_dim), BF16),
        scratch_shapes=[pltpu.VMEM((2, experts, slots), F32)],
        compiler_params=pltpu.CompilerParams(vmem_limit_bytes=16 << 20),
        cost_estimate=pl.CostEstimate(
            flops=2 * tok_count * feat_dim * experts * slots, bytes_accessed=2 << 20, transcendentals=0
        ),
        name="home_rows",
    )(back, onehot, facts)


def attention_grads_kernel(
    home_ref, other_ref, router_ref, cot_ref, normed_ref, facts_ref, gain_ref, hidden2_ref, bias_grad_ref,
    proj_ref, projected_ref, attended_ref, hidden_ref, weight_ref, mix_ref,
    sent_ref, kept_ref, hidden_part_ref, sums_ref, middle_grad_ref, low_ref, back_ref, small_ref, logit_ref,
):
    head_cols = attended_ref.shape[1]
    experts = router_ref.shape[1]
    tok_count = cot_ref.shape[0]
    scale = HEAD ** (-0.5)
    lines = slice(tok_count + 3, tok_count + 11)
    inner = home_ref[lines, :tok_count].astype(F32) + other_ref[lines, :tok_count].astype(F32)
    inner = inner.T
    bias_dot = facts_ref[:, 16 : 16 + experts]
    expert_ids = lax.broadcasted_iota(jnp.int32, (tok_count, experts), 1).astype(F32)
    picks = [facts_ref[:, k : k + 1] == expert_ids for k in range(2)]
    gates = [facts_ref[:, k + 4 : k + 5] for k in range(2)]
    inner_grads = []
    for k in range(2):
        own_bias = jnp.sum(jnp.where(picks[k], bias_dot, 0.0), axis=1, keepdims=True)
        inner_grads.append(inner[:, 2 * k : 2 * k + 1] + inner[:, 2 * k + 1 : 2 * k + 2] + own_bias)
    mean = gates[0] * inner_grads[0] + gates[1] * inner_grads[1]
    logit_grad = 0.0
    for k in range(2):
        logit_grad = logit_grad + jnp.where(picks[k], gates[k] * (inner_grads[k] - mean), 0.0)
    logit_ref[...] = logit_grad.astype(BF16)
    hidden_grad = home_ref[:tok_count, :].astype(F32) + other_ref[:tok_count, :].astype(F32)
    hidden_grad = hidden_grad + nt(logit_ref[...], router_ref[...])
    normed = normed_ref[...]
    inner = hidden_grad * gain_ref[...]
    middle_grad = cot_ref[...].astype(F32) + norm_back(inner, normed, facts_ref[:, 6:7])
    middle_grad_ref[...] = middle_grad
    middle_low = middle_grad.astype(BF16)
    small_ref[...] = jnp.zeros_like(small_ref)
    small_ref[:experts, :] = tn(logit_ref[...], hidden2_ref[...])
    small_ref[experts : 2 * experts, :] = bias_grad_ref[...]
    small_ref[2 * experts : 2 * experts + 1, :] = jnp.sum(hidden_grad * normed, axis=0, keepdims=True)
    small_ref[2 * experts + 1 : 2 * experts + 2, :] = jnp.sum(hidden_grad, axis=0, keepdims=True)
    small_ref[2 * experts + 2 : 2 * experts + 3, :] = jnp.sum(middle_grad, axis=0, keepdims=True)
    back_ref[...] = nt(middle_low, proj_ref[...]).astype(BF16)
    for h in range(head_cols // HEAD):
        cols = slice(h * HEAD, (h + 1) * HEAD)
        queries, key_vals, values_in = (projected_ref[j, :, cols] for j in range(3))
        out_grad = back_ref[:, cols]
        prob_vals = jnp.exp(nt(queries, key_vals) * scale - facts_ref[:, h + 8 : h + 9])
        prob_low = prob_vals.astype(BF16)
        prob_grad = nt(out_grad, values_in)
        row = jnp.sum(prob_vals * prob_grad, axis=-1, keepdims=True)
        score_low = (prob_vals * (prob_grad - row)).astype(BF16)
        low_ref[:, h * HEAD : (h + 1) * HEAD] = (nn(score_low, key_vals) * scale).astype(BF16)
        start = head_cols + h * HEAD
        low_ref[:, start : start + HEAD] = (tn(score_low, queries) * scale).astype(BF16)
        start = start + head_cols
        low_ref[:, start : start + HEAD] = tn(prob_low, out_grad).astype(BF16)
    low = low_ref[...]
    half = kept_ref.shape[0]
    mixed_middle = nt(mix_ref[1], middle_low).astype(BF16)
    small = small_ref[...].astype(BF16)
    for part in range(2):
        rows = slice(part * half, (part + 1) * half)
        pieces = (
            nn(hidden_ref[0, rows, :], low[:, : 2 * head_cols]),
            nt(mix_ref[0, rows, :], small),
            nn(hidden_ref[1, rows, :], low[:, 2 * head_cols :]),
            nn(mixed_middle[rows, :], attended_ref[...]),
        )
        first = 0
        for piece in pieces:
            last = first + piece.shape[1]
            if part == 0:
                kept_ref[:, first:last] = piece
            else:
                sent_ref[:, first:last] = piece.astype(BF16)
            first = last
    part = nt(low[:, :head_cols], weight_ref[0])
    part = part + nt(low[:, head_cols : 2 * head_cols], weight_ref[1])
    part = part + nt(low[:, 2 * head_cols :], weight_ref[2])
    hidden_part_ref[...] = part.astype(BF16)
    sums_ref[...] = jnp.sum(low.astype(F32), axis=0, keepdims=True)


def attention_grads(*operands):
    tok_count, feat_dim = operands[3].shape
    experts = operands[2].shape[1]
    head_cols = operands[9].shape[0]
    small = -(-(2 * experts + 3) // 128) * 128
    width = 4 * head_cols + small
    flops = 2 * tok_count * feat_dim * head_cols * 9 + 2 * feat_dim * feat_dim * (tok_count + small)
    return pl.pallas_call(
        attention_grads_kernel,
        out_shape=(
            jax.ShapeDtypeStruct((feat_dim // 2, width), BF16),
            jax.ShapeDtypeStruct((feat_dim // 2, width), F32),
            jax.ShapeDtypeStruct((tok_count, feat_dim), BF16),
            jax.ShapeDtypeStruct((1, 3 * head_cols), F32),
            jax.ShapeDtypeStruct((tok_count, feat_dim), F32),
        ),
        scratch_shapes=[
            pltpu.VMEM((tok_count, 3 * head_cols), BF16),
            pltpu.VMEM((tok_count, head_cols), BF16),
            pltpu.VMEM((small, feat_dim), F32),
            pltpu.VMEM((tok_count, experts), BF16),
        ],
        compiler_params=pltpu.CompilerParams(vmem_limit_bytes=60 << 20),
        cost_estimate=pl.CostEstimate(
            flops=30 * flops, bytes_accessed=10 << 20, transcendentals=tok_count * tok_count * 6
        ),
        name="attention_grads",
    )(*operands)


def finish_kernel(head_cols, experts, orders, me_ref, mine, mine_b, got, got_b, qkv_ref, proj_ref, router_ref, bias_ref, norm_ref, held_proj, held_small):
    me = me_ref[0]
    count = 1 << len(orders[0])
    feat_dim = qkv_ref.shape[1]
    chunk = feat_dim // count
    half = count // 2
    for spot in range(count):
        starts = []
        for order in orders:
            name = sum(bit for i, bit in enumerate(order) if (spot >> (len(order) - 1 - i)) & 1)
            starts.append(pl.ds(pl.multiple_of((name ^ me) * chunk, chunk), chunk))
        source, source_b = (mine, mine_b) if spot < half else (got, got_b)
        first = (spot % half) * chunk
        piece = source[first : first + chunk, :].astype(F32)
        qkv_ref[0, starts[0], :] = piece[:, :head_cols]
        qkv_ref[1, starts[0], :] = piece[:, head_cols : 2 * head_cols]
        held_small[starts[0], :] = piece[:, 2 * head_cols :]
        piece = source_b[first : first + chunk, :].astype(F32)
        qkv_ref[2, starts[1], :] = piece[:, :head_cols]
        held_proj[starts[1], :] = piece[:, head_cols:]
    proj_ref[...] = held_proj[...].T
    small = held_small[...]
    flat = small.T
    router_ref[...] = flat[:experts]
    bias_ref[...] = flat[experts : 2 * experts]
    norm_ref[...] = flat[2 * experts : 2 * experts + 8]


def finish(me, mine, mine_b, came, came_b, head_cols, experts, feat_dim, orders):
    width = mine.shape[1] - 2 * head_cols
    vmem = pl.BlockSpec(memory_space=pltpu.VMEM)
    return pl.pallas_call(
        lambda *refs: finish_kernel(head_cols, experts, orders, *refs),
        in_specs=[pl.BlockSpec(memory_space=pltpu.SMEM)] + [vmem] * 4,
        out_specs=[vmem] * 5,
        out_shape=(
            jax.ShapeDtypeStruct((3, feat_dim, head_cols), F32),
            jax.ShapeDtypeStruct((head_cols, feat_dim), F32),
            jax.ShapeDtypeStruct((experts, feat_dim), F32),
            jax.ShapeDtypeStruct((experts, feat_dim), F32),
            jax.ShapeDtypeStruct((8, feat_dim), F32),
        ),
        scratch_shapes=[
            pltpu.VMEM((feat_dim, head_cols), F32),
            pltpu.VMEM((feat_dim, width), F32),
        ],
        compiler_params=pltpu.CompilerParams(vmem_limit_bytes=40 << 20),
        name="finish",
    )(me[None], mine, mine_b, came, came_b)


def high_low(values):
    high = values.astype(BF16)
    return high, (values - high.astype(F32)).astype(BF16)


def local(
    inputs,
    norm1_gain,
    norm1_bias,
    qkv_weight,
    qv_bias,
    proj_weight,
    proj_bias,
    norm2_gain,
    norm2_bias,
    router,
    expert_in,
    expert_in_bias,
    expert_out,
    expert_out_bias,
    routes,
    cotangent,
):
    tok_count = inputs.shape[0]
    feat_dim = inputs.shape[1]
    half_dim = feat_dim // 2
    head_cols = qkv_weight.shape[2]
    heads_here = head_cols // HEAD
    images = tok_count // SEQ
    experts = router.shape[1]
    sources = lax.axis_size("dp")
    group_size = sources // experts
    capacity = max(2, (10 * tok_count + 3 * experts - 1) // (3 * experts))
    slots = (capacity + 3 + 15) // 16 * 16
    score_scale = HEAD ** (-0.5)
    plane = lax.axis_index("tensor")
    me = lax.axis_index("dp")
    own_expert = me // group_size
    in_weight, out_weight = expert_in[0], expert_out[0]

    expert_ids = jnp.arange(experts, dtype=jnp.int32)
    slot_ids = jnp.arange(slots, dtype=jnp.int32)
    all_ids = jnp.arange(experts * slots, dtype=jnp.int32)
    pick = [(routes[:, k : k + 1] == expert_ids[None, :]) for k in range(2)]
    named = (pick[0] | pick[1]).astype(BF16)
    before = (
        jnp.arange(tok_count)[:, None] > jnp.arange(tok_count)[None, :]
    ).astype(BF16)
    earlier = nn(before, named)
    rank = [
        jnp.sum(jnp.where(pick[k], earlier, 0.0), axis=1, keepdims=True).astype(jnp.int32)
        for k in range(2)
    ]
    place = [routes[:, k : k + 1] * slots + rank[k] for k in range(2)]
    onehot = ((place[0] == all_ids[None, :]) | (place[1] == all_ids[None, :])).astype(BF16)
    rank_hot = [(rank[k] == slot_ids[None, :]) for k in range(2)]
    pick_low = [pick[k].astype(BF16) for k in range(2)]
    partner = [
        jnp.where(rank_hot[k], routes[:, 1 - k : 2 - k].astype(F32), 0.0).astype(BF16)
        for k in range(2)
    ]
    partner_map = tn(pick_low[0], partner[0]) + tn(pick_low[1], partner[1])

    cot_half = half_of(plane, cotangent, 0)
    cot_send = tn(onehot, cot_half).astype(BF16).reshape(experts, slots, half_dim)
    note = jnp.pad(partner_map.astype(BF16), ((0, 0), (0, half_dim - slots)))[:, None, :]
    cot_send = jnp.where(slot_ids[None, :, None] == slots - 1, note, cot_send)
    cot_send = jnp.repeat(cot_send, group_size, axis=0)
    proj_other = swap(proj_weight)
    proj_full = in_order(plane, proj_weight, proj_other, 0)

    inputs, cot_send = lax.optimization_barrier((inputs, cot_send))
    cot_mine = lax.all_to_all(cot_send, "dp", split_axis=0, concat_axis=0, tiled=True)
    x_in = inputs.astype(F32)
    normed1, inverse1 = norm_parts(x_in)
    hidden1 = (normed1 * norm1_gain + norm1_bias).astype(BF16)
    projected = jnp.einsum("td,jde->jte", hidden1, qkv_weight, preferred_element_type=F32)
    bias_rows = jnp.stack([qv_bias[0], jnp.zeros_like(qv_bias[0]), qv_bias[1]])
    projected = (projected + bias_rows[:, None, :]).astype(BF16)
    projected, proj_full = lax.optimization_barrier((projected, proj_full))
    heads_view = projected.reshape(3, images, SEQ, heads_here, HEAD)
    queries, key_vals, values_in = (heads_view[0], heads_view[1], heads_view[2])
    scores = (
        jnp.einsum("bqhd,bkhd->bhqk", queries, key_vals, preferred_element_type=F32)
        * score_scale
    )
    row_max = jnp.max(scores, axis=-1, keepdims=True)
    exp_scores = jnp.exp(scores - row_max)
    row_total = jnp.sum(exp_scores, axis=-1, keepdims=True)
    lse = (row_max + jnp.log(row_total)).reshape(heads_here, tok_count).T
    prob_low = (exp_scores / row_total).astype(BF16)
    attended = jnp.einsum("bhqk,bkhd->bqhd", prob_low, values_in, preferred_element_type=F32)
    attended = attended.reshape(tok_count, head_cols).astype(BF16)
    attended_all = in_order(plane, attended, swap(attended), 1)
    attended_all, cot_mine = lax.optimization_barrier((attended_all, cot_mine))
    cot_other = swap(cot_mine)
    middle = x_in + nn(attended_all, proj_full) + proj_bias
    normed2, inverse2 = norm_parts(middle)
    hidden2 = (normed2 * norm2_gain + norm2_bias).astype(BF16)

    send = tn(onehot, hidden2).astype(BF16).reshape(experts, slots, feat_dim)
    send = jnp.repeat(send, group_size, axis=0)
    arrived = lax.all_to_all(send, "dp", split_axis=0, concat_axis=0, tiled=True)
    arrived = arrived.reshape(-1, feat_dim)

    logits = nn(hidden2, router)
    chosen = [jnp.sum(jnp.where(pick[k], logits, 0.0), axis=1, keepdims=True) for k in range(2)]
    chosen_max = jnp.maximum(chosen[0], chosen[1])
    chosen_exp = [jnp.exp(chosen[k] - chosen_max) for k in range(2)]
    chosen_sum = chosen_exp[0] + chosen_exp[1]
    gate_vals = [chosen_exp[k] / chosen_sum for k in range(2)]
    gate_map = jnp.where(pick[0], gate_vals[0], 0.0) + jnp.where(pick[1], gate_vals[1], 0.0)
    grad_out = cotangent.astype(F32)
    row_grad = [(gate_vals[k] * grad_out).astype(BF16) for k in range(2)]
    out_bias_grad = tn(pick_low[0], row_grad[0]) + tn(pick_low[1], row_grad[1])

    other_expert = cot_mine[:, slots - 1, :slots].reshape(-1, 1).astype(F32)
    cot_rows = in_order(plane, cot_mine, cot_other, 2).reshape(-1, feat_dim)
    bits = [1 << i for i in range(sources.bit_length() - 1)]
    orders = [bits, bits[:1] + bits[2:] + bits[1:2]]
    chunk = feat_dim // sources

    rows = jnp.arange(feat_dim, dtype=jnp.int32)[None, :]
    cols = jnp.arange(feat_dim, dtype=jnp.int32)[:, None]
    spot = cols // chunk
    mix_t = []
    for order in orders:
        piece = jnp.zeros_like(spot)
        for i, bit in enumerate(order):
            piece = piece | jnp.where((spot >> (len(bits) - 1 - i)) & 1 == 1, bit, 0)
        mix_t.append(
            ((rows // chunk == (piece ^ me)) & (rows % chunk == cols % chunk)).astype(BF16)
        )
    mix_t = jnp.stack(mix_t)
    hidden1_t = jnp.einsum("jqd,td->jqt", mix_t, hidden1, preferred_element_type=F32).astype(BF16)
    bias_dot = lax.dot_general(
        grad_out,
        expert_out_bias,
        (((1,), (1,)), ((), ())),
        precision=lax.Precision.HIGHEST,
        preferred_element_type=F32,
    )
    facts = [routes.astype(F32)] + [r.astype(F32) for r in rank] + gate_vals + [inverse2]
    facts = jnp.concatenate(facts, axis=1)
    facts = jnp.concatenate([facts, jnp.zeros_like(facts[:, :1]), lse], axis=1)
    facts = jnp.pad(facts, ((0, 0), (0, 16 - facts.shape[1])))
    facts = jnp.pad(jnp.concatenate([facts, bias_dot], axis=1), ((0, 0), (0, 112 - experts)))
    ready = (
        mix_t, hidden1_t, facts, onehot, out_bias_grad, normed2, hidden2, projected, attended, gate_map,
        cot_rows,
    )
    arrived, ready = lax.optimization_barrier((arrived, ready))
    (
        mix_t, hidden1_t, facts, onehot, out_bias_grad, normed2, hidden2, projected, attended, gate_map,
        cot_rows,
    ) = ready
    activ_low, act_low, grad_rows, row_send, out_send, in_bias_grad = (
        expert_rows if sources * slots <= 1024 else expert_rows_plain
    )(
        own_expert, arrived, cot_rows, other_expert, router, in_weight, expert_in_bias, out_weight, capacity, slots
    )
    row_send = row_send.reshape(sources, slots, feat_dim)
    row_back = lax.all_to_all(row_send, "dp", split_axis=0, concat_axis=0, tiled=True)
    out_weight_grad = tn(activ_low, grad_rows)
    in_weight_grad = tn(arrived, act_low)
    out_send, out_weight_grad, in_weight_grad = lax.optimization_barrier(
        (out_send, out_weight_grad, in_weight_grad)
    )
    def over_group(x):
        if group_size == 1:
            return x
        shape = (experts, group_size) + x.shape[1:]
        return jnp.sum(x.reshape(shape).astype(F32), axis=1).astype(BF16)

    row_home = home_rows(
        over_group(row_back),
        onehot,
        facts,
    )
    out_send = out_send.reshape(sources, slots, feat_dim)
    row_other = swap(row_home)
    out_back = lax.all_to_all(out_send, "dp", split_axis=0, concat_axis=0, tiled=True)

    sent, kept, hidden1_part, qv_sums, middle_grad = attention_grads(
        row_home,
        row_other,
        router,
        cotangent,
        normed2,
        facts,
        norm2_gain[None],
        hidden2,
        out_bias_grad,
        proj_weight,
        projected,
        attended,
        hidden1_t,
        qkv_weight,
        mix_t,
    )
    hidden1_other = swap(hidden1_part)
    split = sent.shape[1] - 2 * head_cols
    came = across(sent, bits[0], sources)
    total = kept + came.astype(F32)
    totals = [total[:, :split], total[:, split:]]
    for turn in range(1, len(bits)):
        if turn == 2:
            totals, hidden1_other, out_back = lax.optimization_barrier((totals, hidden1_other, out_back))
            out_home = nn(onehot, over_group(out_back).reshape(-1, feat_dim)).astype(BF16)
        if turn == len(bits) - 1:
            totals, out_home = lax.optimization_barrier((totals, out_home))
            out_other = swap(out_home)
        sends = lax.optimization_barrier([t[t.shape[0] // 2 :].astype(BF16) for t in totals])
        cames = [across(t, order[turn], sources) for t, order in zip(sends, orders)]
        totals = [keep_half(t, c) for t, c in zip(totals, cames)]
    hidden1_grad = hidden1_part.astype(F32) + hidden1_other.astype(F32)
    norm1_gain_grad = jnp.sum(hidden1_grad * normed1, axis=0)
    norm1_bias_grad = jnp.sum(hidden1_grad, axis=0)
    input_grad = middle_grad + norm_back(hidden1_grad * norm1_gain, normed1, inverse1)
    bias_home = exact(gate_map, expert_out_bias)
    mine = [t.astype(BF16) for t in totals]
    late = jnp.stack(
        [
            norm1_gain_grad,
            norm1_bias_grad,
            jnp.concatenate([qv_sums[0, :head_cols], qv_sums[0, 2 * head_cols :]]),
        ]
    )
    late = jnp.pad(late, ((0, 5), (0, 0)))

    def late_rows(late):
        high, low = high_low(late)
        both = jnp.pad(jnp.concatenate([high, low], axis=0), ((0, 0), (0, split - feat_dim)))
        return high.astype(F32) + low.astype(F32), both

    def late_sum(own, came):
        came = came[:, :feat_dim].astype(F32)
        return own + (came[:8] + came[8:])

    size = chunk
    for turn in range(len(bits) - 1, 0, -1):
        own, both = late_rows(late)
        first, second = jnp.concatenate([mine[0], both], axis=0), mine[1]
        if turn == 1:
            first, second, out_other = lax.optimization_barrier((first, second, out_other))
        else:
            first, second = lax.optimization_barrier((first, second))
        came = across(first, orders[0][turn], sources)
        came_b = across(second, orders[1][turn], sources)
        late = late_sum(own, came[size:])
        mine = [
            jnp.concatenate([mine[0], came[:size]], axis=0),
            jnp.concatenate([mine[1], came_b], axis=0),
        ]
        size = 2 * size
    out_home = out_home.astype(F32) + out_other.astype(F32)
    output = (middle + (out_home + bias_home)).astype(BF16)
    own, both = late_rows(late)
    first, second, input_grad, output = lax.optimization_barrier(
        (jnp.concatenate([mine[0], both], axis=0), mine[1], input_grad, output)
    )
    came = across(first, bits[0], sources)
    came_b = across(second, bits[0], sources)
    late = late_sum(own, came[size:])
    qv_bias_grad = late[2].reshape(2, head_cols)
    if chunk % 16 == 0:
        qkv_grad, proj_grad, router_grad, out_bias_grad, norm_grads = finish(
            me, first, second, came, came_b, head_cols, experts, feat_dim, orders
        )
        router_grad = router_grad.T
    else:
        first = tn(mix_t[0], jnp.concatenate([mine[0], came[:size]], axis=0))
        second = tn(mix_t[1], jnp.concatenate([mine[1], came_b], axis=0))
        qkv_grad = jnp.stack(
            [first[:, :head_cols], first[:, head_cols : 2 * head_cols], second[:, :head_cols]]
        )
        proj_grad = second[:, head_cols:].T
        router_grad = first[:, 2 * head_cols : 2 * head_cols + experts]
        norm_grads = first[:, 2 * head_cols + experts :].T
        out_bias_grad, norm_grads = norm_grads[:experts], norm_grads[experts:]
    norm2_gain_grad, norm2_bias_grad, proj_bias_grad = norm_grads[0], norm_grads[1], norm_grads[2]
    return (
        output,
        input_grad,
        late[0],
        late[1],
        qkv_grad,
        qv_bias_grad,
        proj_grad,
        proj_bias_grad,
        norm2_gain_grad,
        norm2_bias_grad,
        router_grad,
        in_weight_grad[None],
        in_bias_grad,
        out_weight_grad[None],
        out_bias_grad,
    )


def solution(mesh):
    return jax.shard_map(
        local,
        mesh=mesh,
        in_specs=(
            P("dp", None),
            P(),
            P(),
            P(None, None, "tensor"),
            P(None, "tensor"),
            P("tensor", None),
            P(),
            P(),
            P(),
            P(),
            P("dp", None, "tensor"),
            P("dp", "tensor"),
            P("dp", "tensor", None),
            P(),
            P("dp", None),
            P("dp", None),
        ),
        out_specs=(
            P("dp", None),
            P("dp", None),
            P(),
            P(),
            P(None, None, "tensor"),
            P(None, "tensor"),
            P("tensor", None),
            P(),
            P(),
            P(),
            P(),
            P("dp", None, "tensor"),
            P("dp", "tensor"),
            P("dp", "tensor", None),
            P(),
        ),
        check_vma=False,
    )
```

```python
import jax
import jax.numpy as jnp
from jax import lax
from jax.experimental import pallas as pl
from jax.experimental.pallas import tpu as pltpu
from jax.sharding import PartitionSpec as P

HEAD = 64
SEQ = 197
F32 = jnp.float32
BF16 = jnp.bfloat16

epsilon = 1e-06


def norm_parts(values):
    average = jnp.mean(values, axis=-1, keepdims=True)
    centred = values - average
    inverse = lax.rsqrt(jnp.mean(centred * centred, axis=-1, keepdims=True) + epsilon)
    return (centred * inverse, inverse)


def norm_back(inner_grad, normed, inverse):
    first_mean = jnp.mean(inner_grad, axis=-1, keepdims=True)
    second_mean = jnp.mean(inner_grad * normed, axis=-1, keepdims=True)
    return inverse * (inner_grad - first_mean - normed * second_mean)


def gelu_parts(pre_act):
    normal_cdf = 0.5 * (1.0 + lax.erf(pre_act * 0.7071067811865476))
    density = jnp.exp(-0.5 * pre_act * pre_act) * 0.3989422804014327
    return (pre_act * normal_cdf, normal_cdf + pre_act * density)


def dot(a, b, dims, out=F32):
    return lax.dot_general(a, b, (dims, ((), ())), preferred_element_type=out)


def nn(a, b):
    return dot(a, b, ((1,), (0,)))


def nt(a, b):
    return dot(a, b, ((1,), (1,)))


def tn(a, b):
    return dot(a, b, ((0,), (0,)))


def exact(a, b):
    return lax.dot_general(
        a,
        b,
        (((1,), (0,)), ((), ())),
        precision=lax.Precision.HIGHEST,
        preferred_element_type=F32,
    )


def swap(x):
    return lax.ppermute(x, "tensor", [(0, 1), (1, 0)])


def across(x, bit, count):
    return lax.ppermute(x, "dp", [(i, i ^ bit) for i in range(count)])


def in_order(plane, mine, other, axis):
    first = jnp.where(plane == 0, mine, other)
    second = jnp.where(plane == 0, other, mine)
    return jnp.concatenate([first, second], axis=axis)


def half_of(plane, x, which):
    width = x.shape[-1] // 2
    low, high = x[..., :width], x[..., width:]
    return jnp.where((plane == which), low, high)


def keep_half(total, came):
    middle = total.shape[0] // 2
    return total[:middle] + came.astype(F32)


def expert_kernel(
    capacity, slots, own_ref, arrived_ref, cot_ref, other_ref, router_ref, in_ref, bias_ref, out_ref,
    activ_ref, slope_ref, grad_rows_ref, row_ref, out_rows_ref, bias_grad_ref, gate_ref, row_sum, out_sum,
):
    step = pl.program_id(0)
    count = arrived_ref.shape[0]
    experts = router_ref.shape[1]

    @pl.when(step == 0)
    def _():
        logits = nn(arrived_ref[...], router_ref[...])
        ids = lax.broadcasted_iota(jnp.int32, (count, experts), 1)
        own = jnp.sum(jnp.where(ids == own_ref[0], logits, 0.0), axis=1, keepdims=True)
        other = jnp.sum(jnp.where(ids.astype(F32) == other_ref[...], logits, 0.0), axis=1, keepdims=True)
        top = jnp.maximum(own, other)
        own, other = jnp.exp(own - top), jnp.exp(other - top)
        spot = lax.broadcasted_iota(jnp.int32, (count, 1), 0) % slots
        gate = jnp.where(spot < capacity, own / (own + other), 0.0)
        gate_ref[...] = jnp.broadcast_to(gate, gate_ref.shape)
        grad_rows_ref[...] = (gate * cot_ref[...].astype(F32)).astype(BF16)
        row_sum[...] = jnp.zeros_like(row_sum)
        out_sum[...] = jnp.zeros_like(out_sum)

    pre_act = nn(arrived_ref[...], in_ref[...]) + bias_ref[...]
    activ, slope = gelu_parts(pre_act)
    activ = activ.astype(BF16)
    activ_ref[...] = activ
    grad = nt(grad_rows_ref[...], out_ref[...]) * slope
    bias_grad_ref[...] = jnp.sum(grad, axis=0, keepdims=True)
    grad = grad.astype(BF16)
    slope_ref[...] = grad
    row_sum[...] += nt(grad, in_ref[...])
    out_sum[...] += nn(activ, out_ref[...])

    @pl.when(step == pl.num_programs(0) - 1)
    def _():
        inner = jnp.sum(cot_ref[...].astype(F32) * out_sum[...], axis=1, keepdims=True)
        inner = jnp.broadcast_to(inner, gate_ref.shape).T
        out_rows_ref[...] = (gate_ref[:, :1] * out_sum[...]).astype(BF16)
        spot = lax.broadcasted_iota(jnp.int32, (slots, 128), 0)
        row_ref[...] = row_sum[...].astype(BF16)
        for source in range(count // slots):
            first = source * slots
            line = inner[:1, first : first + slots]
            line = jnp.concatenate([line, jnp.zeros((1, 128 - slots), F32)], axis=1)
            high = line.astype(BF16).astype(F32)
            tail = row_sum[first + slots - 16 : first + slots, :128]
            place = lax.broadcasted_iota(jnp.int32, tail.shape, 0)
            tail = jnp.where(place == 15, high, jnp.where(place == 14, line - high, tail))
            row_ref[first + slots - 16 : first + slots, :128] = tail.astype(BF16)


def expert_rows(own, arrived, cot_rows, other, router, in_weight, in_bias, out_weight, capacity, slots):
    count, feat_dim = arrived.shape
    hidden = in_weight.shape[1]
    block = 512 if hidden % 512 == 0 else hidden
    whole = lambda shape: pl.BlockSpec(shape, lambda i: (0, 0))
    return pl.pallas_call(
        lambda *refs: expert_kernel(capacity, slots, *refs),
        grid=(hidden // block,),
        in_specs=[
            pl.BlockSpec(memory_space=pltpu.SMEM),
            whole((count, feat_dim)),
            whole((count, feat_dim)),
            whole((count, 1)),
            whole(router.shape),
            pl.BlockSpec((feat_dim, block), lambda i: (0, i)),
            pl.BlockSpec((1, block), lambda i: (0, i)),
            pl.BlockSpec((block, feat_dim), lambda i: (i, 0)),
        ],
        out_specs=[
            pl.BlockSpec((count, block), lambda i: (0, i)),
            pl.BlockSpec((count, block), lambda i: (0, i)),
            whole((count, feat_dim)),
            whole((count, feat_dim)),
            whole((count, feat_dim)),
            pl.BlockSpec((1, block), lambda i: (0, i)),
        ],
        out_shape=(
            jax.ShapeDtypeStruct((count, hidden), BF16),
            jax.ShapeDtypeStruct((count, hidden), BF16),
            jax.ShapeDtypeStruct((count, feat_dim), BF16),
            jax.ShapeDtypeStruct((count, feat_dim), BF16),
            jax.ShapeDtypeStruct((count, feat_dim), BF16),
            jax.ShapeDtypeStruct((1, hidden), F32),
        ),
        scratch_shapes=[
            pltpu.VMEM((count, 128), F32),
            pltpu.VMEM((count, feat_dim), F32),
            pltpu.VMEM((count, feat_dim), F32),
        ],
        compiler_params=pltpu.CompilerParams(vmem_limit_bytes=60 << 20),
        cost_estimate=pl.CostEstimate(
            flops=8 * count * feat_dim * hidden, bytes_accessed=12 << 20, transcendentals=2 * count * hidden
        ),
        name="expert_rows",
    )(own[None], arrived, cot_rows, other, router, in_weight, in_bias, out_weight)


def expert_rows_plain(own, arrived, cot_rows, other, router, in_weight, in_bias, out_weight, capacity, slots):
    count, feat_dim = arrived.shape
    logits = nn(arrived, router)
    ids = jnp.arange(router.shape[1], dtype=jnp.int32)[None, :]
    own = jnp.sum(jnp.where(ids == own, logits, 0.0), axis=1, keepdims=True)
    other = jnp.sum(jnp.where(ids.astype(F32) == other, logits, 0.0), axis=1, keepdims=True)
    top = jnp.maximum(own, other)
    own, other = jnp.exp(own - top), jnp.exp(other - top)
    spot = jnp.arange(count, dtype=jnp.int32)[:, None] % slots
    gate = jnp.where(spot < capacity, own / (own + other), 0.0)
    grad_rows = (gate * cot_rows.astype(F32)).astype(BF16)
    activ, slope = gelu_parts(nn(arrived, in_weight) + in_bias)
    activ = activ.astype(BF16)
    grad = nt(grad_rows, out_weight) * slope
    bias_grad = jnp.sum(grad, axis=0, keepdims=True)
    grad = grad.astype(BF16)
    part_out = nn(activ, out_weight)
    inner = jnp.sum(cot_rows.astype(F32) * part_out, axis=1).reshape(-1, slots)
    high, low = high_low(jnp.pad(inner, ((0, 0), (0, feat_dim - slots)))[:, None, :])
    rows = nt(grad, in_weight).astype(BF16).reshape(-1, slots, feat_dim)
    rows = jnp.concatenate([rows[:, : slots - 2], low, high], axis=1).reshape(count, feat_dim)
    return activ, grad, grad_rows, rows, (gate * part_out).astype(BF16), bias_grad


def home_kernel(back_ref, onehot_ref, facts_ref, home_ref, inner_ref):
    experts, slots, feat_dim = back_ref.shape
    tok_count = facts_ref.shape[0]
    home = nn(onehot_ref[...], back_ref[...].reshape(experts * slots, feat_dim))
    home_ref[:tok_count, :] = home.astype(BF16)
    for e in range(experts):
        inner_ref[0, e : e + 1, :] = back_ref[e, slots - 1 : slots, :slots].astype(F32)
        inner_ref[1, e : e + 1, :] = back_ref[e, slots - 2 : slots - 1, :slots].astype(F32)
    expert_ids = lax.broadcasted_iota(jnp.int32, (tok_count, experts), 1).astype(F32)
    slot_ids = lax.broadcasted_iota(jnp.int32, (tok_count, slots), 1).astype(F32)
    lanes = lax.broadcasted_iota(jnp.int32, (tok_count, 128), 1)
    table = jnp.zeros((tok_count, 128), F32)
    for k in range(2):
        hot = jnp.where(facts_ref[:, k : k + 1] == expert_ids, 1.0, 0.0).astype(BF16)
        found = nn(hot, inner_ref[0].astype(BF16)) + nn(hot, inner_ref[1].astype(BF16))
        found = jnp.where(facts_ref[:, k + 2 : k + 3] == slot_ids, found, 0.0)
        found = jnp.sum(found, axis=1, keepdims=True)
        high = found.astype(BF16).astype(F32)
        table = jnp.where(lanes == 2 * k, high, jnp.where(lanes == 2 * k + 1, found - high, table))
    home_ref[tok_count + 3 : tok_count + 11, :tok_count] = table.T[:8, :].astype(BF16)


def home_rows(back, onehot, facts):
    experts, slots, feat_dim = back.shape
    tok_count = facts.shape[0]
    return pl.pallas_call(
        home_kernel,
        out_shape=jax.ShapeDtypeStruct((tok_count + 11, feat_dim), BF16),
        scratch_shapes=[pltpu.VMEM((2, experts, slots), F32)],
        compiler_params=pltpu.CompilerParams(vmem_limit_bytes=16 << 20),
        cost_estimate=pl.CostEstimate(
            flops=2 * tok_count * feat_dim * experts * slots, bytes_accessed=2 << 20, transcendentals=0
        ),
        name="home_rows",
    )(back, onehot, facts)


def attention_grads_kernel(
    home_ref, other_ref, router_ref, cot_ref, normed_ref, facts_ref, gain_ref, hidden2_ref, bias_grad_ref,
    proj_ref, projected_ref, attended_ref, hidden_ref, weight_ref, mix_ref,
    sent_ref, kept_ref, hidden_part_ref, sums_ref, middle_grad_ref, low_ref, back_ref, small_ref, logit_ref,
):
    head_cols = attended_ref.shape[1]
    experts = router_ref.shape[1]
    tok_count = cot_ref.shape[0]
    scale = HEAD ** (-0.5)
    lines = slice(tok_count + 3, tok_count + 11)
    inner = home_ref[lines, :tok_count].astype(F32) + other_ref[lines, :tok_count].astype(F32)
    inner = inner.T
    bias_dot = facts_ref[:, 16 : 16 + experts]
    expert_ids = lax.broadcasted_iota(jnp.int32, (tok_count, experts), 1).astype(F32)
    picks = [facts_ref[:, k : k + 1] == expert_ids for k in range(2)]
    gates = [facts_ref[:, k + 4 : k + 5] for k in range(2)]
    inner_grads = []
    for k in range(2):
        own_bias = jnp.sum(jnp.where(picks[k], bias_dot, 0.0), axis=1, keepdims=True)
        inner_grads.append(inner[:, 2 * k : 2 * k + 1] + inner[:, 2 * k + 1 : 2 * k + 2] + own_bias)
    mean = gates[0] * inner_grads[0] + gates[1] * inner_grads[1]
    logit_grad = 0.0
    for k in range(2):
        logit_grad = logit_grad + jnp.where(picks[k], gates[k] * (inner_grads[k] - mean), 0.0)
    logit_ref[...] = logit_grad.astype(BF16)
    hidden_grad = home_ref[:tok_count, :].astype(F32) + other_ref[:tok_count, :].astype(F32)
    hidden_grad = hidden_grad + nt(logit_ref[...], router_ref[...])
    normed = normed_ref[...]
    inner = hidden_grad * gain_ref[...]
    middle_grad = cot_ref[...].astype(F32) + norm_back(inner, normed, facts_ref[:, 6:7])
    middle_grad_ref[...] = middle_grad
    middle_low = middle_grad.astype(BF16)
    small_ref[...] = jnp.zeros_like(small_ref)
    small_ref[:experts, :] = tn(logit_ref[...], hidden2_ref[...])
    small_ref[experts : 2 * experts, :] = bias_grad_ref[...]
    small_ref[2 * experts : 2 * experts + 1, :] = jnp.sum(hidden_grad * normed, axis=0, keepdims=True)
    small_ref[2 * experts + 1 : 2 * experts + 2, :] = jnp.sum(hidden_grad, axis=0, keepdims=True)
    small_ref[2 * experts + 2 : 2 * experts + 3, :] = jnp.sum(middle_grad, axis=0, keepdims=True)
    back_ref[...] = nt(middle_low, proj_ref[...]).astype(BF16)
    for h in range(head_cols // HEAD):
        cols = slice(h * HEAD, (h + 1) * HEAD)
        queries, key_vals, values_in = (projected_ref[j, :, cols] for j in range(3))
        out_grad = back_ref[:, cols]
        prob_vals = jnp.exp(nt(queries, key_vals) * scale - facts_ref[:, h + 8 : h + 9])
        prob_low = prob_vals.astype(BF16)
        prob_grad = nt(out_grad, values_in)
        row = jnp.sum(prob_vals * prob_grad, axis=-1, keepdims=True)
        score_low = (prob_vals * (prob_grad - row)).astype(BF16)
        low_ref[:, h * HEAD : (h + 1) * HEAD] = (nn(score_low, key_vals) * scale).astype(BF16)
        start = head_cols + h * HEAD
        low_ref[:, start : start + HEAD] = (tn(score_low, queries) * scale).astype(BF16)
        start = start + head_cols
        low_ref[:, start : start + HEAD] = tn(prob_low, out_grad).astype(BF16)
    low = low_ref[...]
    half = kept_ref.shape[0]
    mixed_middle = nt(mix_ref[1], middle_low).astype(BF16)
    small = small_ref[...].astype(BF16)
    for part in range(2):
        rows = slice(part * half, (part + 1) * half)
        pieces = (
            nn(hidden_ref[0, rows, :], low[:, : 2 * head_cols]),
            nt(mix_ref[0, rows, :], small),
            nn(hidden_ref[1, rows, :], low[:, 2 * head_cols :]),
            nn(mixed_middle[rows, :], attended_ref[...]),
        )
        first = 0
        for piece in pieces:
            last = first + piece.shape[1]
            if part == 0:
                kept_ref[:, first:last] = piece
            else:
                sent_ref[:, first:last] = piece.astype(BF16)
            first = last
    part = nt(low[:, :head_cols], weight_ref[0])
    part = part + nt(low[:, head_cols : 2 * head_cols], weight_ref[1])
    part = part + nt(low[:, 2 * head_cols :], weight_ref[2])
    hidden_part_ref[...] = part.astype(BF16)
    sums_ref[...] = jnp.sum(low.astype(F32), axis=0, keepdims=True)


def attention_grads(*operands):
    tok_count, feat_dim = operands[3].shape
    experts = operands[2].shape[1]
    head_cols = operands[9].shape[0]
    small = -(-(2 * experts + 3) // 128) * 128
    width = 4 * head_cols + small
    flops = 2 * tok_count * feat_dim * head_cols * 9 + 2 * feat_dim * feat_dim * (tok_count + small)
    return pl.pallas_call(
        attention_grads_kernel,
        out_shape=(
            jax.ShapeDtypeStruct((feat_dim // 2, width), BF16),
            jax.ShapeDtypeStruct((feat_dim // 2, width), F32),
            jax.ShapeDtypeStruct((tok_count, feat_dim), BF16),
            jax.ShapeDtypeStruct((1, 3 * head_cols), F32),
            jax.ShapeDtypeStruct((tok_count, feat_dim), F32),
        ),
        scratch_shapes=[
            pltpu.VMEM((tok_count, 3 * head_cols), BF16),
            pltpu.VMEM((tok_count, head_cols), BF16),
            pltpu.VMEM((small, feat_dim), F32),
            pltpu.VMEM((tok_count, experts), BF16),
        ],
        compiler_params=pltpu.CompilerParams(vmem_limit_bytes=60 << 20),
        cost_estimate=pl.CostEstimate(
            flops=30 * flops, bytes_accessed=10 << 20, transcendentals=tok_count * tok_count * 6
        ),
        name="attention_grads",
    )(*operands)


def finish_kernel(head_cols, experts, orders, me_ref, mine, mine_b, got, got_b, qkv_ref, proj_ref, router_ref, bias_ref, norm_ref, held_proj, held_small):
    me = me_ref[0]
    count = 1 << len(orders[0])
    feat_dim = qkv_ref.shape[1]
    chunk = feat_dim // count
    half = count // 2
    for spot in range(count):
        starts = []
        for order in orders:
            name = sum(bit for i, bit in enumerate(order) if (spot >> (len(order) - 1 - i)) & 1)
            starts.append(pl.ds(pl.multiple_of((name ^ me) * chunk, chunk), chunk))
        source, source_b = (mine, mine_b) if spot < half else (got, got_b)
        first = (spot % half) * chunk
        piece = source[first : first + chunk, :].astype(F32)
        qkv_ref[0, starts[0], :] = piece[:, :head_cols]
        qkv_ref[1, starts[0], :] = piece[:, head_cols : 2 * head_cols]
        held_small[starts[0], :] = piece[:, 2 * head_cols :]
        piece = source_b[first : first + chunk, :].astype(F32)
        qkv_ref[2, starts[1], :] = piece[:, :head_cols]
        held_proj[starts[1], :] = piece[:, head_cols:]
    proj_ref[...] = held_proj[...].T
    small = held_small[...]
    flat = small.T
    router_ref[...] = flat[:experts]
    bias_ref[...] = flat[experts : 2 * experts]
    norm_ref[...] = flat[2 * experts : 2 * experts + 8]


def finish(me, mine, mine_b, came, came_b, head_cols, experts, feat_dim, orders):
    width = mine.shape[1] - 2 * head_cols
    vmem = pl.BlockSpec(memory_space=pltpu.VMEM)
    return pl.pallas_call(
        lambda *refs: finish_kernel(head_cols, experts, orders, *refs),
        in_specs=[pl.BlockSpec(memory_space=pltpu.SMEM)] + [vmem] * 4,
        out_specs=[vmem] * 5,
        out_shape=(
            jax.ShapeDtypeStruct((3, feat_dim, head_cols), F32),
            jax.ShapeDtypeStruct((head_cols, feat_dim), F32),
            jax.ShapeDtypeStruct((experts, feat_dim), F32),
            jax.ShapeDtypeStruct((experts, feat_dim), F32),
            jax.ShapeDtypeStruct((8, feat_dim), F32),
        ),
        scratch_shapes=[
            pltpu.VMEM((feat_dim, head_cols), F32),
            pltpu.VMEM((feat_dim, width), F32),
        ],
        compiler_params=pltpu.CompilerParams(vmem_limit_bytes=40 << 20),
        name="finish",
    )(me[None], mine, mine_b, came, came_b)


def high_low(values):
    high = values.astype(BF16)
    return high, (values - high.astype(F32)).astype(BF16)


def local(
    inputs,
    norm1_gain,
    norm1_bias,
    qkv_weight,
    qv_bias,
    proj_weight,
    proj_bias,
    norm2_gain,
    norm2_bias,
    router,
    expert_in,
    expert_in_bias,
    expert_out,
    expert_out_bias,
    routes,
    cotangent,
):
    tok_count = inputs.shape[0]
    feat_dim = inputs.shape[1]
    half_dim = feat_dim // 2
    head_cols = qkv_weight.shape[2]
    heads_here = head_cols // HEAD
    images = tok_count // SEQ
    experts = router.shape[1]
    sources = lax.axis_size("dp")
    group_size = sources // experts
    capacity = max(2, (10 * tok_count + 3 * experts - 1) // (3 * experts))
    slots = (capacity + 3 + 15) // 16 * 16
    score_scale = HEAD ** (-0.5)
    plane = lax.axis_index("tensor")
    me = lax.axis_index("dp")
    own_expert = me // group_size
    in_weight, out_weight = expert_in[0], expert_out[0]

    expert_ids = jnp.arange(experts, dtype=jnp.int32)
    slot_ids = jnp.arange(slots, dtype=jnp.int32)
    all_ids = jnp.arange(experts * slots, dtype=jnp.int32)
    pick = [(routes[:, k : k + 1] == expert_ids[None, :]) for k in range(2)]
    named = (pick[0] | pick[1]).astype(BF16)
    before = (
        jnp.arange(tok_count)[:, None] > jnp.arange(tok_count)[None, :]
    ).astype(BF16)
    earlier = nn(before, named)
    rank = [
        jnp.sum(jnp.where(pick[k], earlier, 0.0), axis=1, keepdims=True).astype(jnp.int32)
        for k in range(2)
    ]
    place = [routes[:, k : k + 1] * slots + rank[k] for k in range(2)]
    onehot = ((place[0] == all_ids[None, :]) | (place[1] == all_ids[None, :])).astype(BF16)
    rank_hot = [(rank[k] == slot_ids[None, :]) for k in range(2)]
    pick_low = [pick[k].astype(BF16) for k in range(2)]
    partner = [
        jnp.where(rank_hot[k], routes[:, 1 - k : 2 - k].astype(F32), 0.0).astype(BF16)
        for k in range(2)
    ]
    partner_map = tn(pick_low[0], partner[0]) + tn(pick_low[1], partner[1])

    cot_half = half_of(plane, cotangent, 0)
    cot_send = tn(onehot, cot_half).astype(BF16).reshape(experts, slots, half_dim)
    note = jnp.pad(partner_map.astype(BF16), ((0, 0), (0, half_dim - slots)))[:, None, :]
    cot_send = jnp.where(slot_ids[None, :, None] == slots - 1, note, cot_send)
    cot_send = jnp.repeat(cot_send, group_size, axis=0)
    proj_other = swap(proj_weight)
    proj_full = in_order(plane, proj_weight, proj_other, 0)

    inputs, cot_send = lax.optimization_barrier((inputs, cot_send))
    cot_mine = lax.all_to_all(cot_send, "dp", split_axis=0, concat_axis=0, tiled=True)
    x_in = inputs.astype(F32)
    normed1, inverse1 = norm_parts(x_in)
    hidden1 = (normed1 * norm1_gain + norm1_bias).astype(BF16)
    projected = jnp.einsum("td,jde->jte", hidden1, qkv_weight, preferred_element_type=F32)
    bias_rows = jnp.stack([qv_bias[0], jnp.zeros_like(qv_bias[0]), qv_bias[1]])
    projected = (projected + bias_rows[:, None, :]).astype(BF16)
    projected, proj_full = lax.optimization_barrier((projected, proj_full))
    heads_view = projected.reshape(3, images, SEQ, heads_here, HEAD)
    queries, key_vals, values_in = (heads_view[0], heads_view[1], heads_view[2])
    scores = (
        jnp.einsum("bqhd,bkhd->bhqk", queries, key_vals, preferred_element_type=F32)
        * score_scale
    )
    row_max = jnp.max(scores, axis=-1, keepdims=True)
    exp_scores = jnp.exp(scores - row_max)
    row_total = jnp.sum(exp_scores, axis=-1, keepdims=True)
    lse = (row_max + jnp.log(row_total)).reshape(heads_here, tok_count).T
    prob_low = (exp_scores / row_total).astype(BF16)
    attended = jnp.einsum("bhqk,bkhd->bqhd", prob_low, values_in, preferred_element_type=F32)
    attended = attended.reshape(tok_count, head_cols).astype(BF16)
    attended_all = in_order(plane, attended, swap(attended), 1)
    attended_all, cot_mine = lax.optimization_barrier((attended_all, cot_mine))
    cot_other = swap(cot_mine)
    middle = x_in + nn(attended_all, proj_full) + proj_bias
    normed2, inverse2 = norm_parts(middle)
    hidden2 = (normed2 * norm2_gain + norm2_bias).astype(BF16)

    send = tn(onehot, hidden2).astype(BF16).reshape(experts, slots, feat_dim)
    send = jnp.repeat(send, group_size, axis=0)
    arrived = lax.all_to_all(send, "dp", split_axis=0, concat_axis=0, tiled=True)
    arrived = arrived.reshape(-1, feat_dim)

    logits = nn(hidden2, router)
    chosen = [jnp.sum(jnp.where(pick[k], logits, 0.0), axis=1, keepdims=True) for k in range(2)]
    chosen_max = jnp.maximum(chosen[0], chosen[1])
    chosen_exp = [jnp.exp(chosen[k] - chosen_max) for k in range(2)]
    chosen_sum = chosen_exp[0] + chosen_exp[1]
    gate_vals = [chosen_exp[k] / chosen_sum for k in range(2)]
    gate_map = jnp.where(pick[0], gate_vals[0], 0.0) + jnp.where(pick[1], gate_vals[1], 0.0)
    grad_out = cotangent.astype(F32)
    row_grad = [(gate_vals[k] * grad_out).astype(BF16) for k in range(2)]
    out_bias_grad = tn(pick_low[0], row_grad[0]) + tn(pick_low[1], row_grad[1])

    other_expert = cot_mine[:, slots - 1, :slots].reshape(-1, 1).astype(F32)
    cot_rows = in_order(plane, cot_mine, cot_other, 2).reshape(-1, feat_dim)
    bits = [1 << i for i in range(sources.bit_length() - 1)]
    orders = [bits, bits[:1] + bits[2:] + bits[1:2]]
    chunk = feat_dim // sources

    rows = jnp.arange(feat_dim, dtype=jnp.int32)[None, :]
    cols = jnp.arange(feat_dim, dtype=jnp.int32)[:, None]
    spot = cols // chunk
    mix_t = []
    for order in orders:
        piece = jnp.zeros_like(spot)
        for i, bit in enumerate(order):
            piece = piece | jnp.where((spot >> (len(bits) - 1 - i)) & 1 == 1, bit, 0)
        mix_t.append(
            ((rows // chunk == (piece ^ me)) & (rows % chunk == cols % chunk)).astype(BF16)
        )
    mix_t = jnp.stack(mix_t)
    hidden1_t = jnp.einsum("jqd,td->jqt", mix_t, hidden1, preferred_element_type=F32).astype(BF16)
    bias_dot = lax.dot_general(
        grad_out,
        expert_out_bias,
        (((1,), (1,)), ((), ())),
        precision=lax.Precision.HIGHEST,
        preferred_element_type=F32,
    )
    facts = [routes.astype(F32)] + [r.astype(F32) for r in rank] + gate_vals + [inverse2]
    facts = jnp.concatenate(facts, axis=1)
    facts = jnp.concatenate([facts, jnp.zeros_like(facts[:, :1]), lse], axis=1)
    facts = jnp.pad(facts, ((0, 0), (0, 16 - facts.shape[1])))
    facts = jnp.pad(jnp.concatenate([facts, bias_dot], axis=1), ((0, 0), (0, 112 - experts)))
    ready = (
        mix_t, hidden1_t, facts, onehot, out_bias_grad, normed2, hidden2, projected, attended, gate_map,
        cot_rows,
    )
    arrived, ready = lax.optimization_barrier((arrived, ready))
    (
        mix_t, hidden1_t, facts, onehot, out_bias_grad, normed2, hidden2, projected, attended, gate_map,
        cot_rows,
    ) = ready
    activ_low, act_low, grad_rows, row_send, out_send, in_bias_grad = (
        expert_rows if sources * slots <= 1024 else expert_rows_plain
    )(
        own_expert, arrived, cot_rows, other_expert, router, in_weight, expert_in_bias, out_weight, capacity, slots
    )
    row_send = row_send.reshape(sources, slots, feat_dim)
    row_back = lax.all_to_all(row_send, "dp", split_axis=0, concat_axis=0, tiled=True)
    out_weight_grad = tn(activ_low, grad_rows)
    in_weight_grad = tn(arrived, act_low)
    out_send, out_weight_grad, in_weight_grad = lax.optimization_barrier(
        (out_send, out_weight_grad, in_weight_grad)
    )
    def over_group(x):
        if group_size == 1:
            return x
        shape = (experts, group_size) + x.shape[1:]
        return jnp.sum(x.reshape(shape).astype(F32), axis=1).astype(BF16)

    row_home = home_rows(
        over_group(row_back),
        onehot,
        facts,
    )
    out_send = out_send.reshape(sources, slots, feat_dim)
    row_other = swap(row_home)
    out_back = lax.all_to_all(out_send, "dp", split_axis=0, concat_axis=0, tiled=True)

    sent, kept, hidden1_part, qv_sums, middle_grad = attention_grads(
        row_home,
        row_other,
        router,
        cotangent,
        normed2,
        facts,
        norm2_gain[None],
        hidden2,
        out_bias_grad,
        proj_weight,
        projected,
        attended,
        hidden1_t,
        qkv_weight,
        mix_t,
    )
    hidden1_other = swap(hidden1_part)
    split = sent.shape[1] - 2 * head_cols
    came = across(sent, bits[0], sources)
    total = kept + came.astype(F32)
    totals = [total[:, :split], total[:, split:]]
    out_home = nn(onehot, over_group(out_back).reshape(-1, feat_dim)).astype(BF16)
    for turn in range(1, len(bits)):
        if turn >= 2:
            totals, out_home = lax.optimization_barrier((totals, out_home))
        if turn == len(bits) - 1:
            out_other = swap(out_home)
        if turn == 2:
            totals, hidden1_other = lax.optimization_barrier((totals, hidden1_other))
        sends = lax.optimization_barrier([t[t.shape[0] // 2 :].astype(BF16) for t in totals])
        cames = [across(t, order[turn], sources) for t, order in zip(sends, orders)]
        totals = [keep_half(t, c) for t, c in zip(totals, cames)]
    hidden1_grad = hidden1_part.astype(F32) + hidden1_other.astype(F32)
    norm1_gain_grad = jnp.sum(hidden1_grad * normed1, axis=0)
    norm1_bias_grad = jnp.sum(hidden1_grad, axis=0)
    input_grad = middle_grad + norm_back(hidden1_grad * norm1_gain, normed1, inverse1)
    bias_home = exact(gate_map, expert_out_bias)
    mine = [t.astype(BF16) for t in totals]
    late = jnp.stack(
        [
            norm1_gain_grad,
            norm1_bias_grad,
            jnp.concatenate([qv_sums[0, :head_cols], qv_sums[0, 2 * head_cols :]]),
        ]
    )
    late = jnp.pad(late, ((0, 5), (0, 0)))

    def late_rows(late):
        high, low = high_low(late)
        both = jnp.pad(jnp.concatenate([high, low], axis=0), ((0, 0), (0, split - feat_dim)))
        return high.astype(F32) + low.astype(F32), both

    def late_sum(own, came):
        came = came[:, :feat_dim].astype(F32)
        return own + (came[:8] + came[8:])

    size = chunk
    for turn in range(len(bits) - 1, 0, -1):
        own, both = late_rows(late)
        first, second = jnp.concatenate([mine[0], both], axis=0), mine[1]
        if turn == 1:
            first, second, out_other = lax.optimization_barrier((first, second, out_other))
        else:
            first, second = lax.optimization_barrier((first, second))
        came = across(first, orders[0][turn], sources)
        came_b = across(second, orders[1][turn], sources)
        late = late_sum(own, came[size:])
        mine = [
            jnp.concatenate([mine[0], came[:size]], axis=0),
            jnp.concatenate([mine[1], came_b], axis=0),
        ]
        size = 2 * size
    out_home = out_home.astype(F32) + out_other.astype(F32)
    output = (middle + (out_home + bias_home)).astype(BF16)
    own, both = late_rows(late)
    first, second, input_grad, output = lax.optimization_barrier(
        (jnp.concatenate([mine[0], both], axis=0), mine[1], input_grad, output)
    )
    came = across(first, bits[0], sources)
    came_b = across(second, bits[0], sources)
    late = late_sum(own, came[size:])
    qv_bias_grad = late[2].reshape(2, head_cols)
    if chunk % 16 == 0:
        qkv_grad, proj_grad, router_grad, out_bias_grad, norm_grads = finish(
            me, first, second, came, came_b, head_cols, experts, feat_dim, orders
        )
        router_grad = router_grad.T
    else:
        first = tn(mix_t[0], jnp.concatenate([mine[0], came[:size]], axis=0))
        second = tn(mix_t[1], jnp.concatenate([mine[1], came_b], axis=0))
        qkv_grad = jnp.stack(
            [first[:, :head_cols], first[:, head_cols : 2 * head_cols], second[:, :head_cols]]
        )
        proj_grad = second[:, head_cols:].T
        router_grad = first[:, 2 * head_cols : 2 * head_cols + experts]
        norm_grads = first[:, 2 * head_cols + experts :].T
        out_bias_grad, norm_grads = norm_grads[:experts], norm_grads[experts:]
    norm2_gain_grad, norm2_bias_grad, proj_bias_grad = norm_grads[0], norm_grads[1], norm_grads[2]
    return (
        output,
        input_grad,
        late[0],
        late[1],
        qkv_grad,
        qv_bias_grad,
        proj_grad,
        proj_bias_grad,
        norm2_gain_grad,
        norm2_bias_grad,
        router_grad,
        in_weight_grad[None],
        in_bias_grad,
        out_weight_grad[None],
        out_bias_grad,
    )


def solution(mesh):
    return jax.shard_map(
        local,
        mesh=mesh,
        in_specs=(
            P("dp", None),
            P(),
            P(),
            P(None, None, "tensor"),
            P(None, "tensor"),
            P("tensor", None),
            P(),
            P(),
            P(),
            P(),
            P("dp", None, "tensor"),
            P("dp", "tensor"),
            P("dp", "tensor", None),
            P(),
            P("dp", None),
            P("dp", None),
        ),
        out_specs=(
            P("dp", None),
            P("dp", None),
            P(),
            P(),
            P(None, None, "tensor"),
            P(None, "tensor"),
            P("tensor", None),
            P(),
            P(),
            P(),
            P(),
            P("dp", None, "tensor"),
            P("dp", "tensor"),
            P("dp", "tensor", None),
            P(),
        ),
        check_vma=False,
    )
```
